256 devices in a mesh: ctx: 16 (over y, z_hi), ch: 16 (over x, z_lo, core).
Axes of the slice: x: 4, y: 4, z: 8 (z_hi: 4, z_lo: 2; z = z_hi * 2 + z_lo), core: 2. Of those that a mesh axis runs over, the one named last changes fastest.
Arguments:
- inputs: bfloat16 [8192, 3, 4096], P(('ctx', 'ch')), may hold values from -6 to 6
- short_weight: float32 [7, 3, 4096], P(None, None, 'ch'), may hold values from -2 to 2
- long_filter: bfloat16 [8192, 4096], P(None, 'ch'), may hold values from -2 to 2
- skip_gain: float32 [4096], P('ch'), may hold values from 0.5 to 1.5
Outputs:
- mixed: bfloat16 [8192, 4096], P(('ctx', 'ch'))
The draws below stay inside these ranges and needn't reach their ends.
All inputs are finite; a program needn't handle non-finite values.
Results may differ from the reference program's by a relative error of at most 0.01.
Values may be sent and summed in bfloat16 or wider, within the bound.
No kernel may reach another device: no remote copies, remote signals or barrier semaphores. Data moves between devices by JAX's collectives and lax.ppermute only.
A program may use at most 192 MiB of HBM per device.

```python
import jax
import jax.numpy as jnp

MODEL_WIDTH = 4096
SHORT = 7
SEQUENCE_LENGTH = 8192


def draw_long_filter(key, part):
    key_rows = jax.random.split(key, 8)
    delay_steps = jnp.arange(SEQUENCE_LENGTH, dtype=jnp.float32)[:, None]
    noise = jnp.clip(jax.random.normal(key_rows[0], (SEQUENCE_LENGTH, MODEL_WIDTH), jnp.float32), -4.0, 4.0)
    share = 0.5
    fast = jax.random.uniform(key_rows[1], (MODEL_WIDTH,), jnp.float32) < share
    slow_rate = jnp.exp(jax.random.uniform(key_rows[2], (MODEL_WIDTH,), jnp.float32, jnp.log(0.1), jnp.log(1.2))) / SEQUENCE_LENGTH
    fast_rate = jax.random.uniform(key_rows[3], (MODEL_WIDTH,), jnp.float32, 0.045, 0.08)
    rate = jnp.where(fast, fast_rate, slow_rate)
    initial_pulse = jax.random.randint(key_rows[4], (MODEL_WIDTH,), 0, SEQUENCE_LENGTH).astype(jnp.float32)
    secondary_pulse = jax.random.randint(key_rows[5], (MODEL_WIDTH,), 0, SEQUENCE_LENGTH).astype(jnp.float32)
    initial_decay = jax.random.uniform(key_rows[6], (MODEL_WIDTH,), jnp.float32, 0.5, 0.8)
    secondary_decay = jax.random.uniform(key_rows[7], (MODEL_WIDTH,), jnp.float32, 0.5, 0.8)
    decay_envelope = jnp.exp(-rate * delay_steps)
    decay_envelope = decay_envelope * jnp.where(delay_steps >= initial_pulse, initial_decay, 1.0)
    decay_envelope = decay_envelope * jnp.where(delay_steps >= secondary_pulse, secondary_decay, 1.0)
    amplitude = jnp.sqrt((1.0 - jnp.exp(-2.0 * rate)) / (1.0 - jnp.exp(-2.0 * rate * SEQUENCE_LENGTH)))
    return (amplitude * decay_envelope * noise).astype(jnp.bfloat16)


def levels(rng, dims, pieces, least, top_value):
    level = 1.0
    for axis_at, parts in pieces:
        steps = jax.random.uniform(jax.random.fold_in(jax.random.fold_in(rng, 6), axis_at), (parts,), jnp.float32, least / len(pieces), top_value / len(pieces))
        level = level * jnp.repeat(jnp.exp(steps), dims[axis_at] // parts).reshape((-1,) + (1,) * (len(dims) - 1 - axis_at))
    return level


def normal_values(own_key, dims, width, reach, pieces=(), held_as=jnp.bfloat16):
    array = jax.random.normal(own_key, dims, jnp.float32) * width
    if len(pieces) > 0:
        array = levels(own_key, dims, pieces, -0.22, 0.18) * array
    return jnp.clip(array, min=-reach, max=reach).astype(held_as)


def setup_inputs(seed: int = 0) -> dict:
    splits = jax.random.split(jax.random.key(seed), 5)
    inputs = normal_values(splits[0], (SEQUENCE_LENGTH, 3, MODEL_WIDTH), 1.0, 6.0, ((0, 256),))
    short_weight = normal_values(splits[1], (SHORT, 3, MODEL_WIDTH), SHORT ** -0.5, 2.0, ((2, 16),), jnp.float32)
    long_filter = draw_long_filter(jax.random.fold_in(splits[4], 71), 0)
    skip_gain = jnp.clip(0.5 + 1.0 * jax.random.uniform(splits[3], (MODEL_WIDTH,), jnp.float32) ** levels(splits[3], (MODEL_WIDTH,), ((0, 16),), -0.2, 0.2), 0.5, 1.5)
    return dict(inputs=inputs, short_weight=short_weight, long_filter=long_filter, skip_gain=skip_gain)


def reference(inputs, short_weight, long_filter, skip_gain):
    length = inputs.shape[0]
    signal_in = inputs.astype(jnp.float32)
    padded = jnp.pad(signal_in, ((SHORT - 1, 0), (0, 0), (0, 0)))
    features = jnp.zeros_like(signal_in)
    for offset in range(SHORT):
        begin = SHORT - 1 - offset
        features = features + short_weight[offset].astype(jnp.float32) * padded[begin:begin + length]
    gated = (features[:, 1] * features[:, 2]).astype(jnp.bfloat16)
    signal = gated.astype(jnp.float32)
    span = 2 * length
    filters = long_filter.astype(jnp.float32)
    spectrum = jnp.fft.rfft(signal, n=span, axis=0) * jnp.fft.rfft(filters, n=span, axis=0)
    long_part = jnp.fft.irfft(spectrum, n=span, axis=0)[:length]
    mixed = features[:, 0] * (long_part + skip_gain * signal)
    return mixed.astype(jnp.bfloat16)
```

```python
import functools
import math

import jax
import jax.numpy as jnp
import ml_dtypes
import numpy as np
from jax import lax
from jax.experimental import pallas as pl
from jax.experimental.pallas import tpu as pltpu
from jax.sharding import PartitionSpec as P

SHORT = 7
CTX = 16
CH = 16
DEVICES = CTX * CH
BLOCK = 32
LANES = 128
OWN = 16
GROUPS = LANES // OWN
TILES = BLOCK // GROUPS
LENGTH = DEVICES * BLOCK
WIDTH = DEVICES * OWN
ROWS = DEVICES
F32 = jnp.float32
BF16 = jnp.bfloat16


def halves(table):
    upper = table.astype(ml_dtypes.bfloat16)
    lower = (table - upper.astype(np.float64)).astype(ml_dtypes.bfloat16)
    return upper, lower


@functools.lru_cache(maxsize=None)
def tables():
    turn = 2.0 * math.pi
    freq = (np.arange(ROWS) + 0.5) / (2 * ROWS)
    block = np.arange(ROWS)
    angle = turn * freq[:, None] * block[None, :]
    first = np.concatenate([np.cos(angle), -np.sin(angle)], axis=0)
    upper, lower = halves(first)
    ahead = np.concatenate([upper, lower], axis=1)

    last = np.concatenate([np.cos(angle), -np.sin(angle)], axis=0).T * (2.0 / (2 * LENGTH))
    upper, lower = halves(last)
    back = np.concatenate([upper, upper, lower], axis=1)

    lane = np.arange(LANES)
    place = (np.arange(TILES)[:, None] * GROUPS + lane[None, :] // OWN).reshape(-1)
    angle = turn * freq[:, None] * place[None, :] / BLOCK
    spin_re = np.cos(angle).astype(np.float32)
    spin_im = -np.sin(angle).astype(np.float32)

    angle = turn * np.arange(TILES)[:, None] * (lane[None, :] // OWN) / BLOCK
    turn_rows = np.concatenate([np.cos(angle), -np.sin(angle)], axis=0).astype(np.float32)

    same = (lane[:, None] % OWN) == (lane[None, :] % OWN)
    angle = turn * (lane[:, None] // OWN) * (lane[None, :] // OWN) / GROUPS
    cosine = np.where(same, np.cos(angle), 0.0)
    sine = np.where(same, np.sin(angle), 0.0)
    forward = np.block([[cosine, -sine], [sine, cosine]])
    inverse = np.block([[cosine, sine], [-sine, cosine]])
    upper, lower = halves(forward)
    forward = np.concatenate([upper, upper, lower], axis=0)
    upper, lower = halves(inverse)
    inverse = np.concatenate([upper, upper, lower], axis=0)
    return ahead, back, spin_re, spin_im, turn_rows, forward, inverse


def dot(left, right):
    return jnp.dot(left, right, preferred_element_type=F32)


def split(value):
    upper = value.astype(BF16)
    return upper, (value - upper.astype(F32)).astype(BF16)


def swap_groups(tile):
    sub = lax.broadcasted_iota(jnp.int32, (1, GROUPS, LANES), 1)
    group = lax.broadcasted_iota(jnp.int32, (1, GROUPS, LANES), 2) // OWN
    for step in (4, 2, 1):
        sub_bit = (sub // step) % 2
        group_bit = (group // step) % 2
        shift = step * OWN
        up = pltpu.roll(pltpu.roll(tile, shift, 2), GROUPS - step, 1)
        if step == 4:
            moved = up
        else:
            down = pltpu.roll(pltpu.roll(tile, LANES - shift, 2), step, 1)
            moved = jnp.where(sub_bit == 0, up, down)
        tile = jnp.where(sub_bit == group_bit, tile, moved)
    return tile


def pack_kernel(k_ref, v_ref, out_ref, scratch):
    def column(j, carry):
        for half in range(2):
            lanes = pl.ds(pl.multiple_of(j * 2 * LANES, LANES) + half * LANES, LANES)
            for s, ref in enumerate((k_ref, v_ref)):
                tile = ref[0, :, lanes].astype(F32).reshape(TILES, GROUPS, LANES)
                tile = swap_groups(tile)
                for q in range(TILES):
                    scratch[pl.ds(half * 64 + s * TILES + q, GROUPS, stride=8), :] = tile[q]
            out_ref[half, :, j] = scratch[half * 64 : half * 64 + 64].reshape(8, 8, LANES).astype(BF16)
        return carry

    lax.fori_loop(0, CH, column, 0)


def pack(streams):
    whole = (1, BLOCK, WIDTH)
    return pl.pallas_call(
        pack_kernel,
        grid=(1,),
        out_shape=jax.ShapeDtypeStruct((2, GROUPS, CH, 8, LANES), BF16),
        in_specs=[pl.BlockSpec(whole, lambda g: (1, 0, 0)), pl.BlockSpec(whole, lambda g: (2, 0, 0))],
        out_specs=pl.BlockSpec((2, GROUPS, CH, 8, LANES), lambda g: (0, 0, 0, 0, 0)),
        scratch_shapes=[pltpu.VMEM((LANES, LANES), F32)],
        cost_estimate=pl.CostEstimate(flops=4_000_000, bytes_accessed=1_100_000, transcendentals=0),
        name="pack",
    )(streams, streams)


def forward_transform(signal, ahead, spin_re, spin_im, turn_rows, forward, stage, parts, out_ref):
    stage[...] = dot(ahead[...], signal[...])

    def rows(step, carry):
        at = pl.multiple_of(step * 16, 16)
        here, below = pl.ds(at, 16), pl.ds(at + ROWS, 16)
        real, imag = [], []
        for q in range(TILES):
            lanes = slice(q * LANES, (q + 1) * LANES)
            a, b = stage[here, lanes], stage[below, lanes]
            c, d = spin_re[here, lanes], spin_im[here, lanes]
            real.append(a * c - b * d)
            imag.append(a * d + b * c)
        er, ei = real[0] + real[2], imag[0] + imag[2]
        fr, fi = real[0] - real[2], imag[0] - imag[2]
        gr, gi = real[1] + real[3], imag[1] + imag[3]
        hr, hi = real[1] - real[3], imag[1] - imag[3]
        outs = ((er + gr, ei + gi), (fr + hi, fi - hr), (er - gr, ei - gi), (fr - hi, fi + hr))
        for k, (a, b) in enumerate(outs):
            if k > 0:
                c, d = turn_rows[k : k + 1], turn_rows[TILES + k : TILES + k + 1]
                a, b = a * c - b * d, a * d + b * c
            to = pl.ds(at + k * ROWS, 16)
            parts[to, 0:128], parts[to, 256:384] = split(a)
            parts[to, 128:256], parts[to, 384:512] = split(b)
        return carry

    lax.fori_loop(0, ROWS // 16, rows, 0)
    out_ref[...] = dot(parts[...], forward[0:512]) + dot(parts[:, 0:256], forward[512:768])


def filter_kernel(place, filter_ref, ahead, spin_re, spin_im, turn_rows, forward, out_ref, wide, signal, stage, parts):
    step = pl.program_id(0)
    shift = place[1]
    wide[...] = filter_ref[...].astype(F32)
    group = lax.broadcasted_iota(jnp.int32, (BLOCK, LANES), 1) // OWN
    at = pl.multiple_of(step * BLOCK, BLOCK)
    for q in range(TILES):
        tile = jnp.zeros((BLOCK, LANES), F32)
        for t in range(GROUPS):
            rows = wide[pl.ds(q * GROUPS + t, BLOCK, stride=BLOCK), :]
            if t > 0:
                rows = pltpu.roll(rows, t * OWN, 1)
            tile = jnp.where(group == (shift + t) % GROUPS, rows, tile)
        tile = pltpu.roll(tile, (GROUPS - shift) % GROUPS * OWN, 1).astype(BF16)
        signal[pl.ds(at, BLOCK), q * LANES : (q + 1) * LANES] = tile
        signal[pl.ds(at + ROWS, BLOCK), q * LANES : (q + 1) * LANES] = tile

    @pl.when(step == pl.num_programs(0) - 1)
    def _():
        forward_transform(signal, ahead, spin_re, spin_im, turn_rows, forward, stage, parts, out_ref)


def whole_spec(shape):
    return pl.BlockSpec(shape, lambda *_: (0,) * len(shape))


def filter_transform(place, long_filter, ahead, spin_re, spin_im, turn_rows, forward):
    chunk = BLOCK * BLOCK
    consts = (ahead, spin_re, spin_im, turn_rows, forward)
    return pl.pallas_call(
        filter_kernel,
        out_shape=jax.ShapeDtypeStruct((TILES * ROWS, 2 * LANES), F32),
        grid_spec=pltpu.PrefetchScalarGridSpec(
            num_scalar_prefetch=1,
            grid=(LENGTH // chunk,),
            in_specs=[pl.BlockSpec((chunk, LANES), lambda g, s: (g, s[0]))] + [whole_spec(c.shape) for c in consts],
            out_specs=whole_spec((TILES * ROWS, 2 * LANES)),
            scratch_shapes=[
                pltpu.VMEM((chunk, LANES), F32),
                pltpu.VMEM((2 * ROWS, TILES * LANES), BF16),
                pltpu.VMEM((2 * ROWS, TILES * LANES), F32),
                pltpu.VMEM((TILES * ROWS, 4 * LANES), BF16),
            ],
        ),
        cost_estimate=pl.CostEstimate(flops=2_000_000_000, bytes_accessed=6_000_000, transcendentals=0),
        name="filter_transform",
    )(place, long_filter, *consts)


def conv_kernel(
    packed, taps, gain, ahead, back, spin_re, spin_im, turn_rows, forward, inverse, out_ref,
    wide, signal, stage, parts, product, result,
):
    pad = 8
    wide[0:pad] = jnp.zeros((pad, LANES), F32)
    wide[pad:] = packed[...].astype(F32).reshape(DEVICES * 8, LANES)
    lane = lax.broadcasted_iota(jnp.int32, (BLOCK, LANES), 1)

    def gate(step, carry):
        at = step * BLOCK
        streams = []
        for s in range(2):
            base = pl.multiple_of(at * 8, 8)
            tiles = [wide[pl.ds(base + s * TILES + TILES - 1, BLOCK, stride=8), :]]
            for q in range(TILES):
                tiles.append(wide[pl.ds(base + pad + s * TILES + q, BLOCK, stride=8), :])
            sums = []
            for q in range(TILES):
                total = taps[s : s + 1] * tiles[q + 1]
                for r in range(1, SHORT):
                    shifted = jnp.where(lane < LANES - OWN * r, tiles[q + 1], tiles[q])
                    total = total + taps[2 * r + s : 2 * r + s + 1] * pltpu.roll(shifted, OWN * r, 1)
                sums.append(total)
            streams.append(sums)
        to = pl.multiple_of(at, BLOCK)
        for q in range(TILES):
            gated = (streams[0][q] * streams[1][q]).astype(BF16)
            signal[pl.ds(to, BLOCK), q * LANES : (q + 1) * LANES] = gated
            signal[pl.ds(to + ROWS, BLOCK), q * LANES : (q + 1) * LANES] = gated
        return carry

    lax.fori_loop(0, ROWS // BLOCK, gate, 0)
    forward_transform(signal, ahead, spin_re, spin_im, turn_rows, forward, stage, parts, product)

    def multiply(step, carry):
        here = pl.ds(pl.multiple_of(step * 32, 32), 32)
        a, b = product[here, 0:128], product[here, 128:256]
        c, d = gain[here, 0:128], gain[here, 128:256]
        parts[here, 0:128], parts[here, 256:384] = split(a * c - b * d)
        parts[here, 128:256], parts[here, 384:512] = split(a * d + b * c)
        return carry

    lax.fori_loop(0, TILES * ROWS // 32, multiply, 0)
    product[...] = dot(parts[...], inverse[0:512]) + dot(parts[:, 0:256], inverse[512:768])

    def unspin(step, carry):
        at = pl.multiple_of(step * 16, 16)
        here = pl.ds(at, 16)
        real, imag = [], []
        for k in range(TILES):
            rows = pl.ds(at + k * ROWS, 16)
            a, b = product[rows, 0:128], product[rows, 128:256]
            if k > 0:
                c, d = turn_rows[k : k + 1], turn_rows[TILES + k : TILES + k + 1]
                a, b = a * c + b * d, b * c - a * d
            real.append(a)
            imag.append(b)
        er, ei = real[0] + real[2], imag[0] + imag[2]
        fr, fi = real[0] - real[2], imag[0] - imag[2]
        gr, gi = real[1] + real[3], imag[1] + imag[3]
        hr, hi = real[1] - real[3], imag[1] - imag[3]
        outs = ((er + gr, ei + gi), (fr - hi, fi + hr), (er - gr, ei - gi), (fr + hi, fi - hr))
        for q, (a, b) in enumerate(outs):
            lanes = slice(q * LANES, (q + 1) * LANES)
            c, d = spin_re[here, lanes], spin_im[here, lanes]
            parts[pl.ds(at, 16), lanes], parts[pl.ds(at + 2 * ROWS, 16), lanes] = split(a * c + b * d)
            parts[pl.ds(at + ROWS, 16), lanes], parts[pl.ds(at + 3 * ROWS, 16), lanes] = split(b * c - a * d)
        return carry

    lax.fori_loop(0, ROWS // 16, unspin, 0)
    skip = taps[2 * SHORT : 2 * SHORT + 1]
    for q in range(TILES):
        lanes = slice(q * LANES, (q + 1) * LANES)
        long_part = dot(back[:, 0:1024], parts[:, lanes]) + dot(back[:, 1024:1536], parts[0:512, lanes])
        total = long_part + skip * signal[0:ROWS, lanes].astype(F32)
        result[pl.ds(q, ROWS, stride=TILES), :] = total
    out_ref[...] = result[...].reshape(DEVICES, TILES, LANES).astype(BF16)


def convolve(packed, taps, gain, ahead, back, spin_re, spin_im, turn_rows, forward, inverse):
    return pl.pallas_call(
        conv_kernel,
        out_shape=jax.ShapeDtypeStruct((DEVICES, TILES, LANES), BF16),
        scratch_shapes=[
            pltpu.VMEM((8 + DEVICES * 8, LANES), F32),
            pltpu.VMEM((2 * ROWS, TILES * LANES), BF16),
            pltpu.VMEM((2 * ROWS, TILES * LANES), F32),
            pltpu.VMEM((TILES * ROWS, 4 * LANES), BF16),
            pltpu.VMEM((TILES * ROWS, 2 * LANES), F32),
            pltpu.VMEM((DEVICES * TILES, LANES), F32),
        ],
        cost_estimate=pl.CostEstimate(flops=4_000_000_000, bytes_accessed=6_000_000, transcendentals=0),
        name="convolve",
    )(packed, taps, gain, ahead, back, spin_re, spin_im, turn_rows, forward, inverse)


def query_kernel(x_ref, rim_ref, taps_ref, out_ref):
    def column(j, carry):
        for half in range(2):
            lanes = pl.ds(pl.multiple_of(j * 2 * LANES, LANES) + half * LANES, LANES)
            x = jnp.concatenate([rim_ref[:, lanes].astype(F32), x_ref[0, :, lanes].astype(F32)], axis=0)
            total = jnp.zeros((BLOCK, LANES), F32)
            for r in range(SHORT):
                total = total + taps_ref[j, r : r + 1, half * LANES : (half + 1) * LANES] * x[8 - r : 8 - r + BLOCK]
            out_ref[:, lanes] = total
        return carry

    lax.fori_loop(0, CH, column, 0)


def query_features(streams, rim, taps):
    return pl.pallas_call(
        query_kernel,
        grid=(1,),
        out_shape=jax.ShapeDtypeStruct((BLOCK, WIDTH), F32),
        in_specs=[
            pl.BlockSpec((1, BLOCK, WIDTH), lambda g: (0, 0, 0)),
            whole_spec((8, WIDTH)),
            whole_spec((CH, SHORT, WIDTH // CH)),
        ],
        out_specs=whole_spec((BLOCK, WIDTH)),
        cost_estimate=pl.CostEstimate(flops=4_000_000, bytes_accessed=1_000_000, transcendentals=0),
        name="query_features",
    )(streams, rim, taps)


def mix_kernel(long_ref, query_ref, out_ref, scratch):
    def column(j, carry):
        for half in range(2):
            lanes = pl.ds(pl.multiple_of(j * 2 * LANES, LANES) + half * LANES, LANES)
            scratch[half] = long_ref[half, :, j].astype(F32).reshape(GROUPS * TILES, LANES)
            tile = jnp.stack([scratch[half, pl.ds(q, GROUPS, stride=TILES), :] for q in range(TILES)])
            tile = swap_groups(tile).reshape(BLOCK, LANES)
            out_ref[:, lanes] = (tile * query_ref[:, lanes]).astype(BF16)
        return carry

    lax.fori_loop(0, CH, column, 0)


def mix(long_part, query):
    return pl.pallas_call(
        mix_kernel,
        out_shape=jax.ShapeDtypeStruct((BLOCK, WIDTH), BF16),
        scratch_shapes=[pltpu.VMEM((2, GROUPS * TILES, LANES), F32)],
        cost_estimate=pl.CostEstimate(flops=4_000_000, bytes_accessed=1_000_000, transcendentals=0),
        name="mix",
    )(long_part, query)


def own_rows(short_weight, skip_gain, row):
    taps = lax.dynamic_slice(short_weight, (0, 1, row * OWN), (SHORT, 2, OWN)).reshape(2 * SHORT, OWN)
    skip = lax.dynamic_slice(skip_gain, (row * OWN,), (OWN,)).reshape(1, OWN)
    rows = jnp.concatenate([taps, skip, jnp.zeros((1, OWN), F32)], axis=0)
    return jnp.tile(rows, (1, GROUPS))


def local(inputs, short_weight, long_filter, skip_gain):
    row = lax.axis_index("ctx")
    ahead, back, spin_re, spin_im, turn_rows, forward, inverse = (jnp.asarray(t) for t in tables())
    streams = jnp.transpose(inputs, (1, 0, 2))
    packed = pack(streams).reshape(DEVICES, 8, LANES)
    packed = lax.all_to_all(packed, ("ctx", "ch"), 0, 0, tiled=True)
    rim = lax.ppermute(streams[0, BLOCK - 8 :], ("ctx", "ch"), [(d, d + 1) for d in range(DEVICES - 1)])
    query_taps = lax.all_gather(short_weight[:, 0], "ch")
    place = jnp.stack([row // GROUPS, row % GROUPS]).astype(jnp.int32)
    gain = filter_transform(place, long_filter, ahead, spin_re, spin_im, turn_rows, forward)
    query = query_features(streams, rim, query_taps)
    taps = own_rows(short_weight, skip_gain, row)
    long_part = convolve(packed, taps, gain, ahead, back, spin_re, spin_im, turn_rows, forward, inverse)
    long_part = lax.all_to_all(long_part, ("ctx", "ch"), 0, 0, tiled=True)
    return mix(long_part.reshape(2, GROUPS, CH, TILES, LANES), query)


def solution(mesh):
    in_specs = (P(("ctx", "ch"), None, None), P(None, None, "ch"), P(None, "ch"), P("ch"))
    out_specs = P(("ctx", "ch"), None)
    return jax.shard_map(local, mesh=mesh, in_specs=in_specs, out_specs=out_specs, check_vma=False)
```

```python
import functools
import math

import jax
import jax.numpy as jnp
import ml_dtypes
import numpy as np
from jax import lax
from jax.experimental import pallas as pl
from jax.experimental.pallas import tpu as pltpu
from jax.sharding import PartitionSpec as P

SHORT = 7
CTX = 16
CH = 16
DEVICES = CTX * CH
BLOCK = 32
LANES = 128
OWN = 16
GROUPS = LANES // OWN
TILES = BLOCK // GROUPS
LENGTH = DEVICES * BLOCK
WIDTH = DEVICES * OWN
ROWS = DEVICES
F32 = jnp.float32
BF16 = jnp.bfloat16


def halves(table):
    upper = table.astype(ml_dtypes.bfloat16)
    lower = (table - upper.astype(np.float64)).astype(ml_dtypes.bfloat16)
    return upper, lower


@functools.lru_cache(maxsize=None)
def tables():
    turn = 2.0 * math.pi
    freq = (np.arange(ROWS) + 0.5) / (2 * ROWS)
    block = np.arange(ROWS)
    angle = turn * freq[:, None] * block[None, :]
    first = np.concatenate([np.cos(angle), -np.sin(angle)], axis=0)
    upper, lower = halves(first)
    ahead = np.concatenate([upper, lower], axis=1)

    last = np.concatenate([np.cos(angle), -np.sin(angle)], axis=0).T * (2.0 / (2 * LENGTH))
    upper, lower = halves(last)
    back = np.concatenate([upper, upper, lower], axis=1)

    lane = np.arange(LANES)
    place = (np.arange(TILES)[:, None] * GROUPS + lane[None, :] // OWN).reshape(-1)
    angle = turn * freq[:, None] * place[None, :] / BLOCK
    spin_re = np.cos(angle).astype(np.float32)
    spin_im = -np.sin(angle).astype(np.float32)

    angle = turn * np.arange(TILES)[:, None] * (lane[None, :] // OWN) / BLOCK
    turn_rows = np.concatenate([np.cos(angle), -np.sin(angle)], axis=0).astype(np.float32)

    same = (lane[:, None] % OWN) == (lane[None, :] % OWN)
    angle = turn * (lane[:, None] // OWN) * (lane[None, :] // OWN) / GROUPS
    cosine = np.where(same, np.cos(angle), 0.0)
    sine = np.where(same, np.sin(angle), 0.0)
    forward = np.block([[cosine, -sine], [sine, cosine]])
    inverse = np.block([[cosine, sine], [-sine, cosine]])
    upper, lower = halves(forward)
    forward = np.concatenate([upper, upper, lower], axis=0)
    upper, lower = halves(inverse)
    inverse = np.concatenate([upper, upper, lower], axis=0)
    return ahead, back, spin_re, spin_im, turn_rows, forward, inverse


def dot(left, right):
    return jnp.dot(left, right, preferred_element_type=F32)


def split(value):
    upper = value.astype(BF16)
    return upper, (value - upper.astype(F32)).astype(BF16)


def exchange(tiles):
    group = lax.broadcasted_iota(jnp.int32, (GROUPS, LANES), 1) // OWN
    for step in (4, 2, 1):
        low = (group // step) % 2 == 0
        shift = step * OWN
        moved = list(tiles)
        for t in range(GROUPS):
            if t & step == 0:
                a, b = tiles[t], tiles[t + step]
                if step == 4:
                    across = pltpu.roll(jnp.where(low, b, a), shift, 1)
                    moved[t], moved[t + step] = jnp.where(low, a, across), jnp.where(low, across, b)
                else:
                    moved[t] = jnp.where(low, a, pltpu.roll(b, shift, 1))
                    moved[t + step] = jnp.where(low, pltpu.roll(a, LANES - shift, 1), b)
        tiles = moved
    return tiles


def half_lanes(j, half):
    return pl.ds(pl.multiple_of(j * 2 * LANES, LANES) + half * LANES, LANES)


def pack_kernel(k_ref, v_ref, out_ref, scratch):
    def columns(step, carry):
        for at in range(2):
            j = step * 2 + at
            for half in range(2):
                slot = scratch.at[at * 2 + half]
                for s, ref in enumerate((k_ref, v_ref)):
                    slot[s * BLOCK : (s + 1) * BLOCK] = ref[0, :, half_lanes(j, half)].astype(F32)
                tiles = exchange([slot[pl.ds(t, 8, stride=GROUPS), :] for t in range(GROUPS)])
                for d in range(GROUPS):
                    out_ref[half, d, j] = tiles[d].astype(BF16)
        return carry

    lax.fori_loop(0, CH // 2, columns, 0)


def pack(streams):
    whole = (1, BLOCK, WIDTH)
    return pl.pallas_call(
        pack_kernel,
        grid=(1,),
        out_shape=jax.ShapeDtypeStruct((2, GROUPS, CH, 8, LANES), BF16),
        in_specs=[pl.BlockSpec(whole, lambda g: (1, 0, 0)), pl.BlockSpec(whole, lambda g: (2, 0, 0))],
        out_specs=pl.BlockSpec((2, GROUPS, CH, 8, LANES), lambda g: (0, 0, 0, 0, 0)),
        scratch_shapes=[pltpu.VMEM((4, 2 * BLOCK, LANES), F32)],
        cost_estimate=pl.CostEstimate(flops=4_000_000, bytes_accessed=1_100_000, transcendentals=0),
        name="pack",
    )(streams, streams)


def forward_transform(signal, ahead, spin_re, spin_im, turn_rows, forward, stage, parts, out_ref):
    stage[...] = dot(ahead[...], signal[...])

    def rows(step, carry):
        at = pl.multiple_of(step * 16, 16)
        here, below = pl.ds(at, 16), pl.ds(at + ROWS, 16)
        real, imag = [], []
        for q in range(TILES):
            lanes = slice(q * LANES, (q + 1) * LANES)
            a, b = stage[here, lanes], stage[below, lanes]
            c, d = spin_re[here, lanes], spin_im[here, lanes]
            real.append(a * c - b * d)
            imag.append(a * d + b * c)
        er, ei = real[0] + real[2], imag[0] + imag[2]
        fr, fi = real[0] - real[2], imag[0] - imag[2]
        gr, gi = real[1] + real[3], imag[1] + imag[3]
        hr, hi = real[1] - real[3], imag[1] - imag[3]
        outs = ((er + gr, ei + gi), (fr + hi, fi - hr), (er - gr, ei - gi), (fr - hi, fi + hr))
        for k, (a, b) in enumerate(outs):
            if k > 0:
                c, d = turn_rows[k : k + 1], turn_rows[TILES + k : TILES + k + 1]
                a, b = a * c - b * d, a * d + b * c
            to = pl.ds(at + k * ROWS, 16)
            parts[to, 0:128], parts[to, 256:384] = split(a)
            parts[to, 128:256], parts[to, 384:512] = split(b)
        return carry

    lax.fori_loop(0, ROWS // 16, rows, 0)
    out_ref[...] = dot(parts[...], forward[0:512]) + dot(parts[:, 0:256], forward[512:768])


def filter_kernel(place, filter_ref, ahead, spin_re, spin_im, turn_rows, forward, out_ref, wide, signal, stage, parts):
    step = pl.program_id(0)
    shift = place[1]
    wide[...] = filter_ref[...].astype(F32)
    group = lax.broadcasted_iota(jnp.int32, (BLOCK, LANES), 1) // OWN
    at = pl.multiple_of(step * BLOCK, BLOCK)
    for q in range(TILES):
        tile = jnp.zeros((BLOCK, LANES), F32)
        for t in range(GROUPS):
            rows = wide[pl.ds(q * GROUPS + t, BLOCK, stride=BLOCK), :]
            if t > 0:
                rows = pltpu.roll(rows, t * OWN, 1)
            tile = jnp.where(group == (shift + t) % GROUPS, rows, tile)
        tile = pltpu.roll(tile, (GROUPS - shift) % GROUPS * OWN, 1).astype(BF16)
        signal[pl.ds(at, BLOCK), q * LANES : (q + 1) * LANES] = tile
        signal[pl.ds(at + ROWS, BLOCK), q * LANES : (q + 1) * LANES] = tile

    @pl.when(step == pl.num_programs(0) - 1)
    def _():
        forward_transform(signal, ahead, spin_re, spin_im, turn_rows, forward, stage, parts, out_ref)


def whole_spec(shape):
    return pl.BlockSpec(shape, lambda *_: (0,) * len(shape))


def filter_transform(place, long_filter, ahead, spin_re, spin_im, turn_rows, forward):
    chunk = BLOCK * BLOCK
    consts = (ahead, spin_re, spin_im, turn_rows, forward)
    return pl.pallas_call(
        filter_kernel,
        out_shape=jax.ShapeDtypeStruct((TILES * ROWS, 2 * LANES), F32),
        grid_spec=pltpu.PrefetchScalarGridSpec(
            num_scalar_prefetch=1,
            grid=(LENGTH // chunk,),
            in_specs=[pl.BlockSpec((chunk, LANES), lambda g, s: (g, s[0]))] + [whole_spec(c.shape) for c in consts],
            out_specs=whole_spec((TILES * ROWS, 2 * LANES)),
            scratch_shapes=[
                pltpu.VMEM((chunk, LANES), F32),
                pltpu.VMEM((2 * ROWS, TILES * LANES), BF16),
                pltpu.VMEM((2 * ROWS, TILES * LANES), F32),
                pltpu.VMEM((TILES * ROWS, 4 * LANES), BF16),
            ],
        ),
        cost_estimate=pl.CostEstimate(flops=2_000_000_000, bytes_accessed=6_000_000, transcendentals=0),
        name="filter_transform",
    )(place, long_filter, *consts)


def conv_kernel(
    packed, taps, gain, ahead, back, spin_re, spin_im, turn_rows, forward, inverse, out_ref,
    wide, signal, stage, parts, product, result,
):
    pad = 8
    wide[0:pad] = jnp.zeros((pad, LANES), F32)
    wide[pad:] = packed[...].astype(F32).reshape(DEVICES * 8, LANES)
    lane = lax.broadcasted_iota(jnp.int32, (BLOCK, LANES), 1)

    def gate(step, carry):
        at = step * BLOCK
        streams = []
        for s in range(2):
            base = pl.multiple_of(at * 8, 8)
            tiles = [wide[pl.ds(base + s * TILES + TILES - 1, BLOCK, stride=8), :]]
            for q in range(TILES):
                tiles.append(wide[pl.ds(base + pad + s * TILES + q, BLOCK, stride=8), :])
            sums = []
            for q in range(TILES):
                total = taps[s : s + 1] * tiles[q + 1]
                for r in range(1, SHORT):
                    shifted = jnp.where(lane < LANES - OWN * r, tiles[q + 1], tiles[q])
                    total = total + taps[2 * r + s : 2 * r + s + 1] * pltpu.roll(shifted, OWN * r, 1)
                sums.append(total)
            streams.append(sums)
        to = pl.multiple_of(at, BLOCK)
        for q in range(TILES):
            gated = (streams[0][q] * streams[1][q]).astype(BF16)
            signal[pl.ds(to, BLOCK), q * LANES : (q + 1) * LANES] = gated
            signal[pl.ds(to + ROWS, BLOCK), q * LANES : (q + 1) * LANES] = gated
        return carry

    lax.fori_loop(0, ROWS // BLOCK, gate, 0)
    forward_transform(signal, ahead, spin_re, spin_im, turn_rows, forward, stage, parts, product)

    def multiply(step, carry):
        here = pl.ds(pl.multiple_of(step * 32, 32), 32)
        a, b = product[here, 0:128], product[here, 128:256]
        c, d = gain[here, 0:128], gain[here, 128:256]
        parts[here, 0:128], parts[here, 256:384] = split(a * c - b * d)
        parts[here, 128:256], parts[here, 384:512] = split(a * d + b * c)
        return carry

    lax.fori_loop(0, TILES * ROWS // 32, multiply, 0)
    product[...] = dot(parts[...], inverse[0:512]) + dot(parts[:, 0:256], inverse[512:768])

    def unspin(step, carry):
        at = pl.multiple_of(step * 16, 16)
        here = pl.ds(at, 16)
        real, imag = [], []
        for k in range(TILES):
            rows = pl.ds(at + k * ROWS, 16)
            a, b = product[rows, 0:128], product[rows, 128:256]
            if k > 0:
                c, d = turn_rows[k : k + 1], turn_rows[TILES + k : TILES + k + 1]
                a, b = a * c + b * d, b * c - a * d
            real.append(a)
            imag.append(b)
        er, ei = real[0] + real[2], imag[0] + imag[2]
        fr, fi = real[0] - real[2], imag[0] - imag[2]
        gr, gi = real[1] + real[3], imag[1] + imag[3]
        hr, hi = real[1] - real[3], imag[1] - imag[3]
        outs = ((er + gr, ei + gi), (fr - hi, fi + hr), (er - gr, ei - gi), (fr + hi, fi - hr))
        for q, (a, b) in enumerate(outs):
            lanes = slice(q * LANES, (q + 1) * LANES)
            c, d = spin_re[here, lanes], spin_im[here, lanes]
            parts[pl.ds(at, 16), lanes], parts[pl.ds(at + 2 * ROWS, 16), lanes] = split(a * c + b * d)
            parts[pl.ds(at + ROWS, 16), lanes], parts[pl.ds(at + 3 * ROWS, 16), lanes] = split(b * c - a * d)
        return carry

    lax.fori_loop(0, ROWS // 16, unspin, 0)
    skip = taps[2 * SHORT : 2 * SHORT + 1]
    for q in range(TILES):
        lanes = slice(q * LANES, (q + 1) * LANES)
        long_part = dot(back[:, 0:1024], parts[:, lanes]) + dot(back[:, 1024:1536], parts[0:512, lanes])
        total = long_part + skip * signal[0:ROWS, lanes].astype(F32)
        result[pl.ds(q, ROWS, stride=TILES), :] = total
    out_ref[...] = result[...].reshape(DEVICES, TILES, LANES).astype(BF16)


def convolve(packed, taps, gain, ahead, back, spin_re, spin_im, turn_rows, forward, inverse):
    return pl.pallas_call(
        conv_kernel,
        out_shape=jax.ShapeDtypeStruct((DEVICES, TILES, LANES), BF16),
        scratch_shapes=[
            pltpu.VMEM((8 + DEVICES * 8, LANES), F32),
            pltpu.VMEM((2 * ROWS, TILES * LANES), BF16),
            pltpu.VMEM((2 * ROWS, TILES * LANES), F32),
            pltpu.VMEM((TILES * ROWS, 4 * LANES), BF16),
            pltpu.VMEM((TILES * ROWS, 2 * LANES), F32),
            pltpu.VMEM((DEVICES * TILES, LANES), F32),
        ],
        cost_estimate=pl.CostEstimate(flops=4_000_000_000, bytes_accessed=6_000_000, transcendentals=0),
        name="convolve",
    )(packed, taps, gain, ahead, back, spin_re, spin_im, turn_rows, forward, inverse)


def query_kernel(x_ref, rim_ref, taps_ref, out_ref):
    def column(j, carry):
        for half in range(2):
            lanes = pl.ds(pl.multiple_of(j * 2 * LANES, LANES) + half * LANES, LANES)
            x = jnp.concatenate([rim_ref[:, lanes].astype(F32), x_ref[0, :, lanes].astype(F32)], axis=0)
            total = jnp.zeros((BLOCK, LANES), F32)
            for r in range(SHORT):
                total = total + taps_ref[j, r : r + 1, half * LANES : (half + 1) * LANES] * x[8 - r : 8 - r + BLOCK]
            out_ref[:, lanes] = total
        return carry

    lax.fori_loop(0, CH, column, 0)


def query_features(streams, rim, taps):
    return pl.pallas_call(
        query_kernel,
        grid=(1,),
        out_shape=jax.ShapeDtypeStruct((BLOCK, WIDTH), F32),
        in_specs=[
            pl.BlockSpec((1, BLOCK, WIDTH), lambda g: (0, 0, 0)),
            whole_spec((8, WIDTH)),
            pl.BlockSpec((CH, 8, WIDTH // CH), lambda g: (0, 0, 0)),
        ],
        out_specs=whole_spec((BLOCK, WIDTH)),
        cost_estimate=pl.CostEstimate(flops=4_000_000, bytes_accessed=1_000_000, transcendentals=0),
        name="query_features",
    )(streams, rim, taps)


def mix_kernel(long_ref, query_ref, out_ref, before, after):
    def columns(step, carry):
        for at in range(2):
            j = step * 2 + at
            came, gone = before.at[at], after.at[at]
            for half in range(2):
                came[:, half * TILES : (half + 1) * TILES, :] = long_ref[half, :, j].astype(F32)
            tiles = exchange([came[d] for d in range(GROUPS)])
            for t in range(GROUPS):
                gone[pl.ds(t, 8, stride=GROUPS), :] = tiles[t]
            for half in range(2):
                lanes = half_lanes(j, half)
                out_ref[:, lanes] = (gone[half * BLOCK : (half + 1) * BLOCK] * query_ref[:, lanes]).astype(BF16)
        return carry

    lax.fori_loop(0, CH // 2, columns, 0)


def mix(long_part, query):
    return pl.pallas_call(
        mix_kernel,
        out_shape=jax.ShapeDtypeStruct((BLOCK, WIDTH), BF16),
        scratch_shapes=[pltpu.VMEM((2, GROUPS, 8, LANES), F32), pltpu.VMEM((2, 2 * BLOCK, LANES), F32)],
        cost_estimate=pl.CostEstimate(flops=4_000_000, bytes_accessed=1_000_000, transcendentals=0),
        name="mix",
    )(long_part, query)


def own_rows(short_weight, skip_gain, row):
    taps = lax.dynamic_slice(short_weight, (0, 1, row * OWN), (SHORT, 2, OWN)).reshape(2 * SHORT, OWN)
    skip = lax.dynamic_slice(skip_gain, (row * OWN,), (OWN,)).reshape(1, OWN)
    rows = jnp.concatenate([taps, skip, jnp.zeros((1, OWN), F32)], axis=0)
    return jnp.tile(rows, (1, GROUPS))


def local(inputs, short_weight, long_filter, skip_gain):
    row = lax.axis_index("ctx")
    ahead, back, spin_re, spin_im, turn_rows, forward, inverse = (jnp.asarray(t) for t in tables())
    streams = jnp.transpose(inputs, (1, 0, 2))
    packed = pack(streams).reshape(DEVICES, 8, LANES)
    packed = lax.all_to_all(packed, ("ctx", "ch"), 0, 0, tiled=True)
    rim = lax.ppermute(streams[0, BLOCK - 8 :], ("ctx", "ch"), [(d, d + 1) for d in range(DEVICES - 1)])
    query_taps = lax.all_gather(jnp.pad(short_weight[:, 0], ((0, 64 - SHORT), (0, 0))), "ch")
    place = jnp.stack([row // GROUPS, row % GROUPS]).astype(jnp.int32)
    gain = filter_transform(place, long_filter, ahead, spin_re, spin_im, turn_rows, forward)
    query = query_features(streams, rim, query_taps)
    taps = own_rows(short_weight, skip_gain, row)
    long_part = convolve(packed, taps, gain, ahead, back, spin_re, spin_im, turn_rows, forward, inverse)
    long_part = lax.all_to_all(long_part, ("ctx", "ch"), 0, 0, tiled=True)
    return mix(long_part.reshape(2, GROUPS, CH, TILES, LANES), query)


def solution(mesh):
    in_specs = (P(("ctx", "ch"), None, None), P(None, None, "ch"), P(None, "ch"), P("ch"))
    out_specs = P(("ctx", "ch"), None)
    return jax.shard_map(local, mesh=mesh, in_specs=in_specs, out_specs=out_specs, check_vma=False)
```

```python
import functools
import math

import jax
import jax.numpy as jnp
import ml_dtypes
import numpy as np
from jax import lax
from jax.experimental import pallas as pl
from jax.experimental.pallas import tpu as pltpu
from jax.sharding import PartitionSpec as P

SHORT = 7
CTX = 16
CH = 16
DEVICES = CTX * CH
BLOCK = 32
LANES = 128
OWN = 16
GROUPS = LANES // OWN
TILES = BLOCK // GROUPS
LENGTH = DEVICES * BLOCK
WIDTH = DEVICES * OWN
CHUNK = 16
ROWS = DEVICES
F32 = jnp.float32
VMEM = pl.BlockSpec(memory_space=pltpu.VMEM)
BF16 = jnp.bfloat16


def halves(table):
    upper = table.astype(ml_dtypes.bfloat16)
    lower = (table - upper.astype(np.float64)).astype(ml_dtypes.bfloat16)
    return upper, lower


@functools.lru_cache(maxsize=None)
def tables():
    turn = 2.0 * math.pi
    freq = (np.arange(ROWS) + 0.5) / (2 * ROWS)
    block = np.arange(ROWS)
    angle = turn * freq[:, None] * block[None, :]
    first = np.concatenate([np.cos(angle), -np.sin(angle)], axis=0)
    upper, lower = halves(first)
    ahead = np.concatenate([upper, lower], axis=1)

    last = np.concatenate([np.cos(angle), -np.sin(angle)], axis=0).T * (2.0 / (2 * LENGTH))
    upper, lower = halves(last)
    back = np.concatenate([upper, lower], axis=1)

    lane = np.arange(LANES)
    place = (np.arange(TILES)[:, None] * GROUPS + lane[None, :] // OWN).reshape(-1)
    fine = turn * freq[:CHUNK, None] * place[None, :] / BLOCK
    coarse = turn * (np.arange(ROWS // CHUNK) * CHUNK / (2 * ROWS))[:, None] * place[None, :] / BLOCK
    fine = np.concatenate([np.cos(fine), -np.sin(fine)], axis=1).astype(np.float32)
    coarse = np.concatenate([np.cos(coarse), -np.sin(coarse)], axis=1).astype(np.float32).reshape(-1, 2 * TILES, LANES)

    angle = turn * np.arange(TILES)[:, None] * (lane[None, :] // OWN) / BLOCK
    turn_rows = np.concatenate([np.cos(angle), -np.sin(angle)], axis=0).astype(np.float32)

    same = (lane[:, None] % OWN) == (lane[None, :] % OWN)
    angle = turn * (lane[:, None] // OWN) * (lane[None, :] // OWN) / GROUPS
    cosine = np.where(same, np.cos(angle), 0.0)
    sine = np.where(same, np.sin(angle), 0.0)
    forward = np.block([[cosine, -sine], [sine, cosine]])
    inverse = np.block([[cosine, sine], [-sine, cosine]])
    upper, lower = halves(forward)
    forward = np.concatenate([upper, lower], axis=0)
    upper, lower = halves(inverse)
    inverse = np.concatenate([upper, lower], axis=0)
    return ahead, back, fine, coarse, turn_rows, forward, inverse


def dot(left, right):
    return jnp.dot(left, right, preferred_element_type=F32)


def split(value):
    upper = value.astype(BF16)
    return upper, (value - upper.astype(F32)).astype(BF16)


def exchange(tiles):
    group = lax.broadcasted_iota(jnp.int32, (GROUPS, LANES), 1) // OWN
    for step in (4, 2, 1):
        low = (group // step) % 2 == 0
        shift = step * OWN
        moved = list(tiles)
        for t in range(GROUPS):
            if t & step == 0:
                a, b = tiles[t], tiles[t + step]
                if step == 4:
                    across = pltpu.roll(jnp.where(low, b, a), shift, 1)
                    moved[t], moved[t + step] = jnp.where(low, a, across), jnp.where(low, across, b)
                else:
                    moved[t] = jnp.where(low, a, pltpu.roll(b, shift, 1))
                    moved[t + step] = jnp.where(low, pltpu.roll(a, LANES - shift, 1), b)
        tiles = moved
    return tiles


def half_lanes(j, half):
    return pl.ds(pl.multiple_of(j * 2 * LANES, LANES) + half * LANES, LANES)


def pack_kernel(k_ref, v_ref, out_ref, scratch):
    def columns(step, carry):
        for at in range(2):
            j = step * 2 + at
            for half in range(2):
                slot = scratch.at[at * 2 + half]
                for s, ref in enumerate((k_ref, v_ref)):
                    slot[s * BLOCK : (s + 1) * BLOCK] = ref[0, :, half_lanes(j, half)].astype(F32)
                tiles = exchange([slot[pl.ds(t, 8, stride=GROUPS), :] for t in range(GROUPS)])
                for d in range(GROUPS):
                    out_ref[half, d, j] = tiles[d].astype(BF16)
        return carry

    lax.fori_loop(0, CH // 2, columns, 0)


def pack(streams):
    whole = (1, BLOCK, WIDTH)
    return pl.pallas_call(
        pack_kernel,
        grid=(1,),
        out_shape=jax.ShapeDtypeStruct((2, GROUPS, CH, 8, LANES), BF16),
        in_specs=[pl.BlockSpec(whole, lambda g: (1, 0, 0)), pl.BlockSpec(whole, lambda g: (2, 0, 0))],
        out_specs=pl.BlockSpec((2, GROUPS, CH, 8, LANES), lambda g: (0, 0, 0, 0, 0)),
        scratch_shapes=[pltpu.VMEM((4, 2 * BLOCK, LANES), F32)],
        cost_estimate=pl.CostEstimate(flops=4_000_000, bytes_accessed=1_100_000, transcendentals=0),
        compiler_params=pltpu.CompilerParams(vmem_limit_bytes=8 * 2**20),
        name="pack",
    )(streams, streams)


def spin_rows(fine, coarse, step):
    rows = coarse[step]
    spins = []
    for q in range(TILES):
        re = slice(q * LANES, (q + 1) * LANES)
        im = slice((TILES + q) * LANES, (TILES + q + 1) * LANES)
        a, b = fine[:, re], fine[:, im]
        c, d = rows[q : q + 1], rows[TILES + q : TILES + q + 1]
        spins.append((a * c - b * d, a * d + b * c))
    return spins


def table_dot(parts, table):
    upper = table[0:256]
    return dot(parts[:, 0:256], upper) + dot(parts[:, 256:512], upper) + dot(parts[:, 0:256], table[256:512])


def forward_transform(signal, ahead, fine, coarse, turn_rows, forward, stage, parts, out_ref):
    stage[...] = dot(ahead[...], signal[...])

    def rows(step, carry):
        at = pl.multiple_of(step * 16, 16)
        here, below = pl.ds(at, 16), pl.ds(at + ROWS, 16)
        spins = spin_rows(fine, coarse, step)
        real, imag = [], []
        for q in range(TILES):
            lanes = slice(q * LANES, (q + 1) * LANES)
            a, b = stage[here, lanes], stage[below, lanes]
            c, d = spins[q]
            real.append(a * c - b * d)
            imag.append(a * d + b * c)
        er, ei = real[0] + real[2], imag[0] + imag[2]
        fr, fi = real[0] - real[2], imag[0] - imag[2]
        gr, gi = real[1] + real[3], imag[1] + imag[3]
        hr, hi = real[1] - real[3], imag[1] - imag[3]
        outs = ((er + gr, ei + gi), (fr + hi, fi - hr), (er - gr, ei - gi), (fr - hi, fi + hr))
        for k, (a, b) in enumerate(outs):
            if k > 0:
                c, d = turn_rows[k : k + 1], turn_rows[TILES + k : TILES + k + 1]
                a, b = a * c - b * d, a * d + b * c
            to = pl.ds(at + k * ROWS, 16)
            parts[to, 0:128], parts[to, 256:384] = split(a)
            parts[to, 128:256], parts[to, 384:512] = split(b)
        return carry

    lax.fori_loop(0, ROWS // 16, rows, 0)
    out_ref[...] = table_dot(parts, forward)


def filter_kernel(place, filter_ref, ahead, fine, coarse, turn_rows, forward, out_ref, wide, signal, stage, parts):
    step = pl.program_id(0)
    shift = place[1]
    wide[...] = filter_ref[...].astype(F32)
    group = lax.broadcasted_iota(jnp.int32, (BLOCK, LANES), 1) // OWN
    at = pl.multiple_of(step * BLOCK, BLOCK)
    for q in range(TILES):
        tile = jnp.zeros((BLOCK, LANES), F32)
        for t in range(GROUPS):
            rows = wide[pl.ds(q * GROUPS + t, BLOCK, stride=BLOCK), :]
            if t > 0:
                rows = pltpu.roll(rows, t * OWN, 1)
            tile = jnp.where(group == (shift + t) % GROUPS, rows, tile)
        tile = pltpu.roll(tile, (GROUPS - shift) % GROUPS * OWN, 1).astype(BF16)
        signal[pl.ds(at, BLOCK), q * LANES : (q + 1) * LANES] = tile
        signal[pl.ds(at + ROWS, BLOCK), q * LANES : (q + 1) * LANES] = tile

    @pl.when(step == pl.num_programs(0) - 1)
    def _():
        forward_transform(signal, ahead, fine, coarse, turn_rows, forward, stage, parts, out_ref)


def whole_spec(shape):
    return pl.BlockSpec(shape, lambda *_: (0,) * len(shape))


def filter_transform(place, long_filter, ahead, fine, coarse, turn_rows, forward):
    chunk = BLOCK * BLOCK
    consts = (ahead, fine, coarse, turn_rows, forward)
    return pl.pallas_call(
        filter_kernel,
        out_shape=jax.ShapeDtypeStruct((TILES * ROWS, 2 * LANES), F32),
        grid_spec=pltpu.PrefetchScalarGridSpec(
            num_scalar_prefetch=1,
            grid=(LENGTH // chunk,),
            in_specs=[pl.BlockSpec((chunk, LANES), lambda g, s: (g, s[0]))] + [whole_spec(c.shape) for c in consts],
            out_specs=whole_spec((TILES * ROWS, 2 * LANES)),
            scratch_shapes=[
                pltpu.VMEM((chunk, LANES), F32),
                pltpu.VMEM((2 * ROWS, TILES * LANES), BF16),
                pltpu.VMEM((2 * ROWS, TILES * LANES), F32),
                pltpu.VMEM((TILES * ROWS, 4 * LANES), BF16),
            ],
        ),
        cost_estimate=pl.CostEstimate(flops=2_000_000_000, bytes_accessed=6_000_000, transcendentals=0),
        compiler_params=pltpu.CompilerParams(vmem_limit_bytes=20 * 2**20),
        name="filter_transform",
    )(place, long_filter, *consts)


def conv_kernel(
    packed, taps, gain, ahead, back, fine, coarse, turn_rows, forward, inverse, out_ref,
    wide, signal, stage, parts, product, result,
):
    pad = 8
    wide[0:pad] = jnp.zeros((pad, LANES), F32)
    wide[pad:] = packed[...].astype(F32).reshape(DEVICES * 8, LANES)
    lane = lax.broadcasted_iota(jnp.int32, (BLOCK, LANES), 1)

    def gate(step, carry):
        at = step * BLOCK
        streams = []
        for s in range(2):
            base = pl.multiple_of(at * 8, 8)
            tiles = [wide[pl.ds(base + s * TILES + TILES - 1, BLOCK, stride=8), :]]
            for q in range(TILES):
                tiles.append(wide[pl.ds(base + pad + s * TILES + q, BLOCK, stride=8), :])
            sums = []
            for q in range(TILES):
                total = taps[s : s + 1] * tiles[q + 1]
                for r in range(1, SHORT):
                    shifted = jnp.where(lane < LANES - OWN * r, tiles[q + 1], tiles[q])
                    total = total + taps[2 * r + s : 2 * r + s + 1] * pltpu.roll(shifted, OWN * r, 1)
                sums.append(total)
            streams.append(sums)
        to = pl.multiple_of(at, BLOCK)
        for q in range(TILES):
            gated = (streams[0][q] * streams[1][q]).astype(BF16)
            signal[pl.ds(to, BLOCK), q * LANES : (q + 1) * LANES] = gated
            signal[pl.ds(to + ROWS, BLOCK), q * LANES : (q + 1) * LANES] = gated
        return carry

    lax.fori_loop(0, ROWS // BLOCK, gate, 0)
    forward_transform(signal, ahead, fine, coarse, turn_rows, forward, stage, parts, product)

    def multiply(step, carry):
        here = pl.ds(pl.multiple_of(step * 32, 32), 32)
        a, b = product[here, 0:128], product[here, 128:256]
        c, d = gain[here, 0:128], gain[here, 128:256]
        parts[here, 0:128], parts[here, 256:384] = split(a * c - b * d)
        parts[here, 128:256], parts[here, 384:512] = split(a * d + b * c)
        return carry

    lax.fori_loop(0, TILES * ROWS // 32, multiply, 0)
    product[...] = table_dot(parts, inverse)

    def unspin(step, carry):
        at = pl.multiple_of(step * 16, 16)
        spins = spin_rows(fine, coarse, step)
        real, imag = [], []
        for k in range(TILES):
            rows = pl.ds(at + k * ROWS, 16)
            a, b = product[rows, 0:128], product[rows, 128:256]
            if k > 0:
                c, d = turn_rows[k : k + 1], turn_rows[TILES + k : TILES + k + 1]
                a, b = a * c + b * d, b * c - a * d
            real.append(a)
            imag.append(b)
        er, ei = real[0] + real[2], imag[0] + imag[2]
        fr, fi = real[0] - real[2], imag[0] - imag[2]
        gr, gi = real[1] + real[3], imag[1] + imag[3]
        hr, hi = real[1] - real[3], imag[1] - imag[3]
        outs = ((er + gr, ei + gi), (fr - hi, fi + hr), (er - gr, ei - gi), (fr + hi, fi - hr))
        for q, (a, b) in enumerate(outs):
            lanes = slice(q * LANES, (q + 1) * LANES)
            c, d = spins[q]
            parts[pl.ds(at, 16), lanes], parts[pl.ds(at + 2 * ROWS, 16), lanes] = split(a * c + b * d)
            parts[pl.ds(at + ROWS, 16), lanes], parts[pl.ds(at + 3 * ROWS, 16), lanes] = split(b * c - a * d)
        return carry

    lax.fori_loop(0, ROWS // 16, unspin, 0)
    skip = taps[2 * SHORT : 2 * SHORT + 1]
    for q in range(TILES):
        lanes = slice(q * LANES, (q + 1) * LANES)
        upper, lower = parts[0:512, lanes], parts[512:1024, lanes]
        long_part = dot(back[:, 0:512], upper) + dot(back[:, 0:512], lower) + dot(back[:, 512:1024], upper)
        total = long_part + skip * signal[0:ROWS, lanes].astype(F32)
        result[pl.ds(q, ROWS, stride=TILES), :] = total
    out_ref[...] = result[...].reshape(DEVICES, TILES, LANES).astype(BF16)


def convolve(packed, taps, gain, ahead, back, fine, coarse, turn_rows, forward, inverse):
    return pl.pallas_call(
        conv_kernel,
        out_shape=jax.ShapeDtypeStruct((DEVICES, TILES, LANES), BF16),
        in_specs=[VMEM] * 10,
        out_specs=VMEM,
        scratch_shapes=[
            pltpu.VMEM((8 + DEVICES * 8, LANES), F32),
            pltpu.VMEM((2 * ROWS, TILES * LANES), BF16),
            pltpu.VMEM((2 * ROWS, TILES * LANES), F32),
            pltpu.VMEM((TILES * ROWS, 4 * LANES), BF16),
            pltpu.VMEM((TILES * ROWS, 2 * LANES), F32),
            pltpu.VMEM((DEVICES * TILES, LANES), F32),
        ],
        cost_estimate=pl.CostEstimate(flops=4_000_000_000, bytes_accessed=6_000_000, transcendentals=0),
        compiler_params=pltpu.CompilerParams(vmem_limit_bytes=24 * 2**20),
        name="convolve",
    )(packed, taps, gain, ahead, back, fine, coarse, turn_rows, forward, inverse)


def query_kernel(x_ref, rim_ref, taps_ref, out_ref):
    def column(j, carry):
        for half in range(2):
            lanes = pl.ds(pl.multiple_of(j * 2 * LANES, LANES) + half * LANES, LANES)
            x = jnp.concatenate([rim_ref[:, lanes].astype(F32), x_ref[0, :, lanes].astype(F32)], axis=0)
            total = jnp.zeros((BLOCK, LANES), F32)
            for r in range(SHORT):
                total = total + taps_ref[j, r : r + 1, half * LANES : (half + 1) * LANES] * x[8 - r : 8 - r + BLOCK]
            out_ref[:, lanes] = total
        return carry

    lax.fori_loop(0, CH, column, 0)


def query_features(streams, rim, taps):
    return pl.pallas_call(
        query_kernel,
        grid=(1,),
        out_shape=jax.ShapeDtypeStruct((BLOCK, WIDTH), F32),
        in_specs=[
            pl.BlockSpec((1, BLOCK, WIDTH), lambda g: (0, 0, 0)),
            whole_spec((8, WIDTH)),
            pl.BlockSpec((CH, 8, WIDTH // CH), lambda g: (0, 0, 0)),
        ],
        out_specs=whole_spec((BLOCK, WIDTH)),
        cost_estimate=pl.CostEstimate(flops=4_000_000, bytes_accessed=1_000_000, transcendentals=0),
        compiler_params=pltpu.CompilerParams(vmem_limit_bytes=8 * 2**20),
        name="query_features",
    )(streams, rim, taps)


def mix_kernel(long_ref, query_ref, out_ref, before, after):
    def columns(step, carry):
        for at in range(2):
            j = step * 2 + at
            came, gone = before.at[at], after.at[at]
            for half in range(2):
                came[:, half * TILES : (half + 1) * TILES, :] = long_ref[half, :, j].astype(F32)
            tiles = exchange([came[d] for d in range(GROUPS)])
            for t in range(GROUPS):
                gone[pl.ds(t, 8, stride=GROUPS), :] = tiles[t]
            for half in range(2):
                lanes = half_lanes(j, half)
                out_ref[:, lanes] = (gone[half * BLOCK : (half + 1) * BLOCK] * query_ref[:, lanes]).astype(BF16)
        return carry

    lax.fori_loop(0, CH // 2, columns, 0)


def mix(long_part, query):
    return pl.pallas_call(
        mix_kernel,
        out_shape=jax.ShapeDtypeStruct((BLOCK, WIDTH), BF16),
        in_specs=[VMEM] * 2,
        out_specs=VMEM,
        scratch_shapes=[pltpu.VMEM((2, GROUPS, 8, LANES), F32), pltpu.VMEM((2, 2 * BLOCK, LANES), F32)],
        cost_estimate=pl.CostEstimate(flops=4_000_000, bytes_accessed=1_000_000, transcendentals=0),
        compiler_params=pltpu.CompilerParams(vmem_limit_bytes=8 * 2**20),
        name="mix",
    )(long_part, query)


def own_rows(short_weight, skip_gain, row):
    taps = lax.dynamic_slice(short_weight, (0, 1, row * OWN), (SHORT, 2, OWN)).reshape(2 * SHORT, OWN)
    skip = lax.dynamic_slice(skip_gain, (row * OWN,), (OWN,)).reshape(1, OWN)
    rows = jnp.concatenate([taps, skip, jnp.zeros((1, OWN), F32)], axis=0)
    return jnp.tile(rows, (1, GROUPS))


def local(inputs, short_weight, long_filter, skip_gain):
    row = lax.axis_index("ctx")
    ahead, back, fine, coarse, turn_rows, forward, inverse = (jnp.asarray(t) for t in tables())
    streams = jnp.transpose(inputs, (1, 0, 2))
    packed = pack(streams).reshape(DEVICES, 8, LANES)
    packed = lax.all_to_all(packed, ("ctx", "ch"), 0, 0, tiled=True)
    rim = lax.ppermute(streams[0, BLOCK - 8 :], ("ctx", "ch"), [(d, d + 1) for d in range(DEVICES - 1)])
    query_taps = lax.all_gather(jnp.pad(short_weight[:, 0], ((0, 64 - SHORT), (0, 0))), "ch")
    place = jnp.stack([row // GROUPS, row % GROUPS]).astype(jnp.int32)
    gain = filter_transform(place, long_filter, ahead, fine, coarse, turn_rows, forward)
    query = query_features(streams, rim, query_taps)
    taps = own_rows(short_weight, skip_gain, row)
    long_part = convolve(packed, taps, gain, ahead, back, fine, coarse, turn_rows, forward, inverse)
    long_part = lax.all_to_all(long_part, ("ctx", "ch"), 0, 0, tiled=True)
    return mix(long_part.reshape(2, GROUPS, CH, TILES, LANES), query)


def solution(mesh):
    in_specs = (P(("ctx", "ch"), None, None), P(None, None, "ch"), P(None, "ch"), P("ch"))
    out_specs = P(("ctx", "ch"), None)
    return jax.shard_map(local, mesh=mesh, in_specs=in_specs, out_specs=out_specs, check_vma=False)
```

```python
import functools
import math

import jax
import jax.numpy as jnp
import ml_dtypes
import numpy as np
from jax import lax
from jax.experimental import pallas as pl
from jax.experimental.pallas import tpu as pltpu
from jax.sharding import PartitionSpec as P

SHORT = 7
CTX = 16
CH = 16
DEVICES = CTX * CH
BLOCK = 32
LANES = 128
OWN = 16
GROUPS = LANES // OWN
TILES = BLOCK // GROUPS
LENGTH = DEVICES * BLOCK
WIDTH = DEVICES * OWN
CHUNK = 16
ROWS = DEVICES
F32 = jnp.float32
VMEM = pl.BlockSpec(memory_space=pltpu.VMEM)
BF16 = jnp.bfloat16


def halves(table):
    upper = table.astype(ml_dtypes.bfloat16)
    lower = (table - upper.astype(np.float64)).astype(ml_dtypes.bfloat16)
    return upper, lower


@functools.lru_cache(maxsize=None)
def tables():
    turn = 2.0 * math.pi
    freq = (np.arange(ROWS) + 0.5) / (2 * ROWS)
    block = np.arange(ROWS)
    angle = turn * freq[:, None] * block[None, :]
    first = np.concatenate([np.cos(angle), -np.sin(angle)], axis=0)
    upper, lower = halves(first)
    ahead = np.concatenate([upper, lower], axis=1)

    last = np.concatenate([np.cos(angle), -np.sin(angle)], axis=0).T * (2.0 / (2 * LENGTH))
    upper, lower = halves(last)
    back = np.concatenate([upper, lower], axis=1)

    lane = np.arange(LANES)
    place = (np.arange(TILES)[:, None] * GROUPS + lane[None, :] // OWN).reshape(-1)
    fine = turn * freq[:CHUNK, None] * place[None, :] / BLOCK
    coarse = turn * (np.arange(ROWS // CHUNK) * CHUNK / (2 * ROWS))[:, None] * place[None, :] / BLOCK
    fine = np.concatenate([np.cos(fine), -np.sin(fine)], axis=1).astype(np.float32)
    coarse = np.concatenate([np.cos(coarse), -np.sin(coarse)], axis=1).astype(np.float32).reshape(-1, 2 * TILES, LANES)

    angle = turn * np.arange(TILES)[:, None] * (lane[None, :] // OWN) / BLOCK
    turn_rows = np.concatenate([np.cos(angle), -np.sin(angle)], axis=0).astype(np.float32)

    same = (lane[:, None] % OWN) == (lane[None, :] % OWN)
    angle = turn * (lane[:, None] // OWN) * (lane[None, :] // OWN) / GROUPS
    cosine = np.where(same, np.cos(angle), 0.0)
    sine = np.where(same, np.sin(angle), 0.0)
    forward = np.block([[cosine, -sine], [sine, cosine]])
    inverse = np.block([[cosine, sine], [-sine, cosine]])
    upper, lower = halves(forward)
    forward = np.concatenate([upper, lower], axis=0)
    upper, lower = halves(inverse)
    inverse = np.concatenate([upper, lower], axis=0)
    return ahead, back, fine, coarse, turn_rows, forward, inverse


def dot(left, right):
    return jnp.dot(left, right, preferred_element_type=F32)


def split(value):
    upper = value.astype(BF16)
    return upper, (value - upper.astype(F32)).astype(BF16)


def exchange(tiles):
    group = lax.broadcasted_iota(jnp.int32, (GROUPS, LANES), 1) // OWN
    for step in (4, 2, 1):
        low = (group // step) % 2 == 0
        shift = step * OWN
        moved = list(tiles)
        for t in range(GROUPS):
            if t & step == 0:
                a, b = tiles[t], tiles[t + step]
                if step == 4:
                    across = pltpu.roll(jnp.where(low, b, a), shift, 1)
                    moved[t], moved[t + step] = jnp.where(low, a, across), jnp.where(low, across, b)
                else:
                    moved[t] = jnp.where(low, a, pltpu.roll(b, shift, 1))
                    moved[t + step] = jnp.where(low, pltpu.roll(a, LANES - shift, 1), b)
        tiles = moved
    return tiles


def half_lanes(j, half):
    return pl.ds(pl.multiple_of(j * 2 * LANES, LANES) + half * LANES, LANES)


def pack_kernel(k_ref, v_ref, out_ref, scratch):
    def columns(step, carry):
        for at in range(2):
            j = step * 2 + at
            for half in range(2):
                slot = scratch.at[at * 2 + half]
                for s, ref in enumerate((k_ref, v_ref)):
                    slot[s * BLOCK : (s + 1) * BLOCK] = ref[0, :, half_lanes(j, half)].astype(F32)
                tiles = exchange([slot[pl.ds(t, 8, stride=GROUPS), :] for t in range(GROUPS)])
                for d in range(GROUPS):
                    out_ref[half, d, j] = tiles[d].astype(BF16)
        return carry

    lax.fori_loop(0, CH // 2, columns, 0)


def pack(streams):
    whole = (1, BLOCK, WIDTH)
    return pl.pallas_call(
        pack_kernel,
        grid=(1,),
        out_shape=jax.ShapeDtypeStruct((2, GROUPS, CH, 8, LANES), BF16),
        in_specs=[pl.BlockSpec(whole, lambda g: (1, 0, 0)), pl.BlockSpec(whole, lambda g: (2, 0, 0))],
        out_specs=pl.BlockSpec((2, GROUPS, CH, 8, LANES), lambda g: (0, 0, 0, 0, 0)),
        scratch_shapes=[pltpu.VMEM((4, 2 * BLOCK, LANES), F32)],
        cost_estimate=pl.CostEstimate(flops=4_000_000, bytes_accessed=1_100_000, transcendentals=0),
        compiler_params=pltpu.CompilerParams(vmem_limit_bytes=8 * 2**20),
        name="pack",
    )(streams, streams)


def spin_rows(fine, coarse, step):
    rows = coarse[step]
    spins = []
    for q in range(TILES):
        re = slice(q * LANES, (q + 1) * LANES)
        im = slice((TILES + q) * LANES, (TILES + q + 1) * LANES)
        a, b = fine[:, re], fine[:, im]
        c, d = rows[q : q + 1], rows[TILES + q : TILES + q + 1]
        spins.append((a * c - b * d, a * d + b * c))
    return spins


def table_dot(parts, table):
    upper = table[0:256]
    return dot(parts[:, 0:256], upper) + dot(parts[:, 256:512], upper) + dot(parts[:, 0:256], table[256:512])


def forward_transform(signal, ahead, fine, coarse, turn_rows, forward, stage, parts, out_ref):
    stage[...] = dot(ahead[...], signal[...])

    def rows(step, carry):
        at = pl.multiple_of(step * 16, 16)
        here, below = pl.ds(at, 16), pl.ds(at + ROWS, 16)
        spins = spin_rows(fine, coarse, step)
        real, imag = [], []
        for q in range(TILES):
            lanes = slice(q * LANES, (q + 1) * LANES)
            a, b = stage[here, lanes], stage[below, lanes]
            c, d = spins[q]
            real.append(a * c - b * d)
            imag.append(a * d + b * c)
        er, ei = real[0] + real[2], imag[0] + imag[2]
        fr, fi = real[0] - real[2], imag[0] - imag[2]
        gr, gi = real[1] + real[3], imag[1] + imag[3]
        hr, hi = real[1] - real[3], imag[1] - imag[3]
        outs = ((er + gr, ei + gi), (fr + hi, fi - hr), (er - gr, ei - gi), (fr - hi, fi + hr))
        for k, (a, b) in enumerate(outs):
            if k > 0:
                c, d = turn_rows[k : k + 1], turn_rows[TILES + k : TILES + k + 1]
                a, b = a * c - b * d, a * d + b * c
            to = pl.ds(at + k * ROWS, 16)
            parts[to, 0:128], parts[to, 256:384] = split(a)
            parts[to, 128:256], parts[to, 384:512] = split(b)
        return carry

    lax.fori_loop(0, ROWS // 16, rows, 0)
    out_ref[...] = table_dot(parts, forward)


def filter_kernel(place, filter_ref, ahead, fine, coarse, turn_rows, forward, out_ref, wide, signal, stage, parts):
    step = pl.program_id(0)
    shift = place[1]
    wide[...] = filter_ref[...].astype(F32)
    group = lax.broadcasted_iota(jnp.int32, (BLOCK, LANES), 1) // OWN
    at = pl.multiple_of(step * BLOCK, BLOCK)
    for q in range(TILES):
        tile = jnp.zeros((BLOCK, LANES), F32)
        for t in range(GROUPS):
            rows = wide[pl.ds(q * GROUPS + t, BLOCK, stride=BLOCK), :]
            if t > 0:
                rows = pltpu.roll(rows, t * OWN, 1)
            tile = jnp.where(group == (shift + t) % GROUPS, rows, tile)
        tile = pltpu.roll(tile, (GROUPS - shift) % GROUPS * OWN, 1).astype(BF16)
        signal[pl.ds(at, BLOCK), q * LANES : (q + 1) * LANES] = tile
        signal[pl.ds(at + ROWS, BLOCK), q * LANES : (q + 1) * LANES] = tile

    @pl.when(step == pl.num_programs(0) - 1)
    def _():
        forward_transform(signal, ahead, fine, coarse, turn_rows, forward, stage, parts, out_ref)


def whole_spec(shape):
    return pl.BlockSpec(shape, lambda *_: (0,) * len(shape))


def filter_transform(place, long_filter, ahead, fine, coarse, turn_rows, forward):
    chunk = BLOCK * BLOCK
    consts = (ahead, fine, coarse, turn_rows, forward)
    return pl.pallas_call(
        filter_kernel,
        out_shape=jax.ShapeDtypeStruct((TILES * ROWS, 2 * LANES), F32),
        grid_spec=pltpu.PrefetchScalarGridSpec(
            num_scalar_prefetch=1,
            grid=(LENGTH // chunk,),
            in_specs=[pl.BlockSpec((chunk, LANES), lambda g, s: (g, s[0]))] + [whole_spec(c.shape) for c in consts],
            out_specs=whole_spec((TILES * ROWS, 2 * LANES)),
            scratch_shapes=[
                pltpu.VMEM((chunk, LANES), F32),
                pltpu.VMEM((2 * ROWS, TILES * LANES), BF16),
                pltpu.VMEM((2 * ROWS, TILES * LANES), F32),
                pltpu.VMEM((TILES * ROWS, 4 * LANES), BF16),
            ],
        ),
        cost_estimate=pl.CostEstimate(flops=2_000_000_000, bytes_accessed=6_000_000, transcendentals=0),
        compiler_params=pltpu.CompilerParams(vmem_limit_bytes=58 * 2**20),
        name="filter_transform",
    )(place, long_filter, *consts)


def conv_kernel(
    packed, taps, gain, ahead, back, fine, coarse, turn_rows, forward, inverse, out_ref,
    wide, signal, stage, parts, product, result,
):
    pad = 8
    wide[0:pad] = jnp.zeros((pad, LANES), F32)
    wide[pad:] = packed[...].astype(F32).reshape(DEVICES * 8, LANES)
    lane = lax.broadcasted_iota(jnp.int32, (BLOCK, LANES), 1)

    def gate(step, carry):
        at = step * BLOCK
        streams = []
        for s in range(2):
            base = pl.multiple_of(at * 8, 8)
            tiles = [wide[pl.ds(base + s * TILES + TILES - 1, BLOCK, stride=8), :]]
            for q in range(TILES):
                tiles.append(wide[pl.ds(base + pad + s * TILES + q, BLOCK, stride=8), :])
            sums = []
            for q in range(TILES):
                total = taps[s : s + 1] * tiles[q + 1]
                for r in range(1, SHORT):
                    shifted = jnp.where(lane < LANES - OWN * r, tiles[q + 1], tiles[q])
                    total = total + taps[2 * r + s : 2 * r + s + 1] * pltpu.roll(shifted, OWN * r, 1)
                sums.append(total)
            streams.append(sums)
        to = pl.multiple_of(at, BLOCK)
        for q in range(TILES):
            gated = (streams[0][q] * streams[1][q]).astype(BF16)
            signal[pl.ds(to, BLOCK), q * LANES : (q + 1) * LANES] = gated
            signal[pl.ds(to + ROWS, BLOCK), q * LANES : (q + 1) * LANES] = gated
        return carry

    lax.fori_loop(0, ROWS // BLOCK, gate, 0)
    forward_transform(signal, ahead, fine, coarse, turn_rows, forward, stage, parts, product)

    def multiply(step, carry):
        here = pl.ds(pl.multiple_of(step * 32, 32), 32)
        a, b = product[here, 0:128], product[here, 128:256]
        c, d = gain[here, 0:128], gain[here, 128:256]
        parts[here, 0:128], parts[here, 256:384] = split(a * c - b * d)
        parts[here, 128:256], parts[here, 384:512] = split(a * d + b * c)
        return carry

    lax.fori_loop(0, TILES * ROWS // 32, multiply, 0)
    product[...] = table_dot(parts, inverse)

    def unspin(step, carry):
        at = pl.multiple_of(step * 16, 16)
        spins = spin_rows(fine, coarse, step)
        real, imag = [], []
        for k in range(TILES):
            rows = pl.ds(at + k * ROWS, 16)
            a, b = product[rows, 0:128], product[rows, 128:256]
            if k > 0:
                c, d = turn_rows[k : k + 1], turn_rows[TILES + k : TILES + k + 1]
                a, b = a * c + b * d, b * c - a * d
            real.append(a)
            imag.append(b)
        er, ei = real[0] + real[2], imag[0] + imag[2]
        fr, fi = real[0] - real[2], imag[0] - imag[2]
        gr, gi = real[1] + real[3], imag[1] + imag[3]
        hr, hi = real[1] - real[3], imag[1] - imag[3]
        outs = ((er + gr, ei + gi), (fr - hi, fi + hr), (er - gr, ei - gi), (fr + hi, fi - hr))
        for q, (a, b) in enumerate(outs):
            lanes = slice(q * LANES, (q + 1) * LANES)
            c, d = spins[q]
            parts[pl.ds(at, 16), lanes], parts[pl.ds(at + 2 * ROWS, 16), lanes] = split(a * c + b * d)
            parts[pl.ds(at + ROWS, 16), lanes], parts[pl.ds(at + 3 * ROWS, 16), lanes] = split(b * c - a * d)
        return carry

    lax.fori_loop(0, ROWS // 16, unspin, 0)
    skip = taps[2 * SHORT : 2 * SHORT + 1]
    for q in range(TILES):
        lanes = slice(q * LANES, (q + 1) * LANES)
        upper, lower = parts[0:512, lanes], parts[512:1024, lanes]
        long_part = dot(back[:, 0:512], upper) + dot(back[:, 0:512], lower) + dot(back[:, 512:1024], upper)
        total = long_part + skip * signal[0:ROWS, lanes].astype(F32)
        result[pl.ds(q, ROWS, stride=TILES), :] = total
    out_ref[...] = result[...].reshape(DEVICES, TILES, LANES).astype(BF16)


def convolve(packed, taps, gain, ahead, back, fine, coarse, turn_rows, forward, inverse):
    return pl.pallas_call(
        conv_kernel,
        out_shape=jax.ShapeDtypeStruct((DEVICES, TILES, LANES), BF16),
        in_specs=[VMEM] * 10,
        out_specs=VMEM,
        scratch_shapes=[
            pltpu.VMEM((8 + DEVICES * 8, LANES), F32),
            pltpu.VMEM((2 * ROWS, TILES * LANES), BF16),
            pltpu.VMEM((2 * ROWS, TILES * LANES), F32),
            pltpu.VMEM((TILES * ROWS, 4 * LANES), BF16),
            pltpu.VMEM((TILES * ROWS, 2 * LANES), F32),
            pltpu.VMEM((DEVICES * TILES, LANES), F32),
        ],
        cost_estimate=pl.CostEstimate(flops=4_000_000_000, bytes_accessed=6_000_000, transcendentals=0),
        compiler_params=pltpu.CompilerParams(vmem_limit_bytes=24 * 2**20),
        name="convolve",
    )(packed, taps, gain, ahead, back, fine, coarse, turn_rows, forward, inverse)


def query_kernel(x_ref, rim_ref, taps_ref, out_ref):
    def column(j, carry):
        for half in range(2):
            lanes = pl.ds(pl.multiple_of(j * 2 * LANES, LANES) + half * LANES, LANES)
            x = jnp.concatenate([rim_ref[:, lanes].astype(F32), x_ref[0, :, lanes].astype(F32)], axis=0)
            total = jnp.zeros((BLOCK, LANES), F32)
            for r in range(SHORT):
                total = total + taps_ref[j, r : r + 1, half * LANES : (half + 1) * LANES] * x[8 - r : 8 - r + BLOCK]
            out_ref[:, lanes] = total
        return carry

    lax.fori_loop(0, CH, column, 0)


def query_features(streams, rim, taps):
    return pl.pallas_call(
        query_kernel,
        grid=(1,),
        out_shape=jax.ShapeDtypeStruct((BLOCK, WIDTH), F32),
        in_specs=[
            pl.BlockSpec((1, BLOCK, WIDTH), lambda g: (0, 0, 0)),
            whole_spec((8, WIDTH)),
            whole_spec((CH, SHORT, WIDTH // CH)),
        ],
        out_specs=whole_spec((BLOCK, WIDTH)),
        cost_estimate=pl.CostEstimate(flops=4_000_000, bytes_accessed=1_000_000, transcendentals=0),
        compiler_params=pltpu.CompilerParams(vmem_limit_bytes=8 * 2**20),
        name="query_features",
    )(streams, rim, taps)


def mix_kernel(long_ref, query_ref, out_ref, before, after):
    def columns(step, carry):
        for at in range(2):
            j = step * 2 + at
            came, gone = before.at[at], after.at[at]
            for half in range(2):
                came[:, half * TILES : (half + 1) * TILES, :] = long_ref[half, :, j].astype(F32)
            tiles = exchange([came[d] for d in range(GROUPS)])
            for t in range(GROUPS):
                gone[pl.ds(t, 8, stride=GROUPS), :] = tiles[t]
            for half in range(2):
                lanes = half_lanes(j, half)
                out_ref[:, lanes] = (gone[half * BLOCK : (half + 1) * BLOCK] * query_ref[:, lanes]).astype(BF16)
        return carry

    lax.fori_loop(0, CH // 2, columns, 0)


def mix(long_part, query):
    return pl.pallas_call(
        mix_kernel,
        out_shape=jax.ShapeDtypeStruct((BLOCK, WIDTH), BF16),
        in_specs=[VMEM] * 2,
        out_specs=VMEM,
        scratch_shapes=[pltpu.VMEM((2, GROUPS, 8, LANES), F32), pltpu.VMEM((2, 2 * BLOCK, LANES), F32)],
        cost_estimate=pl.CostEstimate(flops=4_000_000, bytes_accessed=1_000_000, transcendentals=0),
        compiler_params=pltpu.CompilerParams(vmem_limit_bytes=8 * 2**20),
        name="mix",
    )(long_part, query)


def own_rows(short_weight, skip_gain, row):
    taps = lax.dynamic_slice(short_weight, (0, 1, row * OWN), (SHORT, 2, OWN)).reshape(2 * SHORT, OWN)
    skip = lax.dynamic_slice(skip_gain, (row * OWN,), (OWN,)).reshape(1, OWN)
    rows = jnp.concatenate([taps, skip, jnp.zeros((1, OWN), F32)], axis=0)
    return jnp.tile(rows, (1, GROUPS))


def local(inputs, short_weight, long_filter, skip_gain):
    row = lax.axis_index("ctx")
    ahead, back, fine, coarse, turn_rows, forward, inverse = (jnp.asarray(t) for t in tables())
    streams = jnp.transpose(inputs, (1, 0, 2))
    packed = pack(streams).reshape(DEVICES, 8, LANES)
    query_taps, last_rows, packed = lax.optimization_barrier((short_weight[:, 0], streams[0, BLOCK - 8 :], packed))
    packed = lax.all_to_all(packed, ("ctx", "ch"), 0, 0, tiled=True)
    rim = lax.ppermute(last_rows, ("ctx", "ch"), [(d, d + 1) for d in range(DEVICES - 1)])
    near = [[4 * g + d for d in range(4)] for g in range(4)]
    far = [[4 * d + g for d in range(4)] for g in range(4)]
    query_taps = lax.all_gather(query_taps, "ch", axis_index_groups=near)
    query_taps = lax.all_gather(query_taps, "ch", axis_index_groups=far).reshape(CH, SHORT, WIDTH // CH)
    place = jnp.stack([row // GROUPS, row % GROUPS]).astype(jnp.int32)
    gain = filter_transform(place, long_filter, ahead, fine, coarse, turn_rows, forward)
    query = query_features(streams, rim, query_taps)
    taps = own_rows(short_weight, skip_gain, row)
    packed, query = lax.optimization_barrier((packed, query))
    long_part = convolve(packed, taps, gain, ahead, back, fine, coarse, turn_rows, forward, inverse)
    long_part = lax.all_to_all(long_part, ("ctx", "ch"), 0, 0, tiled=True)
    return mix(long_part.reshape(2, GROUPS, CH, TILES, LANES), query)


def solution(mesh):
    in_specs = (P(("ctx", "ch"), None, None), P(None, None, "ch"), P(None, "ch"), P("ch"))
    out_specs = P(("ctx", "ch"), None)
    return jax.shard_map(local, mesh=mesh, in_specs=in_specs, out_specs=out_specs, check_vma=False)
```

```python
import functools
import math

import jax
import jax.numpy as jnp
import ml_dtypes
import numpy as np
from jax import lax
from jax.experimental import pallas as pl
from jax.experimental.pallas import tpu as pltpu
from jax.sharding import PartitionSpec as P

SHORT = 7
STREAMS = 3
CTX = 16
CH = 16
DEVICES = CTX * CH
BLOCK = 32
LANES = 128
OWN = 16
GROUPS = LANES // OWN
TILES = BLOCK // GROUPS
LENGTH = DEVICES * BLOCK
WIDTH = DEVICES * OWN
PACK = 4
CHUNK = 16
ROWS = DEVICES
F32 = jnp.float32
VMEM = pl.BlockSpec(memory_space=pltpu.VMEM)
BF16 = jnp.bfloat16


def halves(table):
    upper = table.astype(ml_dtypes.bfloat16)
    lower = (table - upper.astype(np.float64)).astype(ml_dtypes.bfloat16)
    return upper, lower


@functools.lru_cache(maxsize=None)
def tables():
    turn = 2.0 * math.pi
    freq = (np.arange(ROWS) + 0.5) / (2 * ROWS)
    block = np.arange(ROWS)
    angle = turn * freq[:, None] * block[None, :]
    first = np.concatenate([np.cos(angle), -np.sin(angle)], axis=0)
    upper, lower = halves(first)
    ahead = np.concatenate([upper, lower], axis=1)

    last = np.concatenate([np.cos(angle), -np.sin(angle)], axis=0).T * (2.0 / (2 * LENGTH))
    upper, lower = halves(last)
    back = np.concatenate([upper, lower], axis=1)

    lane = np.arange(LANES)
    place = (np.arange(TILES)[:, None] * GROUPS + lane[None, :] // OWN).reshape(-1)
    fine = turn * freq[:CHUNK, None] * place[None, :] / BLOCK
    coarse = turn * (np.arange(ROWS // CHUNK) * CHUNK / (2 * ROWS))[:, None] * place[None, :] / BLOCK
    fine = np.concatenate([np.cos(fine), -np.sin(fine)], axis=1).astype(np.float32)
    coarse = np.concatenate([np.cos(coarse), -np.sin(coarse)], axis=1).astype(np.float32).reshape(-1, 2 * TILES, LANES)

    angle = turn * np.arange(TILES)[:, None] * (lane[None, :] // OWN) / BLOCK
    turn_rows = np.concatenate([np.cos(angle), -np.sin(angle)], axis=0).astype(np.float32)

    same = (lane[:, None] % OWN) == (lane[None, :] % OWN)
    angle = turn * (lane[:, None] // OWN) * (lane[None, :] // OWN) / GROUPS
    cosine = np.where(same, np.cos(angle), 0.0)
    sine = np.where(same, np.sin(angle), 0.0)
    forward = np.block([[cosine, -sine], [sine, cosine]])
    inverse = np.block([[cosine, sine], [-sine, cosine]])
    upper, lower = halves(forward)
    forward = np.concatenate([upper, lower], axis=0)
    upper, lower = halves(inverse)
    inverse = np.concatenate([upper, lower], axis=0)
    return ahead, back, fine, coarse, turn_rows, forward, inverse


def dot(left, right):
    return jnp.dot(left, right, preferred_element_type=F32)


def split(value):
    upper = value.astype(BF16)
    return upper, (value - upper.astype(F32)).astype(BF16)


def exchange(tiles):
    group = lax.broadcasted_iota(jnp.int32, (GROUPS, LANES), 1) // OWN
    for step in (4, 2, 1):
        low = (group // step) % 2 == 0
        shift = step * OWN
        moved = list(tiles)
        for t in range(GROUPS):
            if t & step == 0:
                a, b = tiles[t], tiles[t + step]
                if step == 4:
                    across = pltpu.roll(jnp.where(low, b, a), shift, 1)
                    moved[t], moved[t + step] = jnp.where(low, a, across), jnp.where(low, across, b)
                else:
                    moved[t] = jnp.where(low, a, pltpu.roll(b, shift, 1))
                    moved[t + step] = jnp.where(low, pltpu.roll(a, LANES - shift, 1), b)
        tiles = moved
    return tiles


def half_lanes(j, half):
    return pl.ds(pl.multiple_of(j * 2 * LANES, LANES) + half * LANES, LANES)


def pack_kernel(q_ref, k_ref, v_ref, out_ref, scratch):
    for j in range(PACK):
        for half in range(2):
            slot = scratch.at[j % 2 * 3 + half]
            lanes = slice((2 * j + half) * LANES, (2 * j + half + 1) * LANES)
            slot[0:BLOCK] = k_ref[0, :, lanes].astype(F32)
            slot[BLOCK : 2 * BLOCK] = v_ref[0, :, lanes].astype(F32)
            tiles = exchange([slot[pl.ds(t, 8, stride=GROUPS), :] for t in range(GROUPS)])
            for d in range(GROUPS):
                out_ref[half, d, j, 0] = tiles[d][0:TILES].astype(BF16)
                out_ref[half, d, j, 1] = tiles[d][TILES:].astype(BF16)
        slot = scratch.at[j % 2 * 3 + 2]
        for half in range(2):
            lanes = slice((2 * j + half) * LANES, (2 * j + half + 1) * LANES)
            slot[half * BLOCK : (half + 1) * BLOCK] = q_ref[0, :, lanes].astype(F32)
        tiles = exchange([slot[pl.ds(t, 8, stride=GROUPS), :] for t in range(GROUPS)])
        for d in range(GROUPS):
            out_ref[0, d, j, 2] = tiles[d][0:TILES].astype(BF16)
            out_ref[1, d, j, 2] = tiles[d][TILES:].astype(BF16)


def pack(streams):
    lanes = PACK * 2 * LANES
    part = (1, BLOCK, lanes)
    return pl.pallas_call(
        pack_kernel,
        grid=(CH // PACK,),
        out_shape=jax.ShapeDtypeStruct((2, GROUPS, CH, 3, TILES, LANES), BF16),
        in_specs=[pl.BlockSpec(part, lambda g, s=s: (s, 0, g)) for s in range(3)],
        out_specs=pl.BlockSpec((2, GROUPS, PACK, 3, TILES, LANES), lambda g: (0, 0, g, 0, 0, 0)),
        scratch_shapes=[pltpu.VMEM((6, 2 * BLOCK, LANES), F32)],
        cost_estimate=pl.CostEstimate(flops=4_000_000, bytes_accessed=1_600_000, transcendentals=0),
        compiler_params=pltpu.CompilerParams(vmem_limit_bytes=58 * 2**20),
        name="pack",
    )(streams, streams, streams)


def spin_rows(fine, coarse, step):
    rows = coarse[step]
    spins = []
    for q in range(TILES):
        re = slice(q * LANES, (q + 1) * LANES)
        im = slice((TILES + q) * LANES, (TILES + q + 1) * LANES)
        a, b = fine[:, re], fine[:, im]
        c, d = rows[q : q + 1], rows[TILES + q : TILES + q + 1]
        spins.append((a * c - b * d, a * d + b * c))
    return spins


def table_dot(parts, table):
    upper = table[0:256]
    return dot(parts[:, 0:256], upper) + dot(parts[:, 256:512], upper) + dot(parts[:, 0:256], table[256:512])


def forward_transform(signal, ahead, fine, coarse, turn_rows, forward, stage, parts, out_ref):
    stage[...] = dot(ahead[...], signal[...])

    def rows(step, carry):
        at = pl.multiple_of(step * 16, 16)
        here, below = pl.ds(at, 16), pl.ds(at + ROWS, 16)
        spins = spin_rows(fine, coarse, step)
        real, imag = [], []
        for q in range(TILES):
            lanes = slice(q * LANES, (q + 1) * LANES)
            a, b = stage[here, lanes], stage[below, lanes]
            c, d = spins[q]
            real.append(a * c - b * d)
            imag.append(a * d + b * c)
        er, ei = real[0] + real[2], imag[0] + imag[2]
        fr, fi = real[0] - real[2], imag[0] - imag[2]
        gr, gi = real[1] + real[3], imag[1] + imag[3]
        hr, hi = real[1] - real[3], imag[1] - imag[3]
        outs = ((er + gr, ei + gi), (fr + hi, fi - hr), (er - gr, ei - gi), (fr - hi, fi + hr))
        for k, (a, b) in enumerate(outs):
            if k > 0:
                c, d = turn_rows[k : k + 1], turn_rows[TILES + k : TILES + k + 1]
                a, b = a * c - b * d, a * d + b * c
            to = pl.ds(at + k * ROWS, 16)
            parts[to, 0:128], parts[to, 256:384] = split(a)
            parts[to, 128:256], parts[to, 384:512] = split(b)
        return carry

    lax.fori_loop(0, ROWS // 16, rows, 0)
    out_ref[...] = table_dot(parts, forward)


def filter_kernel(place, filter_ref, ahead, fine, coarse, turn_rows, forward, out_ref, wide, signal, stage, parts):
    step = pl.program_id(0)
    shift = place[1]
    wide[...] = filter_ref[...].astype(F32)
    group = lax.broadcasted_iota(jnp.int32, (BLOCK, LANES), 1) // OWN
    at = pl.multiple_of(step * BLOCK, BLOCK)
    for q in range(TILES):
        tile = jnp.zeros((BLOCK, LANES), F32)
        for t in range(GROUPS):
            rows = wide[pl.ds(q * GROUPS + t, BLOCK, stride=BLOCK), :]
            if t > 0:
                rows = pltpu.roll(rows, t * OWN, 1)
            tile = jnp.where(group == (shift + t) % GROUPS, rows, tile)
        tile = pltpu.roll(tile, (GROUPS - shift) % GROUPS * OWN, 1).astype(BF16)
        signal[pl.ds(at, BLOCK), q * LANES : (q + 1) * LANES] = tile
        signal[pl.ds(at + ROWS, BLOCK), q * LANES : (q + 1) * LANES] = tile

    @pl.when(step == pl.num_programs(0) - 1)
    def _():
        forward_transform(signal, ahead, fine, coarse, turn_rows, forward, stage, parts, out_ref)


def whole_spec(shape):
    return pl.BlockSpec(shape, lambda *_: (0,) * len(shape))


def filter_transform(place, long_filter, ahead, fine, coarse, turn_rows, forward):
    chunk = BLOCK * BLOCK
    consts = (ahead, fine, coarse, turn_rows, forward)
    return pl.pallas_call(
        filter_kernel,
        out_shape=jax.ShapeDtypeStruct((TILES * ROWS, 2 * LANES), F32),
        grid_spec=pltpu.PrefetchScalarGridSpec(
            num_scalar_prefetch=1,
            grid=(LENGTH // chunk,),
            in_specs=[pl.BlockSpec((chunk, LANES), lambda g, s: (g, s[0]))] + [whole_spec(c.shape) for c in consts],
            out_specs=whole_spec((TILES * ROWS, 2 * LANES)),
            scratch_shapes=[
                pltpu.VMEM((chunk, LANES), F32),
                pltpu.VMEM((2 * ROWS, TILES * LANES), BF16),
                pltpu.VMEM((2 * ROWS, TILES * LANES), F32),
                pltpu.VMEM((TILES * ROWS, 4 * LANES), BF16),
            ],
        ),
        cost_estimate=pl.CostEstimate(flops=2_000_000_000, bytes_accessed=6_000_000, transcendentals=0),
        compiler_params=pltpu.CompilerParams(vmem_limit_bytes=58 * 2**20),
        name="filter_transform",
    )(place, long_filter, *consts)


def conv_kernel(
    packed, taps, gain, ahead, back, fine, coarse, turn_rows, forward, inverse, out_ref,
    wide, wide_q, signal, query, stage, parts, product, result,
):
    wide[0] = jnp.zeros((8, LANES), F32)
    wide_q[0] = jnp.zeros((TILES, LANES), F32)
    wide[1:, 0:TILES] = packed[:, 0].astype(F32)
    wide[1:, TILES:] = packed[:, 1].astype(F32)
    wide_q[1:] = packed[:, 2].astype(F32)
    lane = lax.broadcasted_iota(jnp.int32, (CHUNK, LANES), 1)

    def features(ref, at, base, stream):
        tiles = [ref[pl.ds(at, CHUNK), base + TILES - 1, :]]
        for q in range(TILES):
            tiles.append(ref[pl.ds(at + 1, CHUNK), base + q, :])
        sums = []
        for q in range(TILES):
            total = taps[stream : stream + 1] * tiles[q + 1]
            for r in range(1, SHORT):
                row = STREAMS * r + stream
                shifted = jnp.where(lane < LANES - OWN * r, tiles[q + 1], tiles[q])
                total = total + taps[row : row + 1] * pltpu.roll(shifted, OWN * r, 1)
            sums.append(total)
        return sums

    def gate(step, carry):
        at = pl.multiple_of(step * CHUNK, CHUNK)
        left = features(wide, at, 0, 1)
        right = features(wide, at, TILES, 2)
        for q in range(TILES):
            gated = (left[q] * right[q]).astype(BF16)
            signal[pl.ds(at, CHUNK), q * LANES : (q + 1) * LANES] = gated
            signal[pl.ds(at + ROWS, CHUNK), q * LANES : (q + 1) * LANES] = gated
        outer = features(wide_q, at, 0, 0)
        for q in range(TILES):
            query[pl.ds(at, CHUNK), q * LANES : (q + 1) * LANES] = outer[q]
        return carry

    lax.fori_loop(0, ROWS // CHUNK, gate, 0)
    forward_transform(signal, ahead, fine, coarse, turn_rows, forward, stage, parts, product)

    def multiply(step, carry):
        here = pl.ds(pl.multiple_of(step * 32, 32), 32)
        a, b = product[here, 0:128], product[here, 128:256]
        c, d = gain[here, 0:128], gain[here, 128:256]
        parts[here, 0:128], parts[here, 256:384] = split(a * c - b * d)
        parts[here, 128:256], parts[here, 384:512] = split(a * d + b * c)
        return carry

    lax.fori_loop(0, TILES * ROWS // 32, multiply, 0)
    product[...] = table_dot(parts, inverse)

    def unspin(step, carry):
        at = pl.multiple_of(step * 16, 16)
        spins = spin_rows(fine, coarse, step)
        real, imag = [], []
        for k in range(TILES):
            rows = pl.ds(at + k * ROWS, 16)
            a, b = product[rows, 0:128], product[rows, 128:256]
            if k > 0:
                c, d = turn_rows[k : k + 1], turn_rows[TILES + k : TILES + k + 1]
                a, b = a * c + b * d, b * c - a * d
            real.append(a)
            imag.append(b)
        er, ei = real[0] + real[2], imag[0] + imag[2]
        fr, fi = real[0] - real[2], imag[0] - imag[2]
        gr, gi = real[1] + real[3], imag[1] + imag[3]
        hr, hi = real[1] - real[3], imag[1] - imag[3]
        outs = ((er + gr, ei + gi), (fr - hi, fi + hr), (er - gr, ei - gi), (fr + hi, fi - hr))
        for q, (a, b) in enumerate(outs):
            lanes = slice(q * LANES, (q + 1) * LANES)
            c, d = spins[q]
            parts[pl.ds(at, 16), lanes], parts[pl.ds(at + 2 * ROWS, 16), lanes] = split(a * c + b * d)
            parts[pl.ds(at + ROWS, 16), lanes], parts[pl.ds(at + 3 * ROWS, 16), lanes] = split(b * c - a * d)
        return carry

    lax.fori_loop(0, ROWS // 16, unspin, 0)
    skip = taps[STREAMS * SHORT : STREAMS * SHORT + 1]
    for q in range(TILES):
        lanes = slice(q * LANES, (q + 1) * LANES)
        upper, lower = parts[0:512, lanes], parts[512:1024, lanes]
        long_part = dot(back[:, 0:512], upper) + dot(back[:, 0:512], lower) + dot(back[:, 512:1024], upper)
        total = query[:, lanes] * (long_part + skip * signal[0:ROWS, lanes].astype(F32))
        result[pl.ds(q, ROWS, stride=TILES), :] = total
    out_ref[...] = result[...].reshape(DEVICES, TILES, LANES).astype(BF16)


def convolve(packed, taps, gain, ahead, back, fine, coarse, turn_rows, forward, inverse):
    return pl.pallas_call(
        conv_kernel,
        out_shape=jax.ShapeDtypeStruct((DEVICES, TILES, LANES), BF16),
        in_specs=[VMEM] * 10,
        out_specs=VMEM,
        scratch_shapes=[
            pltpu.VMEM((1 + DEVICES, 8, LANES), F32),
            pltpu.VMEM((1 + DEVICES, TILES, LANES), F32),
            pltpu.VMEM((2 * ROWS, TILES * LANES), BF16),
            pltpu.VMEM((ROWS, TILES * LANES), F32),
            pltpu.VMEM((2 * ROWS, TILES * LANES), F32),
            pltpu.VMEM((TILES * ROWS, 4 * LANES), BF16),
            pltpu.VMEM((TILES * ROWS, 2 * LANES), F32),
            pltpu.VMEM((DEVICES * TILES, LANES), F32),
        ],
        cost_estimate=pl.CostEstimate(flops=4_000_000_000, bytes_accessed=6_000_000, transcendentals=0),
        compiler_params=pltpu.CompilerParams(vmem_limit_bytes=24 * 2**20),
        name="convolve",
    )(packed, taps, gain, ahead, back, fine, coarse, turn_rows, forward, inverse)


def unpack_kernel(mixed_ref, out_ref, before, after):
    def columns(step, carry):
        for at in range(2):
            j = step * 2 + at
            came, gone = before.at[at], after.at[at]
            for half in range(2):
                came[:, half * TILES : (half + 1) * TILES, :] = mixed_ref[half, :, j].astype(F32)
            tiles = exchange([came[d] for d in range(GROUPS)])
            for t in range(GROUPS):
                gone[pl.ds(t, 8, stride=GROUPS), :] = tiles[t]
            for half in range(2):
                out_ref[:, half_lanes(j, half)] = gone[half * BLOCK : (half + 1) * BLOCK].astype(BF16)
        return carry

    lax.fori_loop(0, CH // 2, columns, 0)


def unpack(mixed):
    return pl.pallas_call(
        unpack_kernel,
        out_shape=jax.ShapeDtypeStruct((BLOCK, WIDTH), BF16),
        in_specs=[VMEM],
        out_specs=VMEM,
        scratch_shapes=[pltpu.VMEM((2, GROUPS, 8, LANES), F32), pltpu.VMEM((2, 2 * BLOCK, LANES), F32)],
        cost_estimate=pl.CostEstimate(flops=4_000_000, bytes_accessed=500_000, transcendentals=0),
        compiler_params=pltpu.CompilerParams(vmem_limit_bytes=8 * 2**20),
        name="unpack",
    )(mixed)


def own_rows(short_weight, skip_gain, row):
    count = STREAMS * SHORT
    taps = lax.dynamic_slice(short_weight, (0, 0, row * OWN), (SHORT, STREAMS, OWN)).reshape(count, OWN)
    skip = lax.dynamic_slice(skip_gain, (row * OWN,), (OWN,)).reshape(1, OWN)
    rows = jnp.concatenate([taps, skip, jnp.zeros((-(count + 1) % 8, OWN), F32)], axis=0)
    return jnp.tile(rows, (1, GROUPS))


def local(inputs, short_weight, long_filter, skip_gain):
    row = lax.axis_index("ctx")
    ahead, back, fine, coarse, turn_rows, forward, inverse = (jnp.asarray(t) for t in tables())
    packed = pack(jnp.transpose(inputs, (1, 0, 2))).reshape(DEVICES, STREAMS, TILES, LANES)
    packed = lax.all_to_all(packed, ("ctx", "ch"), 0, 0, tiled=True)
    place = jnp.stack([row // GROUPS, row % GROUPS]).astype(jnp.int32)
    gain = filter_transform(place, long_filter, ahead, fine, coarse, turn_rows, forward)
    taps = own_rows(short_weight, skip_gain, row)
    mixed = convolve(packed, taps, gain, ahead, back, fine, coarse, turn_rows, forward, inverse)
    mixed = lax.all_to_all(mixed, ("ctx", "ch"), 0, 0, tiled=True)
    return unpack(mixed.reshape(2, GROUPS, CH, TILES, LANES))


def solution(mesh):
    in_specs = (P(("ctx", "ch"), None, None), P(None, None, "ch"), P(None, "ch"), P("ch"))
    out_specs = P(("ctx", "ch"), None)
    return jax.shard_map(local, mesh=mesh, in_specs=in_specs, out_specs=out_specs, check_vma=False)
```

```python
import functools
import math

import jax
import jax.numpy as jnp
import ml_dtypes
import numpy as np
from jax import lax
from jax.experimental import pallas as pl
from jax.experimental.pallas import tpu as pltpu
from jax.sharding import PartitionSpec as P

SHORT = 7
CTX = 16
CH = 16
DEVICES = CTX * CH
BLOCK = 32
LANES = 128
OWN = 16
GROUPS = LANES // OWN
TILES = BLOCK // GROUPS
LENGTH = DEVICES * BLOCK
WIDTH = DEVICES * OWN
NEAR = 4
RIM = 8
CHUNK = 16
ROWS = DEVICES
F32 = jnp.float32
VMEM = pl.BlockSpec(memory_space=pltpu.VMEM)
BF16 = jnp.bfloat16


def halves(table):
    upper = table.astype(ml_dtypes.bfloat16)
    lower = (table - upper.astype(np.float64)).astype(ml_dtypes.bfloat16)
    return upper, lower


@functools.lru_cache(maxsize=None)
def tables():
    turn = 2.0 * math.pi
    freq = (np.arange(ROWS) + 0.5) / (2 * ROWS)
    block = np.arange(ROWS)
    angle = turn * freq[:, None] * block[None, :]
    first = np.concatenate([np.cos(angle), -np.sin(angle)], axis=0)
    upper, lower = halves(first)
    ahead = np.concatenate([upper, lower], axis=1)

    last = np.concatenate([np.cos(angle), -np.sin(angle)], axis=0).T * (2.0 / (2 * LENGTH))
    upper, lower = halves(last)
    back = np.concatenate([upper, lower], axis=1)

    lane = np.arange(LANES)
    place = (np.arange(TILES)[:, None] * GROUPS + lane[None, :] // OWN).reshape(-1)
    fine = turn * freq[:CHUNK, None] * place[None, :] / BLOCK
    coarse = turn * (np.arange(ROWS // CHUNK) * CHUNK / (2 * ROWS))[:, None] * place[None, :] / BLOCK
    fine = np.concatenate([np.cos(fine), -np.sin(fine)], axis=1).astype(np.float32)
    coarse = np.concatenate([np.cos(coarse), -np.sin(coarse)], axis=1).astype(np.float32).reshape(-1, 2 * TILES, LANES)

    angle = turn * np.arange(TILES)[:, None] * (lane[None, :] // OWN) / BLOCK
    turn_rows = np.concatenate([np.cos(angle), -np.sin(angle)], axis=0).astype(np.float32)

    same = (lane[:, None] % OWN) == (lane[None, :] % OWN)
    angle = turn * (lane[:, None] // OWN) * (lane[None, :] // OWN) / GROUPS
    cosine = np.where(same, np.cos(angle), 0.0)
    sine = np.where(same, np.sin(angle), 0.0)
    forward = np.block([[cosine, -sine], [sine, cosine]])
    inverse = np.block([[cosine, sine], [-sine, cosine]])
    upper, lower = halves(forward)
    forward = np.concatenate([upper, lower], axis=0)
    upper, lower = halves(inverse)
    inverse = np.concatenate([upper, lower], axis=0)
    return ahead, back, fine, coarse, turn_rows, forward, inverse


def dot(left, right):
    return jnp.dot(left, right, preferred_element_type=F32)


def split(value):
    upper = value.astype(BF16)
    return upper, (value - upper.astype(F32)).astype(BF16)


def exchange(tiles):
    group = lax.broadcasted_iota(jnp.int32, (GROUPS, LANES), 1) // OWN
    for step in (4, 2, 1):
        low = (group // step) % 2 == 0
        shift = step * OWN
        moved = list(tiles)
        for t in range(GROUPS):
            if t & step == 0:
                a, b = tiles[t], tiles[t + step]
                if step == 4:
                    across = pltpu.roll(jnp.where(low, b, a), shift, 1)
                    moved[t], moved[t + step] = jnp.where(low, a, across), jnp.where(low, across, b)
                else:
                    moved[t] = jnp.where(low, a, pltpu.roll(b, shift, 1))
                    moved[t + step] = jnp.where(low, pltpu.roll(a, LANES - shift, 1), b)
        tiles = moved
    return tiles


def half_lanes(j, half):
    return pl.ds(pl.multiple_of(j * 2 * LANES, LANES) + half * LANES, LANES)


def tap_sum(x_ref, rim_ref, taps, b, stream, lanes, half):
    x = jnp.concatenate([rim_ref[stream, :, lanes].astype(F32), x_ref[stream, :, lanes].astype(F32)], axis=0)
    total = jnp.zeros((BLOCK, LANES), F32)
    for r in range(SHORT):
        row = taps[b, stream, r : r + 1, half * LANES : (half + 1) * LANES]
        total = total + row * x[RIM - r : RIM - r + BLOCK]
    return total


def gate_kernel(order, x_ref, rim_ref, taps_0, taps_1, taps_2, taps_3, out_ref, scratch):
    def columns(b, carry):
        for far, taps in enumerate((taps_0, taps_1, taps_2, taps_3)):
            j = order[far * NEAR + b]
            slot = scratch.at[far % 2]
            for half in range(2):
                lanes = half_lanes(j, half)
                gated = tap_sum(x_ref, rim_ref, taps, b, 1, lanes, half) * tap_sum(x_ref, rim_ref, taps, b, 2, lanes, half)
                slot[half * BLOCK : (half + 1) * BLOCK] = gated.astype(BF16).astype(F32)
            tiles = exchange([slot[pl.ds(t, 8, stride=GROUPS), :] for t in range(GROUPS)])
            for d in range(GROUPS):
                out_ref[0, d, j] = tiles[d][0:TILES].astype(BF16)
                out_ref[1, d, j] = tiles[d][TILES:].astype(BF16)
        return carry

    lax.fori_loop(0, NEAR, columns, 0)


def query_kernel(order, x_ref, rim_ref, taps_0, taps_1, taps_2, taps_3, out_ref):
    def columns(b, carry):
        for far, taps in enumerate((taps_0, taps_1, taps_2, taps_3)):
            j = order[far * NEAR + b]
            for half in range(2):
                lanes = half_lanes(j, half)
                out_ref[:, lanes] = tap_sum(x_ref, rim_ref, taps, b, 0, lanes, half)
        return carry

    lax.fori_loop(0, NEAR, columns, 0)


def gate(order, streams, rim, taps):
    return pl.pallas_call(
        gate_kernel,
        out_shape=jax.ShapeDtypeStruct((2, GROUPS, CH, TILES, LANES), BF16),
        in_specs=[pl.BlockSpec(memory_space=pltpu.SMEM)] + [VMEM] * 6,
        out_specs=VMEM,
        scratch_shapes=[pltpu.VMEM((2, 2 * BLOCK, LANES), F32)],
        cost_estimate=pl.CostEstimate(flops=8_000_000, bytes_accessed=1_600_000, transcendentals=0),
        compiler_params=pltpu.CompilerParams(vmem_limit_bytes=8 * 2**20),
        name="gate",
    )(order, streams, rim, *taps)


def query_features(order, streams, rim, taps):
    return pl.pallas_call(
        query_kernel,
        out_shape=jax.ShapeDtypeStruct((BLOCK, WIDTH), F32),
        in_specs=[pl.BlockSpec(memory_space=pltpu.SMEM)] + [VMEM] * 6,
        out_specs=VMEM,
        cost_estimate=pl.CostEstimate(flops=4_000_000, bytes_accessed=1_600_000, transcendentals=0),
        compiler_params=pltpu.CompilerParams(vmem_limit_bytes=8 * 2**20),
        name="query_features",
    )(order, streams, rim, *taps)


def spin_rows(fine, coarse, step):
    rows = coarse[step]
    spins = []
    for q in range(TILES):
        re = slice(q * LANES, (q + 1) * LANES)
        im = slice((TILES + q) * LANES, (TILES + q + 1) * LANES)
        a, b = fine[:, re], fine[:, im]
        c, d = rows[q : q + 1], rows[TILES + q : TILES + q + 1]
        spins.append((a * c - b * d, a * d + b * c))
    return spins


def table_dot(parts, table):
    upper = table[0:256]
    return dot(parts[:, 0:256], upper) + dot(parts[:, 256:512], upper) + dot(parts[:, 0:256], table[256:512])


def forward_transform(signal, ahead, fine, coarse, turn_rows, forward, stage, parts, out_ref):
    stage[...] = dot(ahead[...], signal[...])

    def rows(step, carry):
        at = pl.multiple_of(step * 16, 16)
        here, below = pl.ds(at, 16), pl.ds(at + ROWS, 16)
        spins = spin_rows(fine, coarse, step)
        real, imag = [], []
        for q in range(TILES):
            lanes = slice(q * LANES, (q + 1) * LANES)
            a, b = stage[here, lanes], stage[below, lanes]
            c, d = spins[q]
            real.append(a * c - b * d)
            imag.append(a * d + b * c)
        er, ei = real[0] + real[2], imag[0] + imag[2]
        fr, fi = real[0] - real[2], imag[0] - imag[2]
        gr, gi = real[1] + real[3], imag[1] + imag[3]
        hr, hi = real[1] - real[3], imag[1] - imag[3]
        outs = ((er + gr, ei + gi), (fr + hi, fi - hr), (er - gr, ei - gi), (fr - hi, fi + hr))
        for k, (a, b) in enumerate(outs):
            if k > 0:
                c, d = turn_rows[k : k + 1], turn_rows[TILES + k : TILES + k + 1]
                a, b = a * c - b * d, a * d + b * c
            to = pl.ds(at + k * ROWS, 16)
            parts[to, 0:128], parts[to, 256:384] = split(a)
            parts[to, 128:256], parts[to, 384:512] = split(b)
        return carry

    lax.fori_loop(0, ROWS // 16, rows, 0)
    out_ref[...] = table_dot(parts, forward)


def filter_kernel(place, filter_ref, ahead, fine, coarse, turn_rows, forward, out_ref, wide, signal, stage, parts):
    step = pl.program_id(0)
    shift = place[1]
    wide[...] = filter_ref[:, pl.ds(pl.multiple_of(place[0] * LANES, LANES), LANES)].astype(F32)
    group = lax.broadcasted_iota(jnp.int32, (BLOCK, LANES), 1) // OWN
    at = pl.multiple_of(step * BLOCK, BLOCK)
    for q in range(TILES):
        tile = jnp.zeros((BLOCK, LANES), F32)
        for t in range(GROUPS):
            rows = wide[pl.ds(q * GROUPS + t, BLOCK, stride=BLOCK), :]
            if t > 0:
                rows = pltpu.roll(rows, t * OWN, 1)
            tile = jnp.where(group == (shift + t) % GROUPS, rows, tile)
        tile = pltpu.roll(tile, (GROUPS - shift) % GROUPS * OWN, 1).astype(BF16)
        signal[pl.ds(at, BLOCK), q * LANES : (q + 1) * LANES] = tile
        signal[pl.ds(at + ROWS, BLOCK), q * LANES : (q + 1) * LANES] = tile

    @pl.when(step == pl.num_programs(0) - 1)
    def _():
        forward_transform(signal, ahead, fine, coarse, turn_rows, forward, stage, parts, out_ref)


def whole_spec(shape):
    return pl.BlockSpec(shape, lambda *_: (0,) * len(shape))


def filter_transform(place, long_filter, ahead, fine, coarse, turn_rows, forward):
    chunk = BLOCK * BLOCK
    consts = (ahead, fine, coarse, turn_rows, forward)
    return pl.pallas_call(
        filter_kernel,
        out_shape=jax.ShapeDtypeStruct((TILES * ROWS, 2 * LANES), F32),
        grid_spec=pltpu.PrefetchScalarGridSpec(
            num_scalar_prefetch=1,
            grid=(LENGTH // chunk,),
            in_specs=[pl.BlockSpec((chunk, WIDTH // CH), lambda g, s: (g, 0))] + [whole_spec(c.shape) for c in consts],
            out_specs=whole_spec((TILES * ROWS, 2 * LANES)),
            scratch_shapes=[
                pltpu.VMEM((chunk, LANES), F32),
                pltpu.VMEM((2 * ROWS, TILES * LANES), BF16),
                pltpu.VMEM((2 * ROWS, TILES * LANES), F32),
                pltpu.VMEM((TILES * ROWS, 4 * LANES), BF16),
            ],
        ),
        cost_estimate=pl.CostEstimate(flops=2_000_000_000, bytes_accessed=6_000_000, transcendentals=0),
        compiler_params=pltpu.CompilerParams(vmem_limit_bytes=58 * 2**20),
        name="filter_transform",
    )(place, long_filter, *consts)


def conv_kernel(
    gated, skip, gain, ahead, back, fine, coarse, turn_rows, forward, inverse, out_ref,
    wide, signal, stage, parts, product, result,
):
    wide[...] = gated[...].astype(F32)
    for q in range(TILES):
        tile = wide[:, q, :].astype(BF16)
        signal[0:ROWS, q * LANES : (q + 1) * LANES] = tile
        signal[ROWS:, q * LANES : (q + 1) * LANES] = tile
    forward_transform(signal, ahead, fine, coarse, turn_rows, forward, stage, parts, product)

    def multiply(step, carry):
        here = pl.ds(pl.multiple_of(step * 32, 32), 32)
        a, b = product[here, 0:128], product[here, 128:256]
        c, d = gain[here, 0:128], gain[here, 128:256]
        parts[here, 0:128], parts[here, 256:384] = split(a * c - b * d)
        parts[here, 128:256], parts[here, 384:512] = split(a * d + b * c)
        return carry

    lax.fori_loop(0, TILES * ROWS // 32, multiply, 0)
    product[...] = table_dot(parts, inverse)

    def unspin(step, carry):
        at = pl.multiple_of(step * 16, 16)
        spins = spin_rows(fine, coarse, step)
        real, imag = [], []
        for k in range(TILES):
            rows = pl.ds(at + k * ROWS, 16)
            a, b = product[rows, 0:128], product[rows, 128:256]
            if k > 0:
                c, d = turn_rows[k : k + 1], turn_rows[TILES + k : TILES + k + 1]
                a, b = a * c + b * d, b * c - a * d
            real.append(a)
            imag.append(b)
        er, ei = real[0] + real[2], imag[0] + imag[2]
        fr, fi = real[0] - real[2], imag[0] - imag[2]
        gr, gi = real[1] + real[3], imag[1] + imag[3]
        hr, hi = real[1] - real[3], imag[1] - imag[3]
        outs = ((er + gr, ei + gi), (fr - hi, fi + hr), (er - gr, ei - gi), (fr + hi, fi - hr))
        for q, (a, b) in enumerate(outs):
            lanes = slice(q * LANES, (q + 1) * LANES)
            c, d = spins[q]
            parts[pl.ds(at, 16), lanes], parts[pl.ds(at + 2 * ROWS, 16), lanes] = split(a * c + b * d)
            parts[pl.ds(at + ROWS, 16), lanes], parts[pl.ds(at + 3 * ROWS, 16), lanes] = split(b * c - a * d)
        return carry

    lax.fori_loop(0, ROWS // 16, unspin, 0)
    for q in range(TILES):
        lanes = slice(q * LANES, (q + 1) * LANES)
        upper, lower = parts[0:512, lanes], parts[512:1024, lanes]
        long_part = dot(back[:, 0:512], upper) + dot(back[:, 0:512], lower) + dot(back[:, 512:1024], upper)
        total = long_part + skip[...] * signal[0:ROWS, lanes].astype(F32)
        result[pl.ds(q, ROWS, stride=TILES), :] = total
    out_ref[...] = result[...].reshape(DEVICES, TILES, LANES).astype(BF16)


def convolve(gated, skip, gain, ahead, back, fine, coarse, turn_rows, forward, inverse):
    return pl.pallas_call(
        conv_kernel,
        out_shape=jax.ShapeDtypeStruct((DEVICES, TILES, LANES), BF16),
        in_specs=[VMEM] * 10,
        out_specs=VMEM,
        scratch_shapes=[
            pltpu.VMEM((DEVICES, TILES, LANES), F32),
            pltpu.VMEM((2 * ROWS, TILES * LANES), BF16),
            pltpu.VMEM((2 * ROWS, TILES * LANES), F32),
            pltpu.VMEM((TILES * ROWS, 4 * LANES), BF16),
            pltpu.VMEM((TILES * ROWS, 2 * LANES), F32),
            pltpu.VMEM((DEVICES * TILES, LANES), F32),
        ],
        cost_estimate=pl.CostEstimate(flops=4_000_000_000, bytes_accessed=6_000_000, transcendentals=0),
        compiler_params=pltpu.CompilerParams(vmem_limit_bytes=24 * 2**20),
        name="convolve",
    )(gated, skip, gain, ahead, back, fine, coarse, turn_rows, forward, inverse)


def mix_kernel(long_ref, query_ref, out_ref, before, after):
    def columns(step, carry):
        for at in range(2):
            j = step * 2 + at
            came, gone = before.at[at], after.at[at]
            for half in range(2):
                came[:, half * TILES : (half + 1) * TILES, :] = long_ref[half, :, j].astype(F32)
            tiles = exchange([came[d] for d in range(GROUPS)])
            for t in range(GROUPS):
                gone[pl.ds(t, 8, stride=GROUPS), :] = tiles[t]
            for half in range(2):
                lanes = half_lanes(j, half)
                out_ref[:, lanes] = (gone[half * BLOCK : (half + 1) * BLOCK] * query_ref[:, lanes]).astype(BF16)
        return carry

    lax.fori_loop(0, CH // 2, columns, 0)


def mix(long_part, query):
    return pl.pallas_call(
        mix_kernel,
        out_shape=jax.ShapeDtypeStruct((BLOCK, WIDTH), BF16),
        in_specs=[VMEM] * 2,
        out_specs=VMEM,
        scratch_shapes=[pltpu.VMEM((2, GROUPS, 8, LANES), F32), pltpu.VMEM((2, 2 * BLOCK, LANES), F32)],
        cost_estimate=pl.CostEstimate(flops=4_000_000, bytes_accessed=1_000_000, transcendentals=0),
        compiler_params=pltpu.CompilerParams(vmem_limit_bytes=8 * 2**20),
        name="mix",
    )(long_part, query)


def gather_taps(taps):
    taps = taps[None]
    for bit in (1, 2):
        other = lax.ppermute(taps, "ch", [(d, d ^ bit) for d in range(CH)])
        taps = jnp.concatenate([taps, other], axis=0)
    far = [lax.ppermute(taps, "ch", [(d, (d + NEAR * k) % CH) for d in range(CH)]) for k in range(1, CH // NEAR)]
    return [taps, *far]


def gather_order():
    me = lax.axis_index("ch")
    slot = jnp.arange(CH, dtype=jnp.int32)
    return (me // NEAR - slot // NEAR) % (CH // NEAR) * NEAR + (me % NEAR ^ slot % NEAR)


def local(inputs, short_weight, long_filter, skip_gain):
    row = lax.axis_index("ctx")
    ahead, back, fine, coarse, turn_rows, forward, inverse = (jnp.asarray(t) for t in tables())
    streams = jnp.transpose(inputs, (1, 0, 2))
    order = gather_order()
    rim = lax.ppermute(streams[:, BLOCK - RIM :], ("ctx", "ch"), [(d, d + 1) for d in range(DEVICES - 1)])
    taps = gather_taps(jnp.transpose(short_weight, (1, 0, 2)))
    gated = gate(order, streams, rim, taps).reshape(DEVICES, TILES, LANES)
    place = jnp.stack([row // GROUPS, row % GROUPS]).astype(jnp.int32)
    gated, place, later = lax.optimization_barrier((gated, place, order))
    gated = lax.all_to_all(gated, ("ctx", "ch"), 0, 0, tiled=True)
    gain = filter_transform(place, long_filter, ahead, fine, coarse, turn_rows, forward)
    query = query_features(later, streams, rim, taps)
    skip = jnp.tile(lax.dynamic_slice(skip_gain, (row * OWN,), (OWN,)), GROUPS).reshape(1, LANES)
    gated, query = lax.optimization_barrier((gated, query))
    long_part = convolve(gated, skip, gain, ahead, back, fine, coarse, turn_rows, forward, inverse)
    long_part = lax.all_to_all(long_part, ("ctx", "ch"), 0, 0, tiled=True)
    return mix(long_part.reshape(2, GROUPS, CH, TILES, LANES), query)


def solution(mesh):
    in_specs = (P(("ctx", "ch"), None, None), P(None, None, "ch"), P(None, "ch"), P("ch"))
    out_specs = P(("ctx", "ch"), None)
    return jax.shard_map(local, mesh=mesh, in_specs=in_specs, out_specs=out_specs, check_vma=False)
```

```python
import functools
import math

import jax
import jax.numpy as jnp
import ml_dtypes
import numpy as np
from jax import lax
from jax.experimental import pallas as pl
from jax.experimental.pallas import tpu as pltpu
from jax.sharding import PartitionSpec as P

SHORT = 7
STREAMS = 3
CTX = 16
CH = 16
DEVICES = CTX * CH
BLOCK = 32
LANES = 128
OWN = 16
GROUPS = LANES // OWN
TILES = BLOCK // GROUPS
LENGTH = DEVICES * BLOCK
WIDTH = DEVICES * OWN
PACK = 8
GATE = 32
CHUNK = 16
ROWS = DEVICES
F32 = jnp.float32
VMEM = pl.BlockSpec(memory_space=pltpu.VMEM)
BF16 = jnp.bfloat16


def halves(table):
    upper = table.astype(ml_dtypes.bfloat16)
    lower = (table - upper.astype(np.float64)).astype(ml_dtypes.bfloat16)
    return upper, lower


@functools.lru_cache(maxsize=None)
def tables():
    turn = 2.0 * math.pi
    freq = (np.arange(ROWS) + 0.5) / (2 * ROWS)
    block = np.arange(ROWS)
    angle = turn * freq[:, None] * block[None, :]
    first = np.concatenate([np.cos(angle), -np.sin(angle)], axis=0)
    upper, lower = halves(first)
    ahead = np.concatenate([upper, lower], axis=1)

    last = np.concatenate([np.cos(angle), -np.sin(angle)], axis=0).T * (2.0 / (2 * LENGTH))
    upper, lower = halves(last)
    back = np.concatenate([upper, lower], axis=1)

    lane = np.arange(LANES)
    place = (np.arange(TILES)[:, None] * GROUPS + lane[None, :] // OWN).reshape(-1)
    fine = turn * freq[:CHUNK, None] * place[None, :] / BLOCK
    coarse = turn * (np.arange(ROWS // CHUNK) * CHUNK / (2 * ROWS))[:, None] * place[None, :] / BLOCK
    fine = np.concatenate([np.cos(fine), -np.sin(fine)], axis=1).astype(np.float32)
    coarse = np.concatenate([np.cos(coarse), -np.sin(coarse)], axis=1).astype(np.float32).reshape(-1, 2 * TILES, LANES)

    angle = turn * np.arange(TILES)[:, None] * (lane[None, :] // OWN) / BLOCK
    turn_rows = np.concatenate([np.cos(angle), -np.sin(angle)], axis=0).astype(np.float32)

    same = (lane[:, None] % OWN) == (lane[None, :] % OWN)
    angle = turn * (lane[:, None] // OWN) * (lane[None, :] // OWN) / GROUPS
    cosine = np.where(same, np.cos(angle), 0.0)
    sine = np.where(same, np.sin(angle), 0.0)
    forward = np.block([[cosine, -sine], [sine, cosine]])
    inverse = np.block([[cosine, sine], [-sine, cosine]])
    upper, lower = halves(forward)
    forward = np.concatenate([upper, lower], axis=0)
    upper, lower = halves(inverse)
    inverse = np.concatenate([upper, lower], axis=0)
    return ahead, back, fine, coarse, turn_rows, forward, inverse


def dot(left, right):
    return jnp.dot(left, right, preferred_element_type=F32)


def split(value):
    upper = value.astype(BF16)
    return upper, (value - upper.astype(F32)).astype(BF16)


def exchange(tiles):
    group = lax.broadcasted_iota(jnp.int32, (GROUPS, LANES), 1) // OWN
    for step in (4, 2, 1):
        low = (group // step) % 2 == 0
        shift = step * OWN
        moved = list(tiles)
        for t in range(GROUPS):
            if t & step == 0:
                a, b = tiles[t], tiles[t + step]
                if step == 4:
                    across = pltpu.roll(jnp.where(low, b, a), shift, 1)
                    moved[t], moved[t + step] = jnp.where(low, a, across), jnp.where(low, across, b)
                else:
                    moved[t] = jnp.where(low, a, pltpu.roll(b, shift, 1))
                    moved[t + step] = jnp.where(low, pltpu.roll(a, LANES - shift, 1), b)
        tiles = moved
    return tiles


def half_lanes(j, half):
    return pl.ds(pl.multiple_of(j * 2 * LANES, LANES) + half * LANES, LANES)


def exchange_all(slots):
    before = [[slot[pl.ds(t, 8, stride=GROUPS), :] for t in range(GROUPS)] for slot in slots]
    return [exchange(tiles) for tiles in before]


def pack_kernel(q_ref, k_ref, v_ref, out_ref, scratch):
    slots = [scratch.at[at] for at in range(3 * PACK)]
    for j in range(PACK):
        for half in range(2):
            lanes = slice((2 * j + half) * LANES, (2 * j + half + 1) * LANES)
            slots[3 * j + half][0:BLOCK] = k_ref[0, :, lanes].astype(F32)
            slots[3 * j + half][BLOCK:] = v_ref[0, :, lanes].astype(F32)
            slots[3 * j + 2][half * BLOCK : (half + 1) * BLOCK] = q_ref[0, :, lanes].astype(F32)
    for first in range(0, PACK, 4):
        done = exchange_all(slots[3 * first : 3 * (first + 4)])
        for at in range(4):
            j = first + at
            for half in range(2):
                tiles = done[3 * at + half]
                for d in range(GROUPS):
                    out_ref[half, d, j, 0] = tiles[d][0:TILES].astype(BF16)
                    out_ref[half, d, j, 1] = tiles[d][TILES:].astype(BF16)
            tiles = done[3 * at + 2]
            for d in range(GROUPS):
                out_ref[0, d, j, 2] = tiles[d][0:TILES].astype(BF16)
                out_ref[1, d, j, 2] = tiles[d][TILES:].astype(BF16)


def pack(streams):
    lanes = PACK * 2 * LANES
    part = (1, BLOCK, lanes)
    return pl.pallas_call(
        pack_kernel,
        grid=(CH // PACK,),
        out_shape=jax.ShapeDtypeStruct((2, GROUPS, CH, 3, TILES, LANES), BF16),
        in_specs=[pl.BlockSpec(part, lambda g, s=s: (s, 0, g)) for s in range(3)],
        out_specs=pl.BlockSpec((2, GROUPS, PACK, 3, TILES, LANES), lambda g: (0, 0, g, 0, 0, 0)),
        scratch_shapes=[pltpu.VMEM((3 * PACK, 2 * BLOCK, LANES), F32)],
        cost_estimate=pl.CostEstimate(flops=4_000_000, bytes_accessed=1_600_000, transcendentals=0),
        compiler_params=pltpu.CompilerParams(vmem_limit_bytes=58 * 2**20),
        name="pack",
    )(streams, streams, streams)


def spin_rows(fine, coarse, step):
    rows = coarse[step]
    spins = []
    for q in range(TILES):
        re = slice(q * LANES, (q + 1) * LANES)
        im = slice((TILES + q) * LANES, (TILES + q + 1) * LANES)
        a, b = fine[:, re], fine[:, im]
        c, d = rows[q : q + 1], rows[TILES + q : TILES + q + 1]
        spins.append((a * c - b * d, a * d + b * c))
    return spins


def table_dot(parts, table):
    upper = table[0:256]
    return dot(parts[:, 0:256], upper) + dot(parts[:, 256:512], upper) + dot(parts[:, 0:256], table[256:512])


def forward_transform(signal, ahead, fine, coarse, turn_rows, forward, stage, parts, out_ref):
    stage[...] = dot(ahead[...], signal[...])

    def rows(step, carry):
        at = pl.multiple_of(step * 16, 16)
        here, below = pl.ds(at, 16), pl.ds(at + ROWS, 16)
        spins = spin_rows(fine, coarse, step)
        real, imag = [], []
        for q in range(TILES):
            lanes = slice(q * LANES, (q + 1) * LANES)
            a, b = stage[here, lanes], stage[below, lanes]
            c, d = spins[q]
            real.append(a * c - b * d)
            imag.append(a * d + b * c)
        er, ei = real[0] + real[2], imag[0] + imag[2]
        fr, fi = real[0] - real[2], imag[0] - imag[2]
        gr, gi = real[1] + real[3], imag[1] + imag[3]
        hr, hi = real[1] - real[3], imag[1] - imag[3]
        outs = ((er + gr, ei + gi), (fr + hi, fi - hr), (er - gr, ei - gi), (fr - hi, fi + hr))
        for k, (a, b) in enumerate(outs):
            if k > 0:
                c, d = turn_rows[k : k + 1], turn_rows[TILES + k : TILES + k + 1]
                a, b = a * c - b * d, a * d + b * c
            to = pl.ds(at + k * ROWS, 16)
            parts[to, 0:128], parts[to, 256:384] = split(a)
            parts[to, 128:256], parts[to, 384:512] = split(b)
        return carry

    lax.fori_loop(0, ROWS // 16, rows, 0)
    out_ref[...] = table_dot(parts, forward)


def filter_kernel(place, filter_ref, ahead, fine, coarse, turn_rows, forward, out_ref, wide, signal, stage, parts):
    step = pl.program_id(0)
    shift = place[1]
    wide[...] = filter_ref[...].astype(F32)
    group = lax.broadcasted_iota(jnp.int32, (BLOCK, LANES), 1) // OWN
    at = pl.multiple_of(step * BLOCK, BLOCK)
    for q in range(TILES):
        tile = jnp.zeros((BLOCK, LANES), F32)
        for t in range(GROUPS):
            rows = wide[pl.ds(q * GROUPS + t, BLOCK, stride=BLOCK), :]
            if t > 0:
                rows = pltpu.roll(rows, t * OWN, 1)
            tile = jnp.where(group == (shift + t) % GROUPS, rows, tile)
        tile = pltpu.roll(tile, (GROUPS - shift) % GROUPS * OWN, 1).astype(BF16)
        signal[pl.ds(at, BLOCK), q * LANES : (q + 1) * LANES] = tile
        signal[pl.ds(at + ROWS, BLOCK), q * LANES : (q + 1) * LANES] = tile

    @pl.when(step == pl.num_programs(0) - 1)
    def _():
        forward_transform(signal, ahead, fine, coarse, turn_rows, forward, stage, parts, out_ref)


def whole_spec(shape):
    return pl.BlockSpec(shape, lambda *_: (0,) * len(shape))


def filter_transform(place, long_filter, ahead, fine, coarse, turn_rows, forward):
    chunk = BLOCK * BLOCK
    consts = (ahead, fine, coarse, turn_rows, forward)
    return pl.pallas_call(
        filter_kernel,
        out_shape=jax.ShapeDtypeStruct((TILES * ROWS, 2 * LANES), F32),
        grid_spec=pltpu.PrefetchScalarGridSpec(
            num_scalar_prefetch=1,
            grid=(LENGTH // chunk,),
            in_specs=[pl.BlockSpec((chunk, LANES), lambda g, s: (g, s[0]))] + [whole_spec(c.shape) for c in consts],
            out_specs=whole_spec((TILES * ROWS, 2 * LANES)),
            scratch_shapes=[
                pltpu.VMEM((chunk, LANES), F32),
                pltpu.VMEM((2 * ROWS, TILES * LANES), BF16),
                pltpu.VMEM((2 * ROWS, TILES * LANES), F32),
                pltpu.VMEM((TILES * ROWS, 4 * LANES), BF16),
            ],
        ),
        cost_estimate=pl.CostEstimate(flops=2_000_000_000, bytes_accessed=6_000_000, transcendentals=0),
        compiler_params=pltpu.CompilerParams(vmem_limit_bytes=58 * 2**20),
        name="filter_transform",
    )(place, long_filter, *consts)


def conv_kernel(
    packed, taps, gain_ref, ahead, back, fine, coarse, turn_rows, forward, inverse, out_ref,
    wide, wide_q, signal, query, stage, parts, product, result, gain, arrived,
):
    fetch = pltpu.make_async_copy(gain_ref, gain, arrived)
    fetch.start()
    wide[0] = jnp.zeros((8, LANES), F32)
    wide_q[0] = jnp.zeros((TILES, LANES), F32)
    wide[1:, 0:TILES] = packed[:, 0].astype(F32)
    wide[1:, TILES:] = packed[:, 1].astype(F32)
    wide_q[1:] = packed[:, 2].astype(F32)
    lane = lax.broadcasted_iota(jnp.int32, (GATE, LANES), 1)

    def features(ref, at, base, stream):
        tiles = [ref[pl.ds(at, GATE), base + TILES - 1, :]]
        for q in range(TILES):
            tiles.append(ref[pl.ds(at + 1, GATE), base + q, :])
        sums = []
        for q in range(TILES):
            total = taps[stream : stream + 1] * tiles[q + 1]
            for r in range(1, SHORT):
                row = STREAMS * r + stream
                shifted = jnp.where(lane < LANES - OWN * r, tiles[q + 1], tiles[q])
                total = total + taps[row : row + 1] * pltpu.roll(shifted, OWN * r, 1)
            sums.append(total)
        return sums

    def gate(step, carry):
        at = pl.multiple_of(step * GATE, GATE)
        left = features(wide, at, 0, 1)
        right = features(wide, at, TILES, 2)
        for q in range(TILES):
            gated = (left[q] * right[q]).astype(BF16)
            signal[pl.ds(at, GATE), q * LANES : (q + 1) * LANES] = gated
            signal[pl.ds(at + ROWS, GATE), q * LANES : (q + 1) * LANES] = gated
        outer = features(wide_q, at, 0, 0)
        for q in range(TILES):
            query[pl.ds(at, GATE), q * LANES : (q + 1) * LANES] = outer[q]
        return carry

    lax.fori_loop(0, ROWS // GATE, gate, 0)
    forward_transform(signal, ahead, fine, coarse, turn_rows, forward, stage, parts, product)

    fetch.wait()

    def multiply(step, carry):
        here = pl.ds(pl.multiple_of(step * 32, 32), 32)
        a, b = product[here, 0:128], product[here, 128:256]
        c, d = gain[here, 0:128], gain[here, 128:256]
        parts[here, 0:128], parts[here, 256:384] = split(a * c - b * d)
        parts[here, 128:256], parts[here, 384:512] = split(a * d + b * c)
        return carry

    lax.fori_loop(0, TILES * ROWS // 32, multiply, 0)
    product[...] = table_dot(parts, inverse)

    def unspin(step, carry):
        at = pl.multiple_of(step * 16, 16)
        spins = spin_rows(fine, coarse, step)
        real, imag = [], []
        for k in range(TILES):
            rows = pl.ds(at + k * ROWS, 16)
            a, b = product[rows, 0:128], product[rows, 128:256]
            if k > 0:
                c, d = turn_rows[k : k + 1], turn_rows[TILES + k : TILES + k + 1]
                a, b = a * c + b * d, b * c - a * d
            real.append(a)
            imag.append(b)
        er, ei = real[0] + real[2], imag[0] + imag[2]
        fr, fi = real[0] - real[2], imag[0] - imag[2]
        gr, gi = real[1] + real[3], imag[1] + imag[3]
        hr, hi = real[1] - real[3], imag[1] - imag[3]
        outs = ((er + gr, ei + gi), (fr - hi, fi + hr), (er - gr, ei - gi), (fr + hi, fi - hr))
        for q, (a, b) in enumerate(outs):
            lanes = slice(q * LANES, (q + 1) * LANES)
            c, d = spins[q]
            parts[pl.ds(at, 16), lanes], parts[pl.ds(at + 2 * ROWS, 16), lanes] = split(a * c + b * d)
            parts[pl.ds(at + ROWS, 16), lanes], parts[pl.ds(at + 3 * ROWS, 16), lanes] = split(b * c - a * d)
        return carry

    lax.fori_loop(0, ROWS // 16, unspin, 0)
    skip = taps[STREAMS * SHORT : STREAMS * SHORT + 1]
    for q in range(TILES):
        lanes = slice(q * LANES, (q + 1) * LANES)
        upper, lower = parts[0:512, lanes], parts[512:1024, lanes]
        long_part = dot(back[:, 0:512], upper) + dot(back[:, 0:512], lower) + dot(back[:, 512:1024], upper)
        total = query[:, lanes] * (long_part + skip * signal[0:ROWS, lanes].astype(F32))
        result[pl.ds(q, ROWS, stride=TILES), :] = total
    out_ref[...] = result[...].reshape(DEVICES, TILES, LANES).astype(BF16)


def convolve(packed, taps, gain, ahead, back, fine, coarse, turn_rows, forward, inverse):
    return pl.pallas_call(
        conv_kernel,
        out_shape=jax.ShapeDtypeStruct((DEVICES, TILES, LANES), BF16),
        in_specs=[VMEM] * 2 + [pl.BlockSpec(memory_space=pltpu.HBM)] + [VMEM] * 7,
        out_specs=VMEM,
        scratch_shapes=[
            pltpu.VMEM((1 + DEVICES, 8, LANES), F32),
            pltpu.VMEM((1 + DEVICES, TILES, LANES), F32),
            pltpu.VMEM((2 * ROWS, TILES * LANES), BF16),
            pltpu.VMEM((ROWS, TILES * LANES), F32),
            pltpu.VMEM((2 * ROWS, TILES * LANES), F32),
            pltpu.VMEM((TILES * ROWS, 4 * LANES), BF16),
            pltpu.VMEM((TILES * ROWS, 2 * LANES), F32),
            pltpu.VMEM((DEVICES * TILES, LANES), F32),
            pltpu.VMEM((TILES * ROWS, 2 * LANES), F32),
            pltpu.SemaphoreType.DMA,
        ],
        cost_estimate=pl.CostEstimate(flops=4_000_000_000, bytes_accessed=6_000_000, transcendentals=0),
        compiler_params=pltpu.CompilerParams(vmem_limit_bytes=24 * 2**20),
        name="convolve",
    )(packed, taps, gain, ahead, back, fine, coarse, turn_rows, forward, inverse)


def unpack_kernel(mixed_ref, out_ref, before, after):
    for first in range(0, CH, 8):
        for at in range(8):
            for half in range(2):
                before[first + at, :, half * TILES : (half + 1) * TILES, :] = mixed_ref[half, :, first + at].astype(F32)
        done = [[before[first + at, d] for d in range(GROUPS)] for at in range(8)]
        done = [exchange(tiles) for tiles in done]
        for at in range(8):
            for t in range(GROUPS):
                after[first + at, pl.ds(t, 8, stride=GROUPS), :] = done[at][t]
    for j in range(CH):
        for half in range(2):
            lanes = slice((2 * j + half) * LANES, (2 * j + half + 1) * LANES)
            out_ref[:, lanes] = after[j, half * BLOCK : (half + 1) * BLOCK].astype(BF16)


def unpack(mixed):
    return pl.pallas_call(
        unpack_kernel,
        out_shape=jax.ShapeDtypeStruct((BLOCK, WIDTH), BF16),
        in_specs=[VMEM],
        out_specs=VMEM,
        scratch_shapes=[pltpu.VMEM((CH, GROUPS, 8, LANES), F32), pltpu.VMEM((CH, 2 * BLOCK, LANES), F32)],
        cost_estimate=pl.CostEstimate(flops=4_000_000, bytes_accessed=500_000, transcendentals=0),
        compiler_params=pltpu.CompilerParams(vmem_limit_bytes=8 * 2**20),
        name="unpack",
    )(mixed)


def own_rows(short_weight, skip_gain, row):
    count = STREAMS * SHORT
    taps = lax.dynamic_slice(short_weight, (0, 0, row * OWN), (SHORT, STREAMS, OWN)).reshape(count, OWN)
    skip = lax.dynamic_slice(skip_gain, (row * OWN,), (OWN,)).reshape(1, OWN)
    rows = jnp.concatenate([taps, skip, jnp.zeros((-(count + 1) % 8, OWN), F32)], axis=0)
    return jnp.tile(rows, (1, GROUPS))


def local(inputs, short_weight, long_filter, skip_gain):
    row = lax.axis_index("ctx")
    ahead, back, fine, coarse, turn_rows, forward, inverse = (jnp.asarray(t) for t in tables())
    packed = pack(jnp.transpose(inputs, (1, 0, 2))).reshape(DEVICES, STREAMS, TILES, LANES)
    packed = lax.all_to_all(packed, ("ctx", "ch"), 0, 0, tiled=True)
    place = jnp.stack([row // GROUPS, row % GROUPS]).astype(jnp.int32)
    gain = filter_transform(place, long_filter, ahead, fine, coarse, turn_rows, forward)
    taps = own_rows(short_weight, skip_gain, row)
    mixed = convolve(packed, taps, gain, ahead, back, fine, coarse, turn_rows, forward, inverse)
    mixed = lax.all_to_all(mixed, ("ctx", "ch"), 0, 0, tiled=True)
    return unpack(mixed.reshape(2, GROUPS, CH, TILES, LANES))


def solution(mesh):
    in_specs = (P(("ctx", "ch"), None, None), P(None, None, "ch"), P(None, "ch"), P("ch"))
    out_specs = P(("ctx", "ch"), None)
    return jax.shard_map(local, mesh=mesh, in_specs=in_specs, out_specs=out_specs, check_vma=False)
```

```python
import functools
import math

import jax
import jax.numpy as jnp
import ml_dtypes
import numpy as np
from jax import lax
from jax.experimental import pallas as pl
from jax.experimental.pallas import tpu as pltpu
from jax.sharding import PartitionSpec as P

SHORT = 7
STREAMS = 2
CTX = 16
CH = 16
DEVICES = CTX * CH
BLOCK = 32
LANES = 128
OWN = 16
GROUPS = LANES // OWN
TILES = BLOCK // GROUPS
LENGTH = DEVICES * BLOCK
WIDTH = DEVICES * OWN
PACK = 8
NEAR = 4
RIM = 8
GATE = 32
CHUNK = 16
ROWS = DEVICES
F32 = jnp.float32
VMEM = pl.BlockSpec(memory_space=pltpu.VMEM)
BF16 = jnp.bfloat16


def halves(table):
    upper = table.astype(ml_dtypes.bfloat16)
    lower = (table - upper.astype(np.float64)).astype(ml_dtypes.bfloat16)
    return upper, lower


@functools.lru_cache(maxsize=None)
def tables():
    turn = 2.0 * math.pi
    freq = (np.arange(ROWS) + 0.5) / (2 * ROWS)
    block = np.arange(ROWS)
    angle = turn * freq[:, None] * block[None, :]
    first = np.concatenate([np.cos(angle), -np.sin(angle)], axis=0)
    upper, lower = halves(first)
    ahead = np.concatenate([upper, lower], axis=1)

    last = np.concatenate([np.cos(angle), -np.sin(angle)], axis=0).T * (2.0 / (2 * LENGTH))
    upper, lower = halves(last)
    back = np.concatenate([upper, lower], axis=1)

    lane = np.arange(LANES)
    place = (np.arange(TILES)[:, None] * GROUPS + lane[None, :] // OWN).reshape(-1)
    fine = turn * freq[:CHUNK, None] * place[None, :] / BLOCK
    coarse = turn * (np.arange(ROWS // CHUNK) * CHUNK / (2 * ROWS))[:, None] * place[None, :] / BLOCK
    fine = np.concatenate([np.cos(fine), -np.sin(fine)], axis=1).astype(np.float32)
    coarse = np.concatenate([np.cos(coarse), -np.sin(coarse)], axis=1).astype(np.float32).reshape(-1, 2 * TILES, LANES)

    angle = turn * np.arange(TILES)[:, None] * (lane[None, :] // OWN) / BLOCK
    turn_rows = np.concatenate([np.cos(angle), -np.sin(angle)], axis=0).astype(np.float32)

    same = (lane[:, None] % OWN) == (lane[None, :] % OWN)
    angle = turn * (lane[:, None] // OWN) * (lane[None, :] // OWN) / GROUPS
    cosine = np.where(same, np.cos(angle), 0.0)
    sine = np.where(same, np.sin(angle), 0.0)
    forward = np.block([[cosine, -sine], [sine, cosine]])
    inverse = np.block([[cosine, sine], [-sine, cosine]])
    upper, lower = halves(forward)
    forward = np.concatenate([upper, lower], axis=0)
    upper, lower = halves(inverse)
    inverse = np.concatenate([upper, lower], axis=0)
    return ahead, back, fine, coarse, turn_rows, forward, inverse


def dot(left, right):
    return jnp.dot(left, right, preferred_element_type=F32)


def split(value):
    upper = value.astype(BF16)
    return upper, (value - upper.astype(F32)).astype(BF16)


def exchange(tiles):
    group = lax.broadcasted_iota(jnp.int32, (GROUPS, LANES), 1) // OWN
    for step in (4, 2, 1):
        low = (group // step) % 2 == 0
        shift = step * OWN
        moved = list(tiles)
        for t in range(GROUPS):
            if t & step == 0:
                a, b = tiles[t], tiles[t + step]
                if step == 4:
                    across = pltpu.roll(jnp.where(low, b, a), shift, 1)
                    moved[t], moved[t + step] = jnp.where(low, a, across), jnp.where(low, across, b)
                else:
                    moved[t] = jnp.where(low, a, pltpu.roll(b, shift, 1))
                    moved[t + step] = jnp.where(low, pltpu.roll(a, LANES - shift, 1), b)
        tiles = moved
    return tiles


def half_lanes(j, half):
    return pl.ds(pl.multiple_of(j * 2 * LANES, LANES) + half * LANES, LANES)


def exchange_all(slots):
    before = [[slot[pl.ds(t, 8, stride=GROUPS), :] for t in range(GROUPS)] for slot in slots]
    return [exchange(tiles) for tiles in before]


def pack_kernel(k_ref, v_ref, out_ref, scratch):
    slots = [scratch.at[at] for at in range(2 * PACK)]
    for at, slot in enumerate(slots):
        lanes = slice(at * LANES, (at + 1) * LANES)
        slot[0:BLOCK] = k_ref[0, :, lanes].astype(F32)
        slot[BLOCK:] = v_ref[0, :, lanes].astype(F32)
    for first in range(0, 2 * PACK, 8):
        for at, tiles in enumerate(exchange_all(slots[first : first + 8])):
            j, half = divmod(first + at, 2)
            for d in range(GROUPS):
                out_ref[half, d, j] = tiles[d].astype(BF16)


def pack(streams):
    lanes = PACK * 2 * LANES
    part = (1, BLOCK, lanes)
    return pl.pallas_call(
        pack_kernel,
        grid=(CH // PACK,),
        out_shape=jax.ShapeDtypeStruct((2, GROUPS, CH, 8, LANES), BF16),
        in_specs=[pl.BlockSpec(part, lambda g: (1, 0, g)), pl.BlockSpec(part, lambda g: (2, 0, g))],
        out_specs=pl.BlockSpec((2, GROUPS, PACK, 8, LANES), lambda g: (0, 0, g, 0, 0)),
        scratch_shapes=[pltpu.VMEM((2 * PACK, 2 * BLOCK, LANES), F32)],
        cost_estimate=pl.CostEstimate(flops=4_000_000, bytes_accessed=1_100_000, transcendentals=0),
        compiler_params=pltpu.CompilerParams(vmem_limit_bytes=58 * 2**20),
        name="pack",
    )(streams, streams)


def query_kernel(order, x_ref, rim_ref, taps_0, taps_1, taps_2, taps_3, out_ref):
    def columns(b, carry):
        for far, taps in enumerate((taps_0, taps_1, taps_2, taps_3)):
            j = order[far * NEAR + b]
            for half in range(2):
                lanes = pl.ds(pl.multiple_of(j * 2 * LANES, LANES) + half * LANES, LANES)
                x = jnp.concatenate([rim_ref[:, lanes].astype(F32), x_ref[0, :, lanes].astype(F32)], axis=0)
                total = jnp.zeros((BLOCK, LANES), F32)
                for r in range(SHORT):
                    row = taps[b, r : r + 1, half * LANES : (half + 1) * LANES]
                    total = total + row * x[RIM - r : RIM - r + BLOCK]
                out_ref[:, lanes] = total
        return carry

    lax.fori_loop(0, NEAR, columns, 0)


def query_features(order, streams, rim, taps):
    return pl.pallas_call(
        query_kernel,
        out_shape=jax.ShapeDtypeStruct((BLOCK, WIDTH), F32),
        in_specs=[pl.BlockSpec(memory_space=pltpu.SMEM)] + [VMEM] * (2 + CH // NEAR),
        out_specs=VMEM,
        cost_estimate=pl.CostEstimate(flops=4_000_000, bytes_accessed=1_000_000, transcendentals=0),
        compiler_params=pltpu.CompilerParams(vmem_limit_bytes=8 * 2**20),
        name="query_features",
    )(order, streams, rim, *taps)


def spin_rows(fine, coarse, step):
    rows = coarse[step]
    spins = []
    for q in range(TILES):
        re = slice(q * LANES, (q + 1) * LANES)
        im = slice((TILES + q) * LANES, (TILES + q + 1) * LANES)
        a, b = fine[:, re], fine[:, im]
        c, d = rows[q : q + 1], rows[TILES + q : TILES + q + 1]
        spins.append((a * c - b * d, a * d + b * c))
    return spins


def table_dot(parts, table):
    upper = table[0:256]
    return dot(parts[:, 0:256], upper) + dot(parts[:, 256:512], upper) + dot(parts[:, 0:256], table[256:512])


def forward_transform(signal, ahead, fine, coarse, turn_rows, forward, stage, parts, out_ref):
    stage[...] = dot(ahead[...], signal[...])

    def rows(step, carry):
        at = pl.multiple_of(step * 16, 16)
        here, below = pl.ds(at, 16), pl.ds(at + ROWS, 16)
        spins = spin_rows(fine, coarse, step)
        real, imag = [], []
        for q in range(TILES):
            lanes = slice(q * LANES, (q + 1) * LANES)
            a, b = stage[here, lanes], stage[below, lanes]
            c, d = spins[q]
            real.append(a * c - b * d)
            imag.append(a * d + b * c)
        er, ei = real[0] + real[2], imag[0] + imag[2]
        fr, fi = real[0] - real[2], imag[0] - imag[2]
        gr, gi = real[1] + real[3], imag[1] + imag[3]
        hr, hi = real[1] - real[3], imag[1] - imag[3]
        outs = ((er + gr, ei + gi), (fr + hi, fi - hr), (er - gr, ei - gi), (fr - hi, fi + hr))
        for k, (a, b) in enumerate(outs):
            if k > 0:
                c, d = turn_rows[k : k + 1], turn_rows[TILES + k : TILES + k + 1]
                a, b = a * c - b * d, a * d + b * c
            to = pl.ds(at + k * ROWS, 16)
            parts[to, 0:128], parts[to, 256:384] = split(a)
            parts[to, 128:256], parts[to, 384:512] = split(b)
        return carry

    lax.fori_loop(0, ROWS // 16, rows, 0)
    out_ref[...] = table_dot(parts, forward)


def filter_kernel(place, filter_ref, ahead, fine, coarse, turn_rows, forward, out_ref, wide, signal, stage, parts):
    step = pl.program_id(0)
    shift = place[1]
    wide[...] = filter_ref[...].astype(F32)
    group = lax.broadcasted_iota(jnp.int32, (BLOCK, LANES), 1) // OWN
    at = pl.multiple_of(step * BLOCK, BLOCK)
    for q in range(TILES):
        tile = jnp.zeros((BLOCK, LANES), F32)
        for t in range(GROUPS):
            rows = wide[pl.ds(q * GROUPS + t, BLOCK, stride=BLOCK), :]
            if t > 0:
                rows = pltpu.roll(rows, t * OWN, 1)
            tile = jnp.where(group == (shift + t) % GROUPS, rows, tile)
        signal[pl.ds(at, BLOCK), q * LANES : (q + 1) * LANES] = tile.astype(BF16)

    @pl.when(step == pl.num_programs(0) - 1)
    def _():
        source = lax.broadcasted_iota(jnp.int32, (LANES, LANES), 0)
        target = lax.broadcasted_iota(jnp.int32, (LANES, LANES), 1)
        move = jnp.where(source == (target + shift * OWN) % LANES, 1.0, 0.0).astype(BF16)
        for q in range(TILES):
            lanes = slice(q * LANES, (q + 1) * LANES)
            tile = dot(signal[0:ROWS, lanes], move).astype(BF16)
            signal[0:ROWS, lanes] = tile
            signal[ROWS:, lanes] = tile
        forward_transform(signal, ahead, fine, coarse, turn_rows, forward, stage, parts, out_ref)


def whole_spec(shape):
    return pl.BlockSpec(shape, lambda *_: (0,) * len(shape))


def filter_transform(place, long_filter, ahead, fine, coarse, turn_rows, forward):
    chunk = BLOCK * BLOCK
    consts = (ahead, fine, coarse, turn_rows, forward)
    return pl.pallas_call(
        filter_kernel,
        out_shape=jax.ShapeDtypeStruct((TILES * ROWS, 2 * LANES), F32),
        grid_spec=pltpu.PrefetchScalarGridSpec(
            num_scalar_prefetch=1,
            grid=(LENGTH // chunk,),
            in_specs=[pl.BlockSpec((chunk, LANES), lambda g, s: (g, s[0]))] + [whole_spec(c.shape) for c in consts],
            out_specs=whole_spec((TILES * ROWS, 2 * LANES)),
            scratch_shapes=[
                pltpu.VMEM((chunk, LANES), F32),
                pltpu.VMEM((2 * ROWS, TILES * LANES), BF16),
                pltpu.VMEM((2 * ROWS, TILES * LANES), F32),
                pltpu.VMEM((TILES * ROWS, 4 * LANES), BF16),
            ],
        ),
        cost_estimate=pl.CostEstimate(flops=2_000_000_000, bytes_accessed=6_000_000, transcendentals=0),
        compiler_params=pltpu.CompilerParams(vmem_limit_bytes=58 * 2**20),
        name="filter_transform",
    )(place, long_filter, *consts)


def conv_kernel(
    packed, taps, gain_ref, ahead, back, fine, coarse, turn_rows, forward, inverse, out_ref,
    wide, signal, stage, parts, product, result, gain, arrived,
):
    fetch = pltpu.make_async_copy(gain_ref, gain, arrived)
    fetch.start()
    wide[0] = jnp.zeros((8, LANES), F32)
    wide[1:] = packed[...].astype(F32)
    lane = lax.broadcasted_iota(jnp.int32, (GATE, LANES), 1)

    def features(ref, at, base, stream):
        tiles = [ref[pl.ds(at, GATE), base + TILES - 1, :]]
        for q in range(TILES):
            tiles.append(ref[pl.ds(at + 1, GATE), base + q, :])
        sums = []
        for q in range(TILES):
            total = taps[stream : stream + 1] * tiles[q + 1]
            for r in range(1, SHORT):
                row = STREAMS * r + stream
                shifted = jnp.where(lane < LANES - OWN * r, tiles[q + 1], tiles[q])
                total = total + taps[row : row + 1] * pltpu.roll(shifted, OWN * r, 1)
            sums.append(total)
        return sums

    def gate(step, carry):
        at = pl.multiple_of(step * GATE, GATE)
        left = features(wide, at, 0, 0)
        right = features(wide, at, TILES, 1)
        for q in range(TILES):
            gated = (left[q] * right[q]).astype(BF16)
            signal[pl.ds(at, GATE), q * LANES : (q + 1) * LANES] = gated
            signal[pl.ds(at + ROWS, GATE), q * LANES : (q + 1) * LANES] = gated
        return carry

    lax.fori_loop(0, ROWS // GATE, gate, 0)
    forward_transform(signal, ahead, fine, coarse, turn_rows, forward, stage, parts, product)

    fetch.wait()

    def multiply(step, carry):
        here = pl.ds(pl.multiple_of(step * 32, 32), 32)
        a, b = product[here, 0:128], product[here, 128:256]
        c, d = gain[here, 0:128], gain[here, 128:256]
        parts[here, 0:128], parts[here, 256:384] = split(a * c - b * d)
        parts[here, 128:256], parts[here, 384:512] = split(a * d + b * c)
        return carry

    lax.fori_loop(0, TILES * ROWS // 32, multiply, 0)
    product[...] = table_dot(parts, inverse)

    def unspin(step, carry):
        at = pl.multiple_of(step * 16, 16)
        spins = spin_rows(fine, coarse, step)
        real, imag = [], []
        for k in range(TILES):
            rows = pl.ds(at + k * ROWS, 16)
            a, b = product[rows, 0:128], product[rows, 128:256]
            if k > 0:
                c, d = turn_rows[k : k + 1], turn_rows[TILES + k : TILES + k + 1]
                a, b = a * c + b * d, b * c - a * d
            real.append(a)
            imag.append(b)
        er, ei = real[0] + real[2], imag[0] + imag[2]
        fr, fi = real[0] - real[2], imag[0] - imag[2]
        gr, gi = real[1] + real[3], imag[1] + imag[3]
        hr, hi = real[1] - real[3], imag[1] - imag[3]
        outs = ((er + gr, ei + gi), (fr - hi, fi + hr), (er - gr, ei - gi), (fr + hi, fi - hr))
        for q, (a, b) in enumerate(outs):
            lanes = slice(q * LANES, (q + 1) * LANES)
            c, d = spins[q]
            parts[pl.ds(at, 16), lanes], parts[pl.ds(at + 2 * ROWS, 16), lanes] = split(a * c + b * d)
            parts[pl.ds(at + ROWS, 16), lanes], parts[pl.ds(at + 3 * ROWS, 16), lanes] = split(b * c - a * d)
        return carry

    lax.fori_loop(0, ROWS // 16, unspin, 0)
    skip = taps[STREAMS * SHORT : STREAMS * SHORT + 1]
    for q in range(TILES):
        lanes = slice(q * LANES, (q + 1) * LANES)
        upper, lower = parts[0:512, lanes], parts[512:1024, lanes]
        long_part = dot(back[:, 0:512], upper) + dot(back[:, 0:512], lower) + dot(back[:, 512:1024], upper)
        total = long_part + skip * signal[0:ROWS, lanes].astype(F32)
        result[pl.ds(q, ROWS, stride=TILES), :] = total
    out_ref[...] = result[...].reshape(DEVICES, TILES, LANES).astype(BF16)


def convolve(packed, taps, gain, ahead, back, fine, coarse, turn_rows, forward, inverse):
    return pl.pallas_call(
        conv_kernel,
        out_shape=jax.ShapeDtypeStruct((DEVICES, TILES, LANES), BF16),
        in_specs=[VMEM] * 2 + [pl.BlockSpec(memory_space=pltpu.HBM)] + [VMEM] * 7,
        out_specs=VMEM,
        scratch_shapes=[
            pltpu.VMEM((1 + DEVICES, 8, LANES), F32),
            pltpu.VMEM((2 * ROWS, TILES * LANES), BF16),
            pltpu.VMEM((2 * ROWS, TILES * LANES), F32),
            pltpu.VMEM((TILES * ROWS, 4 * LANES), BF16),
            pltpu.VMEM((TILES * ROWS, 2 * LANES), F32),
            pltpu.VMEM((DEVICES * TILES, LANES), F32),
            pltpu.VMEM((TILES * ROWS, 2 * LANES), F32),
            pltpu.SemaphoreType.DMA,
        ],
        cost_estimate=pl.CostEstimate(flops=4_000_000_000, bytes_accessed=6_000_000, transcendentals=0),
        compiler_params=pltpu.CompilerParams(vmem_limit_bytes=24 * 2**20),
        name="convolve",
    )(packed, taps, gain, ahead, back, fine, coarse, turn_rows, forward, inverse)


def mix_kernel(mixed_ref, query_ref, out_ref, before, after):
    for first in range(0, CH, 8):
        for at in range(8):
            for half in range(2):
                before[first + at, :, half * TILES : (half + 1) * TILES, :] = mixed_ref[half, :, first + at].astype(F32)
        done = [[before[first + at, d] for d in range(GROUPS)] for at in range(8)]
        done = [exchange(tiles) for tiles in done]
        for at in range(8):
            for t in range(GROUPS):
                after[first + at, pl.ds(t, 8, stride=GROUPS), :] = done[at][t]
    for j in range(CH):
        for half in range(2):
            lanes = slice((2 * j + half) * LANES, (2 * j + half + 1) * LANES)
            out_ref[:, lanes] = (after[j, half * BLOCK : (half + 1) * BLOCK] * query_ref[:, lanes]).astype(BF16)


def mix(long_part, query):
    return pl.pallas_call(
        mix_kernel,
        out_shape=jax.ShapeDtypeStruct((BLOCK, WIDTH), BF16),
        in_specs=[VMEM] * 2,
        out_specs=VMEM,
        scratch_shapes=[pltpu.VMEM((CH, GROUPS, 8, LANES), F32), pltpu.VMEM((CH, 2 * BLOCK, LANES), F32)],
        cost_estimate=pl.CostEstimate(flops=4_000_000, bytes_accessed=500_000, transcendentals=0),
        compiler_params=pltpu.CompilerParams(vmem_limit_bytes=8 * 2**20),
        name="mix",
    )(long_part, query)


def own_rows(short_weight, skip_gain, row):
    count = STREAMS * SHORT
    taps = lax.dynamic_slice(short_weight, (0, 1, row * OWN), (SHORT, STREAMS, OWN)).reshape(count, OWN)
    skip = lax.dynamic_slice(skip_gain, (row * OWN,), (OWN,)).reshape(1, OWN)
    rows = jnp.concatenate([taps, skip, jnp.zeros((-(count + 1) % 8, OWN), F32)], axis=0)
    return jnp.tile(rows, (1, GROUPS))


def gather_taps(taps):
    taps = taps[None]
    for bit in (1, 2):
        other = lax.ppermute(taps, "ch", [(d, d ^ bit) for d in range(CH)])
        taps = jnp.concatenate([taps, other], axis=0)
    far = [lax.ppermute(taps, "ch", [(d, (d + NEAR * k) % CH) for d in range(CH)]) for k in range(1, CH // NEAR)]
    return [taps, *far]


def gather_order():
    me = lax.axis_index("ch")
    slot = jnp.arange(CH, dtype=jnp.int32)
    return (me // NEAR - slot // NEAR) % (CH // NEAR) * NEAR + (me % NEAR ^ slot % NEAR)


def local(inputs, short_weight, long_filter, skip_gain):
    row = lax.axis_index("ctx")
    ahead, back, fine, coarse, turn_rows, forward, inverse = (jnp.asarray(t) for t in tables())
    streams = jnp.transpose(inputs, (1, 0, 2))
    packed = pack(streams).reshape(DEVICES, 8, LANES)
    place = jnp.stack([row // GROUPS, row % GROUPS]).astype(jnp.int32)
    packed, later, place = lax.optimization_barrier((packed, streams, place))
    query_taps = gather_taps(short_weight[:, 0])
    packed = lax.all_to_all(packed, ("ctx", "ch"), 0, 0, tiled=True)
    rim = lax.ppermute(later[0, BLOCK - RIM :], ("ctx", "ch"), [(d, d + 1) for d in range(DEVICES - 1)])
    gain = filter_transform(place, long_filter, ahead, fine, coarse, turn_rows, forward)
    query = query_features(gather_order(), streams, rim, query_taps)
    taps = own_rows(short_weight, skip_gain, row)
    packed, query = lax.optimization_barrier((packed, query))
    long_part = convolve(packed, taps, gain, ahead, back, fine, coarse, turn_rows, forward, inverse)
    long_part = lax.all_to_all(long_part, ("ctx", "ch"), 0, 0, tiled=True)
    return mix(long_part.reshape(2, GROUPS, CH, TILES, LANES), query)


def solution(mesh):
    in_specs = (P(("ctx", "ch"), None, None), P(None, None, "ch"), P(None, "ch"), P("ch"))
    out_specs = P(("ctx", "ch"), None)
    return jax.shard_map(local, mesh=mesh, in_specs=in_specs, out_specs=out_specs, check_vma=False)
```

```python
import functools
import math

import jax
import jax.numpy as jnp
import ml_dtypes
import numpy as np
from jax import lax
from jax.experimental import pallas as pl
from jax.experimental.pallas import tpu as pltpu
from jax.sharding import PartitionSpec as P

SHORT = 7
STREAMS = 3
CTX = 16
CH = 16
DEVICES = CTX * CH
BLOCK = 32
LANES = 128
OWN = 16
GROUPS = LANES // OWN
TILES = BLOCK // GROUPS
LENGTH = DEVICES * BLOCK
WIDTH = DEVICES * OWN
PACK = 4
CHUNK = 16
ROWS = DEVICES
F32 = jnp.float32
VMEM = pl.BlockSpec(memory_space=pltpu.VMEM)
BF16 = jnp.bfloat16


def halves(table):
    upper = table.astype(ml_dtypes.bfloat16)
    lower = (table - upper.astype(np.float64)).astype(ml_dtypes.bfloat16)
    return upper, lower


@functools.lru_cache(maxsize=None)
def tables():
    turn = 2.0 * math.pi
    freq = (np.arange(ROWS) + 0.5) / (2 * ROWS)
    block = np.arange(ROWS)
    angle = turn * freq[:, None] * block[None, :]
    first = np.concatenate([np.cos(angle), -np.sin(angle)], axis=0)
    upper, lower = halves(first)
    ahead = np.concatenate([upper, lower], axis=1)

    last = np.concatenate([np.cos(angle), -np.sin(angle)], axis=0).T * (2.0 / (2 * LENGTH))
    upper, lower = halves(last)
    back = np.concatenate([upper, lower], axis=1)

    lane = np.arange(LANES)
    place = (np.arange(TILES)[:, None] * GROUPS + lane[None, :] // OWN).reshape(-1)
    fine = turn * freq[:CHUNK, None] * place[None, :] / BLOCK
    coarse = turn * (np.arange(ROWS // CHUNK) * CHUNK / (2 * ROWS))[:, None] * place[None, :] / BLOCK
    fine = np.concatenate([np.cos(fine), -np.sin(fine)], axis=1).astype(np.float32)
    coarse = np.concatenate([np.cos(coarse), -np.sin(coarse)], axis=1).astype(np.float32).reshape(-1, 2 * TILES, LANES)

    angle = turn * np.arange(TILES)[:, None] * (lane[None, :] // OWN) / BLOCK
    turn_rows = np.concatenate([np.cos(angle), -np.sin(angle)], axis=0).astype(np.float32)

    same = (lane[:, None] % OWN) == (lane[None, :] % OWN)
    angle = turn * (lane[:, None] // OWN) * (lane[None, :] // OWN) / GROUPS
    cosine = np.where(same, np.cos(angle), 0.0)
    sine = np.where(same, np.sin(angle), 0.0)
    forward = np.block([[cosine, -sine], [sine, cosine]])
    inverse = np.block([[cosine, sine], [-sine, cosine]])
    upper, lower = halves(forward)
    forward = np.concatenate([upper, lower], axis=0)
    upper, lower = halves(inverse)
    inverse = np.concatenate([upper, lower], axis=0)
    return ahead, back, fine, coarse, turn_rows, forward, inverse


def dot(left, right):
    return jnp.dot(left, right, preferred_element_type=F32)


def split(value):
    upper = value.astype(BF16)
    return upper, (value - upper.astype(F32)).astype(BF16)


def exchange(tiles):
    lane = lax.broadcasted_iota(jnp.int32, (GROUPS, LANES), 1)
    for step in (4, 2, 1):
        shift = step * OWN
        low = (lane & shift) == 0
        moved = list(tiles)
        for t in range(GROUPS):
            if t & step == 0:
                a, b = tiles[t], tiles[t + step]
                if step == 4:
                    across = pltpu.roll(jnp.where(low, b, a), shift, 1)
                    moved[t], moved[t + step] = jnp.where(low, a, across), jnp.where(low, across, b)
                else:
                    moved[t] = jnp.where(low, a, pltpu.roll(b, shift, 1))
                    moved[t + step] = jnp.where(low, pltpu.roll(a, LANES - shift, 1), b)
        tiles = moved
    return tiles


def half_lanes(j, half):
    return pl.ds(pl.multiple_of(j * 2 * LANES, LANES) + half * LANES, LANES)


def exchange_all(slots):
    before = [[slot[pl.ds(t, 8, stride=GROUPS), :] for t in range(GROUPS)] for slot in slots]
    return [exchange(tiles) for tiles in before]


def pack_kernel(q_ref, k_ref, v_ref, out_ref, scratch):
    slots = [scratch.at[at] for at in range(3 * PACK)]
    for j in range(PACK):
        for half in range(2):
            lanes = slice((2 * j + half) * LANES, (2 * j + half + 1) * LANES)
            slots[3 * j + half][0:BLOCK] = k_ref[0, :, lanes].astype(F32)
            slots[3 * j + half][BLOCK:] = v_ref[0, :, lanes].astype(F32)
            slots[3 * j + 2][half * BLOCK : (half + 1) * BLOCK] = q_ref[0, :, lanes].astype(F32)
    for first in range(0, PACK, 4):
        done = exchange_all(slots[3 * first : 3 * (first + 4)])
        for at in range(4):
            j = first + at
            for half in range(2):
                tiles = done[3 * at + half]
                for d in range(GROUPS):
                    out_ref[half, d, j, 0] = tiles[d][0:TILES].astype(BF16)
                    out_ref[half, d, j, 1] = tiles[d][TILES:].astype(BF16)
            tiles = done[3 * at + 2]
            for d in range(GROUPS):
                out_ref[0, d, j, 2] = tiles[d][0:TILES].astype(BF16)
                out_ref[1, d, j, 2] = tiles[d][TILES:].astype(BF16)


def pack(streams):
    lanes = PACK * 2 * LANES
    part = (1, BLOCK, lanes)
    return pl.pallas_call(
        pack_kernel,
        grid=(CH // PACK,),
        out_shape=jax.ShapeDtypeStruct((2, GROUPS, CH, 3, TILES, LANES), BF16),
        in_specs=[pl.BlockSpec(part, lambda g, s=s: (s, 0, g)) for s in range(3)],
        out_specs=pl.BlockSpec((2, GROUPS, PACK, 3, TILES, LANES), lambda g: (0, 0, g, 0, 0, 0)),
        scratch_shapes=[pltpu.VMEM((3 * PACK, 2 * BLOCK, LANES), F32)],
        cost_estimate=pl.CostEstimate(flops=4_000_000, bytes_accessed=1_600_000, transcendentals=0),
        compiler_params=pltpu.CompilerParams(vmem_limit_bytes=58 * 2**20),
        name="pack",
    )(streams, streams, streams)


def spin_rows(fine, coarse, step):
    rows = coarse[step]
    spins = []
    for q in range(TILES):
        re = slice(q * LANES, (q + 1) * LANES)
        im = slice((TILES + q) * LANES, (TILES + q + 1) * LANES)
        a, b = fine[:, re], fine[:, im]
        c, d = rows[q : q + 1], rows[TILES + q : TILES + q + 1]
        spins.append((a * c - b * d, a * d + b * c))
    return spins


def table_dot(upper, lower, table):
    return dot(upper, table[0:256]) + dot(lower, table[0:256]) + dot(upper, table[256:512])


def forward_transform(signal, ahead, fine, coarse, turn_rows, stage, parts):
    stage[...] = dot(ahead[...], signal[...])

    def rows(step, carry):
        at = pl.multiple_of(step * 16, 16)
        here, below = pl.ds(at, 16), pl.ds(at + ROWS, 16)
        spins = spin_rows(fine, coarse, step)
        real, imag = [], []
        for q in range(TILES):
            lanes = slice(q * LANES, (q + 1) * LANES)
            a, b = stage[here, lanes], stage[below, lanes]
            c, d = spins[q]
            real.append(a * c - b * d)
            imag.append(a * d + b * c)
        er, ei = real[0] + real[2], imag[0] + imag[2]
        fr, fi = real[0] - real[2], imag[0] - imag[2]
        gr, gi = real[1] + real[3], imag[1] + imag[3]
        hr, hi = real[1] - real[3], imag[1] - imag[3]
        outs = ((er + gr, ei + gi), (fr + hi, fi - hr), (er - gr, ei - gi), (fr - hi, fi + hr))
        for k, (a, b) in enumerate(outs):
            if k > 0:
                c, d = turn_rows[k : k + 1], turn_rows[TILES + k : TILES + k + 1]
                a, b = a * c - b * d, a * d + b * c
            to = pl.ds(at + k * ROWS, 16)
            parts[to, 0:128], parts[to, 256:384] = split(a)
            parts[to, 128:256], parts[to, 384:512] = split(b)
        return carry

    lax.fori_loop(0, ROWS // 16, rows, 0)


def filter_kernel(place, filter_ref, ahead, fine, coarse, turn_rows, forward, out_ref, wide, signal, stage, parts):
    step = pl.program_id(0)
    shift = place[1]
    wide[...] = filter_ref[...].astype(F32)
    group = lax.broadcasted_iota(jnp.int32, (BLOCK, LANES), 1) // OWN
    at = pl.multiple_of(step * BLOCK, BLOCK)
    for q in range(TILES):
        tile = jnp.zeros((BLOCK, LANES), F32)
        for t in range(GROUPS):
            rows = wide[pl.ds(q * GROUPS + t, BLOCK, stride=BLOCK), :]
            if t > 0:
                rows = pltpu.roll(rows, t * OWN, 1)
            tile = jnp.where(group == (shift + t) % GROUPS, rows, tile)
        tile = pltpu.roll(tile, (GROUPS - shift) % GROUPS * OWN, 1).astype(BF16)
        signal[pl.ds(at, BLOCK), q * LANES : (q + 1) * LANES] = tile
        signal[pl.ds(at + ROWS, BLOCK), q * LANES : (q + 1) * LANES] = tile

    @pl.when(step == pl.num_programs(0) - 1)
    def _():
        forward_transform(signal, ahead, fine, coarse, turn_rows, stage, parts)
        out_ref[...] = table_dot(parts[:, 0:256], parts[:, 256:512], forward)


def whole_spec(shape):
    return pl.BlockSpec(shape, lambda *_: (0,) * len(shape))


def filter_transform(place, long_filter, ahead, fine, coarse, turn_rows, forward):
    chunk = BLOCK * BLOCK
    consts = (ahead, fine, coarse, turn_rows, forward)
    return pl.pallas_call(
        filter_kernel,
        out_shape=jax.ShapeDtypeStruct((TILES * ROWS, 2 * LANES), F32),
        grid_spec=pltpu.PrefetchScalarGridSpec(
            num_scalar_prefetch=1,
            grid=(LENGTH // chunk,),
            in_specs=[pl.BlockSpec((chunk, LANES), lambda g, s: (g, s[0]))] + [whole_spec(c.shape) for c in consts],
            out_specs=whole_spec((TILES * ROWS, 2 * LANES)),
            scratch_shapes=[
                pltpu.VMEM((chunk, LANES), F32),
                pltpu.VMEM((2 * ROWS, TILES * LANES), BF16),
                pltpu.VMEM((2 * ROWS, TILES * LANES), F32),
                pltpu.VMEM((TILES * ROWS, 4 * LANES), BF16),
            ],
        ),
        cost_estimate=pl.CostEstimate(flops=2_000_000_000, bytes_accessed=6_000_000, transcendentals=0),
        compiler_params=pltpu.CompilerParams(vmem_limit_bytes=58 * 2**20),
        name="filter_transform",
    )(place, long_filter, *consts)


def conv_kernel(
    packed, bands, skip, gain_ref, ahead, back, fine, coarse, turn_rows, forward, inverse, out_ref,
    wide, wide_q, signal, query, stage, parts, product, result, gain, arrived,
):
    fetch = pltpu.make_async_copy(gain_ref, gain, arrived)
    fetch.start()
    wide[0] = jnp.zeros((8, LANES), F32)
    wide_q[0] = jnp.zeros((TILES, LANES), F32)
    wide[1:, 0:TILES] = packed[:, 0].astype(F32)
    wide[1:, TILES:] = packed[:, 1].astype(F32)
    wide_q[1:] = packed[:, 2].astype(F32)
    for q in range(TILES):
        lanes = slice(q * LANES, (q + 1) * LANES)
        sums = []
        for stream, (ref, base) in enumerate(((wide_q, 0), (wide, 0), (wide, TILES))):
            before = ref[0:DEVICES, base + TILES - 1, :] if q == 0 else ref[1:, base + q - 1, :]
            both = jnp.concatenate([before.astype(BF16), ref[1:, base + q, :].astype(BF16)], axis=1)
            halves_of = dot(both, bands[stream])
            sums.append(halves_of[:, 0:LANES] + halves_of[:, LANES:])
        query[:, lanes] = sums[0]
        gated = (sums[1] * sums[2]).astype(BF16)
        signal[0:ROWS, lanes] = gated
        signal[ROWS:, lanes] = gated
    forward_transform(signal, ahead, fine, coarse, turn_rows, stage, parts)
    fetch.wait()
    for k in range(TILES):
        rows = slice(k * ROWS, (k + 1) * ROWS)
        mid = table_dot(parts[rows, 0:256], parts[rows, 256:512], forward)
        a, b = mid[:, 0:LANES], mid[:, LANES:]
        c, d = gain[rows, 0:LANES], gain[rows, LANES:]
        re_upper, re_lower = split(a * c - b * d)
        im_upper, im_lower = split(a * d + b * c)
        upper = jnp.concatenate([re_upper, im_upper], axis=1)
        lower = jnp.concatenate([re_lower, im_lower], axis=1)
        product[rows] = table_dot(upper, lower, inverse)

    def unspin(step, carry):
        at = pl.multiple_of(step * 16, 16)
        spins = spin_rows(fine, coarse, step)
        real, imag = [], []
        for k in range(TILES):
            rows = pl.ds(at + k * ROWS, 16)
            a, b = product[rows, 0:128], product[rows, 128:256]
            if k > 0:
                c, d = turn_rows[k : k + 1], turn_rows[TILES + k : TILES + k + 1]
                a, b = a * c + b * d, b * c - a * d
            real.append(a)
            imag.append(b)
        er, ei = real[0] + real[2], imag[0] + imag[2]
        fr, fi = real[0] - real[2], imag[0] - imag[2]
        gr, gi = real[1] + real[3], imag[1] + imag[3]
        hr, hi = real[1] - real[3], imag[1] - imag[3]
        outs = ((er + gr, ei + gi), (fr - hi, fi + hr), (er - gr, ei - gi), (fr + hi, fi - hr))
        for q, (a, b) in enumerate(outs):
            lanes = slice(q * LANES, (q + 1) * LANES)
            c, d = spins[q]
            parts[pl.ds(at, 16), lanes], parts[pl.ds(at + 2 * ROWS, 16), lanes] = split(a * c + b * d)
            parts[pl.ds(at + ROWS, 16), lanes], parts[pl.ds(at + 3 * ROWS, 16), lanes] = split(b * c - a * d)
        return carry

    lax.fori_loop(0, ROWS // 16, unspin, 0)
    for q in range(TILES):
        lanes = slice(q * LANES, (q + 1) * LANES)
        upper, lower = parts[0:512, lanes], parts[512:1024, lanes]
        long_part = dot(back[:, 0:512], upper) + dot(back[:, 0:512], lower) + dot(back[:, 512:1024], upper)
        total = query[:, lanes] * (long_part + skip[...] * signal[0:ROWS, lanes].astype(F32))
        result[pl.ds(q, ROWS, stride=TILES), :] = total
    out_ref[...] = result[...].reshape(DEVICES, TILES, LANES).astype(BF16)


def convolve(packed, bands, skip, gain, ahead, back, fine, coarse, turn_rows, forward, inverse):
    return pl.pallas_call(
        conv_kernel,
        out_shape=jax.ShapeDtypeStruct((DEVICES, TILES, LANES), BF16),
        in_specs=[VMEM] * 3 + [pl.BlockSpec(memory_space=pltpu.HBM)] + [VMEM] * 7,
        out_specs=VMEM,
        scratch_shapes=[
            pltpu.VMEM((1 + DEVICES, 8, LANES), F32),
            pltpu.VMEM((1 + DEVICES, TILES, LANES), F32),
            pltpu.VMEM((2 * ROWS, TILES * LANES), BF16),
            pltpu.VMEM((ROWS, TILES * LANES), F32),
            pltpu.VMEM((2 * ROWS, TILES * LANES), F32),
            pltpu.VMEM((TILES * ROWS, 4 * LANES), BF16),
            pltpu.VMEM((TILES * ROWS, 2 * LANES), F32),
            pltpu.VMEM((DEVICES * TILES, LANES), F32),
            pltpu.VMEM((TILES * ROWS, 2 * LANES), F32),
            pltpu.SemaphoreType.DMA,
        ],
        cost_estimate=pl.CostEstimate(flops=4_000_000_000, bytes_accessed=6_000_000, transcendentals=0),
        compiler_params=pltpu.CompilerParams(vmem_limit_bytes=24 * 2**20),
        name="convolve",
    )(packed, bands, skip, gain, ahead, back, fine, coarse, turn_rows, forward, inverse)


def unpack_kernel(mixed_ref, out_ref, before, after):
    for first in range(0, CH, 8):
        for at in range(8):
            for half in range(2):
                before[first + at, :, half * TILES : (half + 1) * TILES, :] = mixed_ref[half, :, first + at].astype(F32)
        done = [[before[first + at, d] for d in range(GROUPS)] for at in range(8)]
        done = [exchange(tiles) for tiles in done]
        for at in range(8):
            for t in range(GROUPS):
                after[first + at, pl.ds(t, 8, stride=GROUPS), :] = done[at][t]
    for j in range(CH):
        for half in range(2):
            lanes = slice((2 * j + half) * LANES, (2 * j + half + 1) * LANES)
            out_ref[:, lanes] = after[j, half * BLOCK : (half + 1) * BLOCK].astype(BF16)


def unpack(mixed):
    return pl.pallas_call(
        unpack_kernel,
        out_shape=jax.ShapeDtypeStruct((BLOCK, WIDTH), BF16),
        in_specs=[VMEM],
        out_specs=VMEM,
        scratch_shapes=[pltpu.VMEM((CH, GROUPS, 8, LANES), F32), pltpu.VMEM((CH, 2 * BLOCK, LANES), F32)],
        cost_estimate=pl.CostEstimate(flops=4_000_000, bytes_accessed=500_000, transcendentals=0),
        compiler_params=pltpu.CompilerParams(vmem_limit_bytes=8 * 2**20),
        name="unpack",
    )(mixed)


def band_kernel(taps, out_ref):
    for at in range(0, 2 * LANES, 64):
        row = lax.broadcasted_iota(jnp.int32, (64, LANES), 0) + at
        lane = lax.broadcasted_iota(jnp.int32, (64, LANES), 1)
        lag = (lane >> 4) - ((row & LANES - 1) >> 4) + jnp.where(row < LANES, GROUPS, 0)
        lag = jnp.where(((row ^ lane) & OWN - 1) == 0, lag, -1)
        for stream in range(STREAMS):
            band = jnp.zeros((64, LANES), F32)
            for r in range(SHORT):
                band = jnp.where(lag == r, taps[STREAMS * r + stream : STREAMS * r + stream + 1], band)
            out_ref[stream, at : at + 64, 0:LANES], out_ref[stream, at : at + 64, LANES:] = split(band)


def short_bands(taps):
    return pl.pallas_call(
        band_kernel,
        out_shape=jax.ShapeDtypeStruct((STREAMS, 2 * LANES, 2 * LANES), BF16),
        in_specs=[VMEM],
        out_specs=VMEM,
        cost_estimate=pl.CostEstimate(flops=2_000_000, bytes_accessed=500_000, transcendentals=0),
        compiler_params=pltpu.CompilerParams(vmem_limit_bytes=8 * 2**20),
        name="short_bands",
    )(taps)


def own_rows(short_weight, row):
    count = STREAMS * SHORT
    taps = lax.dynamic_slice(short_weight, (0, 0, row * OWN), (SHORT, STREAMS, OWN)).reshape(count, OWN)
    return jnp.tile(jnp.pad(taps, ((0, -count % 8), (0, 0))), (1, GROUPS))


def local(inputs, short_weight, long_filter, skip_gain):
    row = lax.axis_index("ctx")
    ahead, back, fine, coarse, turn_rows, forward, inverse = (jnp.asarray(t) for t in tables())
    packed = pack(jnp.transpose(inputs, (1, 0, 2))).reshape(DEVICES, STREAMS, TILES, LANES)
    packed = lax.all_to_all(packed, ("ctx", "ch"), 0, 0, tiled=True)
    place = jnp.stack([row // GROUPS, row % GROUPS]).astype(jnp.int32)
    gain = filter_transform(place, long_filter, ahead, fine, coarse, turn_rows, forward)
    bands = short_bands(own_rows(short_weight, row))
    skip = jnp.tile(lax.dynamic_slice(skip_gain, (row * OWN,), (OWN,)), GROUPS).reshape(1, LANES)
    mixed = convolve(packed, bands, skip, gain, ahead, back, fine, coarse, turn_rows, forward, inverse)
    mixed = lax.all_to_all(mixed, ("ctx", "ch"), 0, 0, tiled=True)
    return unpack(mixed.reshape(2, GROUPS, CH, TILES, LANES))


def solution(mesh):
    in_specs = (P(("ctx", "ch"), None, None), P(None, None, "ch"), P(None, "ch"), P("ch"))
    out_specs = P(("ctx", "ch"), None)
    return jax.shard_map(local, mesh=mesh, in_specs=in_specs, out_specs=out_specs, check_vma=False)
```

```python
import functools
import math

import jax
import jax.numpy as jnp
import ml_dtypes
import numpy as np
from jax import lax
from jax.experimental import pallas as pl
from jax.experimental.pallas import tpu as pltpu
from jax.sharding import PartitionSpec as P

SHORT = 7
STREAMS = 3
CTX = 16
CH = 16
DEVICES = CTX * CH
BLOCK = 32
LANES = 128
OWN = 16
GROUPS = LANES // OWN
TILES = BLOCK // GROUPS
LENGTH = DEVICES * BLOCK
WIDTH = DEVICES * OWN
PACK = 4
HELD = 40
CHUNK = 16
ROWS = DEVICES
F32 = jnp.float32
VMEM = pl.BlockSpec(memory_space=pltpu.VMEM)
BF16 = jnp.bfloat16


def halves(table):
    upper = table.astype(ml_dtypes.bfloat16)
    lower = (table - upper.astype(np.float64)).astype(ml_dtypes.bfloat16)
    return upper, lower


@functools.lru_cache(maxsize=None)
def tables():
    turn = 2.0 * math.pi
    freq = (np.arange(ROWS) + 0.5) / (2 * ROWS)
    block = np.arange(ROWS)
    angle = turn * freq[:, None] * block[None, :]
    first = np.concatenate([np.cos(angle), -np.sin(angle)], axis=0)
    upper, lower = halves(first)
    ahead = np.concatenate([upper, lower], axis=1)

    last = np.concatenate([np.cos(angle), -np.sin(angle)], axis=0).T * (2.0 / (2 * LENGTH))
    upper, lower = halves(last)
    back = np.concatenate([upper, lower], axis=1)

    lane = np.arange(LANES)
    place = (np.arange(TILES)[:, None] * GROUPS + lane[None, :] // OWN).reshape(-1)
    fine = turn * freq[:CHUNK, None] * place[None, :] / BLOCK
    coarse = turn * (np.arange(ROWS // CHUNK) * CHUNK / (2 * ROWS))[:, None] * place[None, :] / BLOCK
    fine = np.concatenate([np.cos(fine), -np.sin(fine)], axis=1).astype(np.float32)
    coarse = np.concatenate([np.cos(coarse), -np.sin(coarse)], axis=1).astype(np.float32).reshape(-1, 2 * TILES, LANES)

    angle = turn * np.arange(TILES)[:, None] * (lane[None, :] // OWN) / BLOCK
    turn_rows = np.concatenate([np.cos(angle), -np.sin(angle)], axis=0).astype(np.float32)

    same = (lane[:, None] % OWN) == (lane[None, :] % OWN)
    angle = turn * (lane[:, None] // OWN) * (lane[None, :] // OWN) / GROUPS
    cosine = np.where(same, np.cos(angle), 0.0)
    sine = np.where(same, np.sin(angle), 0.0)
    forward = np.block([[cosine, -sine], [sine, cosine]])
    inverse = np.block([[cosine, sine], [-sine, cosine]])
    upper, lower = halves(forward)
    forward = np.concatenate([upper, lower], axis=0)
    upper, lower = halves(inverse)
    inverse = np.concatenate([upper, lower], axis=0)
    return ahead, back, fine, coarse, turn_rows, forward, inverse


def dot(left, right):
    return jnp.dot(left, right, preferred_element_type=F32)


def split(value):
    upper = value.astype(BF16)
    return upper, (value - upper.astype(F32)).astype(BF16)


def exchange(tiles):
    lane = lax.broadcasted_iota(jnp.int32, (GROUPS, LANES), 1)
    for step in (4, 2, 1):
        shift = step * OWN
        low = (lane & shift) == 0
        moved = list(tiles)
        for t in range(GROUPS):
            if t & step == 0:
                a, b = tiles[t], tiles[t + step]
                if step == 4:
                    across = pltpu.roll(jnp.where(low, b, a), shift, 1)
                    moved[t], moved[t + step] = jnp.where(low, a, across), jnp.where(low, across, b)
                else:
                    moved[t] = jnp.where(low, a, pltpu.roll(b, shift, 1))
                    moved[t + step] = jnp.where(low, pltpu.roll(a, LANES - shift, 1), b)
        tiles = moved
    return tiles


def half_lanes(j, half):
    return pl.ds(pl.multiple_of(j * 2 * LANES, LANES) + half * LANES, LANES)


def exchange_all(slots):
    before = [[slot[pl.ds(t, 8, stride=GROUPS), :] for t in range(GROUPS)] for slot in slots]
    return [exchange(tiles) for tiles in before]


def pack_kernel(q_ref, k_ref, v_ref, out_ref, scratch):
    slots = [scratch.at[at] for at in range(3 * PACK)]
    for j in range(PACK):
        for half in range(2):
            lanes = slice((2 * j + half) * LANES, (2 * j + half + 1) * LANES)
            slots[3 * j + half][0:BLOCK] = k_ref[0, :, lanes].astype(F32)
            slots[3 * j + half][BLOCK:] = v_ref[0, :, lanes].astype(F32)
            slots[3 * j + 2][half * BLOCK : (half + 1) * BLOCK] = q_ref[0, :, lanes].astype(F32)
    for first in range(0, PACK, 4):
        done = exchange_all(slots[3 * first : 3 * (first + 4)])
        for at in range(4):
            j = first + at
            for half in range(2):
                tiles = done[3 * at + half]
                for d in range(GROUPS):
                    out_ref[half, d, j, 0] = tiles[d][0:TILES].astype(BF16)
                    out_ref[half, d, j, 1] = tiles[d][TILES:].astype(BF16)
            tiles = done[3 * at + 2]
            for d in range(GROUPS):
                out_ref[0, d, j, 2] = tiles[d][0:TILES].astype(BF16)
                out_ref[1, d, j, 2] = tiles[d][TILES:].astype(BF16)


def pack(streams):
    lanes = PACK * 2 * LANES
    part = (1, BLOCK, lanes)
    return pl.pallas_call(
        pack_kernel,
        grid=(CH // PACK,),
        out_shape=jax.ShapeDtypeStruct((2, GROUPS, CH, 3, TILES, LANES), BF16),
        in_specs=[pl.BlockSpec(part, lambda g, s=s: (s, 0, g)) for s in range(3)],
        out_specs=pl.BlockSpec((2, GROUPS, PACK, 3, TILES, LANES), lambda g: (0, 0, g, 0, 0, 0)),
        scratch_shapes=[pltpu.VMEM((3 * PACK, 2 * BLOCK, LANES), F32)],
        cost_estimate=pl.CostEstimate(flops=4_000_000, bytes_accessed=1_600_000, transcendentals=0),
        compiler_params=pltpu.CompilerParams(vmem_limit_bytes=58 * 2**20),
        name="pack",
    )(streams, streams, streams)


def spin_rows(fine, coarse, step):
    rows = coarse[step]
    spins = []
    for q in range(TILES):
        re = slice(q * LANES, (q + 1) * LANES)
        im = slice((TILES + q) * LANES, (TILES + q + 1) * LANES)
        a, b = fine[:, re], fine[:, im]
        c, d = rows[q : q + 1], rows[TILES + q : TILES + q + 1]
        spins.append((a * c - b * d, a * d + b * c))
    return spins


def table_dot(upper, lower, table):
    return dot(upper, table[0:256]) + dot(lower, table[0:256]) + dot(upper, table[256:512])


def forward_transform(signal, ahead, fine, coarse, turn_rows, stage, parts):
    stage[...] = dot(ahead[...], signal[...])

    def rows(step, carry):
        at = pl.multiple_of(step * 16, 16)
        here, below = pl.ds(at, 16), pl.ds(at + ROWS, 16)
        spins = spin_rows(fine, coarse, step)
        real, imag = [], []
        for q in range(TILES):
            lanes = slice(q * LANES, (q + 1) * LANES)
            a, b = stage[here, lanes], stage[below, lanes]
            c, d = spins[q]
            real.append(a * c - b * d)
            imag.append(a * d + b * c)
        er, ei = real[0] + real[2], imag[0] + imag[2]
        fr, fi = real[0] - real[2], imag[0] - imag[2]
        gr, gi = real[1] + real[3], imag[1] + imag[3]
        hr, hi = real[1] - real[3], imag[1] - imag[3]
        outs = ((er + gr, ei + gi), (fr + hi, fi - hr), (er - gr, ei - gi), (fr - hi, fi + hr))
        for k, (a, b) in enumerate(outs):
            if k > 0:
                c, d = turn_rows[k : k + 1], turn_rows[TILES + k : TILES + k + 1]
                a, b = a * c - b * d, a * d + b * c
            to = pl.ds(at + k * ROWS, 16)
            parts[to, 0:128], parts[to, 256:384] = split(a)
            parts[to, 128:256], parts[to, 384:512] = split(b)
        return carry

    lax.fori_loop(0, ROWS // 16, rows, 0, unroll=2)


def filter_kernel(place, filter_ref, ahead, fine, coarse, turn_rows, forward, out_ref, wide, signal, stage, parts, result, sent):
    step = pl.program_id(0)
    shift = place[1]
    wide[...] = filter_ref[...].astype(F32)
    group = lax.broadcasted_iota(jnp.int32, (BLOCK, LANES), 1) // OWN
    at = pl.multiple_of(step * BLOCK, BLOCK)
    for q in range(TILES):
        tile = jnp.zeros((BLOCK, LANES), F32)
        for t in range(GROUPS):
            rows = wide[pl.ds(q * GROUPS + t, BLOCK, stride=BLOCK), :]
            if t > 0:
                rows = pltpu.roll(rows, t * OWN, 1)
            tile = jnp.where(group == (shift + t) % GROUPS, rows, tile)
        tile = pltpu.roll(tile, (GROUPS - shift) % GROUPS * OWN, 1).astype(BF16)
        signal[pl.ds(at, BLOCK), q * LANES : (q + 1) * LANES] = tile
        signal[pl.ds(at + ROWS, BLOCK), q * LANES : (q + 1) * LANES] = tile

    @pl.when(step == pl.num_programs(0) - 1)
    def _():
        forward_transform(signal, ahead, fine, coarse, turn_rows, stage, parts)
        result[...] = table_dot(parts[:, 0:256], parts[:, 256:512], forward)
        send = pltpu.make_async_copy(result, out_ref.at[0 : TILES * ROWS], sent)
        send.start()
        send.wait()


def whole_spec(shape):
    return pl.BlockSpec(shape, lambda *_: (0,) * len(shape))


def filter_transform(place, long_filter, ahead, fine, coarse, turn_rows, forward):
    chunk = BLOCK * BLOCK
    consts = (ahead, fine, coarse, turn_rows, forward)
    return pl.pallas_call(
        filter_kernel,
        out_shape=jax.ShapeDtypeStruct((HELD * TILES * ROWS, 2 * LANES), F32),
        grid_spec=pltpu.PrefetchScalarGridSpec(
            num_scalar_prefetch=1,
            grid=(LENGTH // chunk,),
            in_specs=[pl.BlockSpec((chunk, LANES), lambda g, s: (g, s[0]))] + [whole_spec(c.shape) for c in consts],
            out_specs=pl.BlockSpec(memory_space=pl.ANY),
            scratch_shapes=[
                pltpu.VMEM((chunk, LANES), F32),
                pltpu.VMEM((2 * ROWS, TILES * LANES), BF16),
                pltpu.VMEM((2 * ROWS, TILES * LANES), F32),
                pltpu.VMEM((TILES * ROWS, 4 * LANES), BF16),
                pltpu.VMEM((TILES * ROWS, 2 * LANES), F32),
                pltpu.SemaphoreType.DMA,
            ],
        ),
        cost_estimate=pl.CostEstimate(flops=2_000_000_000, bytes_accessed=6_000_000, transcendentals=0),
        compiler_params=pltpu.CompilerParams(vmem_limit_bytes=58 * 2**20),
        name="filter_transform",
    )(place, long_filter, *consts)


def conv_kernel(
    packed, bands, skip, gain_ref, ahead, back, fine, coarse, turn_rows, forward, inverse, out_ref,
    wide, wide_q, signal, query, stage, parts, product, result, gain, arrived,
):
    fetch = pltpu.make_async_copy(gain_ref.at[0 : TILES * ROWS], gain, arrived)
    fetch.start()
    wide[0] = jnp.zeros((8, LANES), F32)
    wide_q[0] = jnp.zeros((TILES, LANES), F32)
    wide[1:, 0:TILES] = packed[:, 0].astype(F32)
    wide[1:, TILES:] = packed[:, 1].astype(F32)
    wide_q[1:] = packed[:, 2].astype(F32)
    for q in range(TILES):
        lanes = slice(q * LANES, (q + 1) * LANES)
        sums = []
        for stream, (ref, base) in enumerate(((wide_q, 0), (wide, 0), (wide, TILES))):
            before = ref[0:DEVICES, base + TILES - 1, :] if q == 0 else ref[1:, base + q - 1, :]
            both = jnp.concatenate([before.astype(BF16), ref[1:, base + q, :].astype(BF16)], axis=1)
            halves_of = dot(both, bands[stream])
            sums.append(halves_of[:, 0:LANES] + halves_of[:, LANES:])
        query[:, lanes] = sums[0]
        gated = (sums[1] * sums[2]).astype(BF16)
        signal[0:ROWS, lanes] = gated
        signal[ROWS:, lanes] = gated
    forward_transform(signal, ahead, fine, coarse, turn_rows, stage, parts)
    fetch.wait()
    for k in range(TILES):
        rows = slice(k * ROWS, (k + 1) * ROWS)
        mid = table_dot(parts[rows, 0:256], parts[rows, 256:512], forward)
        a, b = mid[:, 0:LANES], mid[:, LANES:]
        c, d = gain[rows, 0:LANES], gain[rows, LANES:]
        re_upper, re_lower = split(a * c - b * d)
        im_upper, im_lower = split(a * d + b * c)
        upper = jnp.concatenate([re_upper, im_upper], axis=1)
        lower = jnp.concatenate([re_lower, im_lower], axis=1)
        product[rows] = table_dot(upper, lower, inverse)

    def unspin(step, carry):
        at = pl.multiple_of(step * 16, 16)
        spins = spin_rows(fine, coarse, step)
        real, imag = [], []
        for k in range(TILES):
            rows = pl.ds(at + k * ROWS, 16)
            a, b = product[rows, 0:128], product[rows, 128:256]
            if k > 0:
                c, d = turn_rows[k : k + 1], turn_rows[TILES + k : TILES + k + 1]
                a, b = a * c + b * d, b * c - a * d
            real.append(a)
            imag.append(b)
        er, ei = real[0] + real[2], imag[0] + imag[2]
        fr, fi = real[0] - real[2], imag[0] - imag[2]
        gr, gi = real[1] + real[3], imag[1] + imag[3]
        hr, hi = real[1] - real[3], imag[1] - imag[3]
        outs = ((er + gr, ei + gi), (fr - hi, fi + hr), (er - gr, ei - gi), (fr + hi, fi - hr))
        for q, (a, b) in enumerate(outs):
            lanes = slice(q * LANES, (q + 1) * LANES)
            c, d = spins[q]
            parts[pl.ds(at, 16), lanes], parts[pl.ds(at + 2 * ROWS, 16), lanes] = split(a * c + b * d)
            parts[pl.ds(at + ROWS, 16), lanes], parts[pl.ds(at + 3 * ROWS, 16), lanes] = split(b * c - a * d)
        return carry

    lax.fori_loop(0, ROWS // 16, unspin, 0, unroll=2)
    for q in range(TILES):
        lanes = slice(q * LANES, (q + 1) * LANES)
        upper, lower = parts[0:512, lanes], parts[512:1024, lanes]
        long_part = dot(back[:, 0:512], upper) + dot(back[:, 0:512], lower) + dot(back[:, 512:1024], upper)
        total = query[:, lanes] * (long_part + skip[...] * signal[0:ROWS, lanes].astype(F32))
        result[pl.ds(q, ROWS, stride=TILES), :] = total
    out_ref[...] = result[...].reshape(DEVICES, TILES, LANES).astype(BF16)


def convolve(packed, bands, skip, gain, ahead, back, fine, coarse, turn_rows, forward, inverse):
    return pl.pallas_call(
        conv_kernel,
        out_shape=jax.ShapeDtypeStruct((DEVICES, TILES, LANES), BF16),
        in_specs=[VMEM] * 3 + [pl.BlockSpec(memory_space=pl.ANY)] + [VMEM] * 7,
        out_specs=VMEM,
        scratch_shapes=[
            pltpu.VMEM((1 + DEVICES, 8, LANES), F32),
            pltpu.VMEM((1 + DEVICES, TILES, LANES), F32),
            pltpu.VMEM((2 * ROWS, TILES * LANES), BF16),
            pltpu.VMEM((ROWS, TILES * LANES), F32),
            pltpu.VMEM((2 * ROWS, TILES * LANES), F32),
            pltpu.VMEM((TILES * ROWS, 4 * LANES), BF16),
            pltpu.VMEM((TILES * ROWS, 2 * LANES), F32),
            pltpu.VMEM((DEVICES * TILES, LANES), F32),
            pltpu.VMEM((TILES * ROWS, 2 * LANES), F32),
            pltpu.SemaphoreType.DMA,
        ],
        cost_estimate=pl.CostEstimate(flops=4_000_000_000, bytes_accessed=6_000_000, transcendentals=0),
        compiler_params=pltpu.CompilerParams(vmem_limit_bytes=24 * 2**20),
        name="convolve",
    )(packed, bands, skip, gain, ahead, back, fine, coarse, turn_rows, forward, inverse)


def unpack_kernel(mixed_ref, out_ref, before, after):
    for first in range(0, CH, 8):
        for at in range(8):
            for half in range(2):
                before[first + at, :, half * TILES : (half + 1) * TILES, :] = mixed_ref[half, :, first + at].astype(F32)
        done = [[before[first + at, d] for d in range(GROUPS)] for at in range(8)]
        done = [exchange(tiles) for tiles in done]
        for at in range(8):
            for t in range(GROUPS):
                after[first + at, pl.ds(t, 8, stride=GROUPS), :] = done[at][t]
    for j in range(CH):
        for half in range(2):
            lanes = slice((2 * j + half) * LANES, (2 * j + half + 1) * LANES)
            out_ref[:, lanes] = after[j, half * BLOCK : (half + 1) * BLOCK].astype(BF16)


def unpack(mixed):
    return pl.pallas_call(
        unpack_kernel,
        out_shape=jax.ShapeDtypeStruct((BLOCK, WIDTH), BF16),
        in_specs=[VMEM],
        out_specs=VMEM,
        scratch_shapes=[pltpu.VMEM((CH, GROUPS, 8, LANES), F32), pltpu.VMEM((CH, 2 * BLOCK, LANES), F32)],
        cost_estimate=pl.CostEstimate(flops=4_000_000, bytes_accessed=500_000, transcendentals=0),
        compiler_params=pltpu.CompilerParams(vmem_limit_bytes=8 * 2**20),
        name="unpack",
    )(mixed)


def band_kernel(taps, out_ref):
    for at in range(0, 2 * LANES, 64):
        row = lax.broadcasted_iota(jnp.int32, (64, LANES), 0) + at
        lane = lax.broadcasted_iota(jnp.int32, (64, LANES), 1)
        lag = (lane >> 4) - ((row & LANES - 1) >> 4) + jnp.where(row < LANES, GROUPS, 0)
        lag = jnp.where(((row ^ lane) & OWN - 1) == 0, lag, -1)
        for stream in range(STREAMS):
            band = jnp.zeros((64, LANES), F32)
            for r in range(SHORT):
                band = jnp.where(lag == r, taps[STREAMS * r + stream : STREAMS * r + stream + 1], band)
            out_ref[stream, at : at + 64, 0:LANES], out_ref[stream, at : at + 64, LANES:] = split(band)


def short_bands(taps):
    return pl.pallas_call(
        band_kernel,
        out_shape=jax.ShapeDtypeStruct((STREAMS, 2 * LANES, 2 * LANES), BF16),
        in_specs=[VMEM],
        out_specs=VMEM,
        cost_estimate=pl.CostEstimate(flops=2_000_000, bytes_accessed=500_000, transcendentals=0),
        compiler_params=pltpu.CompilerParams(vmem_limit_bytes=8 * 2**20),
        name="short_bands",
    )(taps)


def own_rows(short_weight, row):
    count = STREAMS * SHORT
    taps = lax.dynamic_slice(short_weight, (0, 0, row * OWN), (SHORT, STREAMS, OWN)).reshape(count, OWN)
    return jnp.tile(jnp.pad(taps, ((0, -count % 8), (0, 0))), (1, GROUPS))


def local(inputs, short_weight, long_filter, skip_gain):
    row = lax.axis_index("ctx")
    ahead, back, fine, coarse, turn_rows, forward, inverse = (jnp.asarray(t) for t in tables())
    packed = pack(jnp.transpose(inputs, (1, 0, 2))).reshape(DEVICES, STREAMS, TILES, LANES)
    packed = lax.all_to_all(packed, ("ctx", "ch"), 0, 0, tiled=True)
    place = jnp.stack([row // GROUPS, row % GROUPS]).astype(jnp.int32)
    gain = filter_transform(place, long_filter, ahead, fine, coarse, turn_rows, forward)
    bands = short_bands(own_rows(short_weight, row))
    skip = jnp.tile(lax.dynamic_slice(skip_gain, (row * OWN,), (OWN,)), GROUPS).reshape(1, LANES)
    mixed = convolve(packed, bands, skip, gain, ahead, back, fine, coarse, turn_rows, forward, inverse)
    mixed = lax.all_to_all(mixed, ("ctx", "ch"), 0, 0, tiled=True)
    return unpack(mixed.reshape(2, GROUPS, CH, TILES, LANES))


def solution(mesh):
    in_specs = (P(("ctx", "ch"), None, None), P(None, None, "ch"), P(None, "ch"), P("ch"))
    out_specs = P(("ctx", "ch"), None)
    return jax.shard_map(local, mesh=mesh, in_specs=in_specs, out_specs=out_specs, check_vma=False)
```

```python
import functools
import math

import jax
import jax.numpy as jnp
import ml_dtypes
import numpy as np
from jax import lax
from jax.experimental import pallas as pl
from jax.experimental.pallas import tpu as pltpu
from jax.sharding import PartitionSpec as P

SHORT = 7
STREAMS = 3
CTX = 16
CH = 16
DEVICES = CTX * CH
BLOCK = 32
LANES = 128
OWN = 16
GROUPS = LANES // OWN
TILES = BLOCK // GROUPS
LENGTH = DEVICES * BLOCK
WIDTH = DEVICES * OWN
PACK = 4
HELD = 40
MESSAGE = STREAMS * TILES
MESSAGE_PAD = 16
CHUNK = 16
ROWS = DEVICES
F32 = jnp.float32
VMEM = pl.BlockSpec(memory_space=pltpu.VMEM)
BF16 = jnp.bfloat16


def halves(table):
    upper = table.astype(ml_dtypes.bfloat16)
    lower = (table - upper.astype(np.float64)).astype(ml_dtypes.bfloat16)
    return upper, lower


@functools.lru_cache(maxsize=None)
def tables():
    turn = 2.0 * math.pi
    freq = (np.arange(ROWS) + 0.5) / (2 * ROWS)
    block = np.arange(ROWS)
    angle = turn * freq[:, None] * block[None, :]
    first = np.concatenate([np.cos(angle), -np.sin(angle)], axis=0)
    upper, lower = halves(first)
    ahead = np.concatenate([upper, lower], axis=1)

    last = np.concatenate([np.cos(angle), -np.sin(angle)], axis=0).T * (2.0 / (2 * LENGTH))
    upper, lower = halves(last)
    back = np.concatenate([upper, lower], axis=1)

    lane = np.arange(LANES)
    place = (np.arange(TILES)[:, None] * GROUPS + lane[None, :] // OWN).reshape(-1)
    fine = turn * freq[:CHUNK, None] * place[None, :] / BLOCK
    coarse = turn * (np.arange(ROWS // CHUNK) * CHUNK / (2 * ROWS))[:, None] * place[None, :] / BLOCK
    fine = np.concatenate([np.cos(fine), -np.sin(fine)], axis=1).astype(np.float32)
    coarse = np.concatenate([np.cos(coarse), -np.sin(coarse)], axis=1).astype(np.float32).reshape(-1, 2 * TILES, LANES)

    angle = turn * np.arange(TILES)[:, None] * (lane[None, :] // OWN) / BLOCK
    turn_rows = np.concatenate([np.cos(angle), -np.sin(angle)], axis=0).astype(np.float32)

    same = (lane[:, None] % OWN) == (lane[None, :] % OWN)
    angle = turn * (lane[:, None] // OWN) * (lane[None, :] // OWN) / GROUPS
    cosine = np.where(same, np.cos(angle), 0.0)
    sine = np.where(same, np.sin(angle), 0.0)
    forward = np.block([[cosine, -sine], [sine, cosine]])
    inverse = np.block([[cosine, sine], [-sine, cosine]])
    upper, lower = halves(forward)
    forward = np.concatenate([upper, lower], axis=0)
    upper, lower = halves(inverse)
    inverse = np.concatenate([upper, lower], axis=0)
    return ahead, back, fine, coarse, turn_rows, forward, inverse


def dot(left, right):
    return jnp.dot(left, right, preferred_element_type=F32)


def split(value):
    upper = value.astype(BF16)
    return upper, (value - upper.astype(F32)).astype(BF16)


def exchange(tiles):
    lane = lax.broadcasted_iota(jnp.int32, (GROUPS, LANES), 1)
    for step in (4, 2, 1):
        shift = step * OWN
        low = (lane & shift) == 0
        moved = list(tiles)
        for t in range(GROUPS):
            if t & step == 0:
                a, b = tiles[t], tiles[t + step]
                if step == 4:
                    across = pltpu.roll(jnp.where(low, b, a), shift, 1)
                    moved[t], moved[t + step] = jnp.where(low, a, across), jnp.where(low, across, b)
                else:
                    moved[t] = jnp.where(low, a, pltpu.roll(b, shift, 1))
                    moved[t + step] = jnp.where(low, pltpu.roll(a, LANES - shift, 1), b)
        tiles = moved
    return tiles


def half_lanes(j, half):
    return pl.ds(pl.multiple_of(j * 2 * LANES, LANES) + half * LANES, LANES)


def exchange_all(slots):
    before = [[slot[pl.ds(t, 8, stride=GROUPS), :] for t in range(GROUPS)] for slot in slots]
    return [exchange(tiles) for tiles in before]


def pack_kernel(q_ref, k_ref, v_ref, out_ref, scratch):
    slots = [scratch.at[at] for at in range(3 * PACK)]
    for pair in range(PACK // 2):
        for half in range(2):
            for at in range(6):
                later, stream = divmod(at, 3)
                tile = 2 * (2 * pair + later) + half
                lanes = slice(tile * LANES, (tile + 1) * LANES)
                slot = slots[(pair * 2 + half) * 3 + at // 2]
                rows = (k_ref, v_ref, q_ref)[stream][0, :, lanes].astype(F32)
                slot[at % 2 * BLOCK : (at % 2 + 1) * BLOCK] = rows
    for first in range(0, 3 * PACK, 6):
        for at, tiles in enumerate(exchange_all(slots[first : first + 6])):
            which, third = divmod(first + at, 3)
            pair, half = divmod(which, 2)
            for d in range(GROUPS):
                out_ref[half, d, pair, third] = tiles[d].astype(BF16)


def pack(streams):
    lanes = PACK * 2 * LANES
    part = (1, BLOCK, lanes)
    return pl.pallas_call(
        pack_kernel,
        grid=(CH // PACK,),
        out_shape=jax.ShapeDtypeStruct((2, GROUPS, CH // 2, 3, 8, LANES), BF16),
        in_specs=[pl.BlockSpec(part, lambda g, s=s: (s, 0, g)) for s in range(3)],
        out_specs=pl.BlockSpec((2, GROUPS, PACK // 2, 3, 8, LANES), lambda g: (0, 0, g, 0, 0, 0)),
        scratch_shapes=[pltpu.VMEM((3 * PACK, 2 * BLOCK, LANES), F32)],
        cost_estimate=pl.CostEstimate(flops=4_000_000, bytes_accessed=1_600_000, transcendentals=0),
        compiler_params=pltpu.CompilerParams(vmem_limit_bytes=58 * 2**20),
        name="pack",
    )(streams, streams, streams)


def spin_rows(fine, coarse, step):
    rows = coarse[step]
    spins = []
    for q in range(TILES):
        re = slice(q * LANES, (q + 1) * LANES)
        im = slice((TILES + q) * LANES, (TILES + q + 1) * LANES)
        a, b = fine[:, re], fine[:, im]
        c, d = rows[q : q + 1], rows[TILES + q : TILES + q + 1]
        spins.append((a * c - b * d, a * d + b * c))
    return spins


def table_dot(upper, lower, table):
    return dot(upper, table[0:256]) + dot(lower, table[0:256]) + dot(upper, table[256:512])


def forward_transform(signal, ahead, fine, coarse, turn_rows, stage, parts):
    stage[...] = dot(ahead[...], signal[...])

    def rows(step, carry):
        at = pl.multiple_of(step * 16, 16)
        here, below = pl.ds(at, 16), pl.ds(at + ROWS, 16)
        spins = spin_rows(fine, coarse, step)
        real, imag = [], []
        for q in range(TILES):
            lanes = slice(q * LANES, (q + 1) * LANES)
            a, b = stage[here, lanes], stage[below, lanes]
            c, d = spins[q]
            real.append(a * c - b * d)
            imag.append(a * d + b * c)
        er, ei = real[0] + real[2], imag[0] + imag[2]
        fr, fi = real[0] - real[2], imag[0] - imag[2]
        gr, gi = real[1] + real[3], imag[1] + imag[3]
        hr, hi = real[1] - real[3], imag[1] - imag[3]
        outs = ((er + gr, ei + gi), (fr + hi, fi - hr), (er - gr, ei - gi), (fr - hi, fi + hr))
        for k, (a, b) in enumerate(outs):
            if k > 0:
                c, d = turn_rows[k : k + 1], turn_rows[TILES + k : TILES + k + 1]
                a, b = a * c - b * d, a * d + b * c
            to = pl.ds(at + k * ROWS, 16)
            parts[to, 0:128], parts[to, 256:384] = split(a)
            parts[to, 128:256], parts[to, 384:512] = split(b)
        return carry

    lax.fori_loop(0, ROWS // 16, rows, 0, unroll=2)


def filter_kernel(place, filter_ref, ahead, fine, coarse, turn_rows, forward, out_ref, wide, signal, stage, parts, result, sent):
    step = pl.program_id(0)
    shift = place[1]
    wide[...] = filter_ref[...].astype(F32)
    group = lax.broadcasted_iota(jnp.int32, (BLOCK, LANES), 1) // OWN
    at = pl.multiple_of(step * BLOCK, BLOCK)
    for q in range(TILES):
        tile = jnp.zeros((BLOCK, LANES), F32)
        for t in range(GROUPS):
            rows = wide[pl.ds(q * GROUPS + t, BLOCK, stride=BLOCK), :]
            if t > 0:
                rows = pltpu.roll(rows, t * OWN, 1)
            tile = jnp.where(group == (shift + t) % GROUPS, rows, tile)
        tile = pltpu.roll(tile, (GROUPS - shift) % GROUPS * OWN, 1).astype(BF16)
        signal[pl.ds(at, BLOCK), q * LANES : (q + 1) * LANES] = tile
        signal[pl.ds(at + ROWS, BLOCK), q * LANES : (q + 1) * LANES] = tile

    @pl.when(step == pl.num_programs(0) - 1)
    def _():
        forward_transform(signal, ahead, fine, coarse, turn_rows, stage, parts)
        result[...] = table_dot(parts[:, 0:256], parts[:, 256:512], forward)
        send = pltpu.make_async_copy(result, out_ref.at[0 : TILES * ROWS], sent)
        send.start()
        send.wait()


def whole_spec(shape):
    return pl.BlockSpec(shape, lambda *_: (0,) * len(shape))


def filter_transform(place, long_filter, ahead, fine, coarse, turn_rows, forward):
    chunk = BLOCK * BLOCK
    consts = (ahead, fine, coarse, turn_rows, forward)
    return pl.pallas_call(
        filter_kernel,
        out_shape=jax.ShapeDtypeStruct((HELD * TILES * ROWS, 2 * LANES), F32),
        grid_spec=pltpu.PrefetchScalarGridSpec(
            num_scalar_prefetch=1,
            grid=(LENGTH // chunk,),
            in_specs=[pl.BlockSpec((chunk, LANES), lambda g, s: (g, s[0]))] + [whole_spec(c.shape) for c in consts],
            out_specs=pl.BlockSpec(memory_space=pl.ANY),
            scratch_shapes=[
                pltpu.VMEM((chunk, LANES), F32),
                pltpu.VMEM((2 * ROWS, TILES * LANES), BF16),
                pltpu.VMEM((2 * ROWS, TILES * LANES), F32),
                pltpu.VMEM((TILES * ROWS, 4 * LANES), BF16),
                pltpu.VMEM((TILES * ROWS, 2 * LANES), F32),
                pltpu.SemaphoreType.DMA,
            ],
        ),
        cost_estimate=pl.CostEstimate(flops=2_000_000_000, bytes_accessed=6_000_000, transcendentals=0),
        compiler_params=pltpu.CompilerParams(vmem_limit_bytes=58 * 2**20),
        name="filter_transform",
    )(place, long_filter, *consts)


def conv_kernel(
    packed, bands, skip, gain_ref, ahead, back, fine, coarse, turn_rows, forward, inverse, out_ref,
    wide, signal, query, stage, parts, product, result, gain, arrived,
):
    fetch = pltpu.make_async_copy(gain_ref.at[0 : TILES * ROWS], gain, arrived)
    fetch.start()
    wide[0:MESSAGE_PAD] = jnp.zeros((MESSAGE_PAD, LANES), F32)
    wide[MESSAGE_PAD:] = packed[...].astype(F32).reshape(DEVICES * MESSAGE, LANES)

    def rows_of(stream, q):
        at = MESSAGE_PAD + stream * TILES + q
        if q < 0:
            at += TILES - MESSAGE
        return wide[pl.ds(at, DEVICES, stride=MESSAGE), :].astype(BF16)

    for q in range(TILES):
        lanes = slice(q * LANES, (q + 1) * LANES)
        sums = []
        for stream in range(STREAMS):
            both = jnp.concatenate([rows_of(stream, q - 1), rows_of(stream, q)], axis=1)
            halves_of = dot(both, bands[(stream + 1) % STREAMS])
            sums.append(halves_of[:, 0:LANES] + halves_of[:, LANES:])
        query[:, lanes] = sums[2]
        gated = (sums[0] * sums[1]).astype(BF16)
        signal[0:ROWS, lanes] = gated
        signal[ROWS:, lanes] = gated
    forward_transform(signal, ahead, fine, coarse, turn_rows, stage, parts)
    fetch.wait()
    for k in range(TILES):
        rows = slice(k * ROWS, (k + 1) * ROWS)
        mid = table_dot(parts[rows, 0:256], parts[rows, 256:512], forward)
        a, b = mid[:, 0:LANES], mid[:, LANES:]
        c, d = gain[rows, 0:LANES], gain[rows, LANES:]
        re_upper, re_lower = split(a * c - b * d)
        im_upper, im_lower = split(a * d + b * c)
        upper = jnp.concatenate([re_upper, im_upper], axis=1)
        lower = jnp.concatenate([re_lower, im_lower], axis=1)
        product[rows] = table_dot(upper, lower, inverse)

    def unspin(step, carry):
        at = pl.multiple_of(step * 16, 16)
        spins = spin_rows(fine, coarse, step)
        real, imag = [], []
        for k in range(TILES):
            rows = pl.ds(at + k * ROWS, 16)
            a, b = product[rows, 0:128], product[rows, 128:256]
            if k > 0:
                c, d = turn_rows[k : k + 1], turn_rows[TILES + k : TILES + k + 1]
                a, b = a * c + b * d, b * c - a * d
            real.append(a)
            imag.append(b)
        er, ei = real[0] + real[2], imag[0] + imag[2]
        fr, fi = real[0] - real[2], imag[0] - imag[2]
        gr, gi = real[1] + real[3], imag[1] + imag[3]
        hr, hi = real[1] - real[3], imag[1] - imag[3]
        outs = ((er + gr, ei + gi), (fr - hi, fi + hr), (er - gr, ei - gi), (fr + hi, fi - hr))
        for q, (a, b) in enumerate(outs):
            lanes = slice(q * LANES, (q + 1) * LANES)
            c, d = spins[q]
            parts[pl.ds(at, 16), lanes], parts[pl.ds(at + 2 * ROWS, 16), lanes] = split(a * c + b * d)
            parts[pl.ds(at + ROWS, 16), lanes], parts[pl.ds(at + 3 * ROWS, 16), lanes] = split(b * c - a * d)
        return carry

    lax.fori_loop(0, ROWS // 16, unspin, 0, unroll=2)
    for q in range(TILES):
        lanes = slice(q * LANES, (q + 1) * LANES)
        upper, lower = parts[0:512, lanes], parts[512:1024, lanes]
        long_part = dot(back[:, 0:512], upper) + dot(back[:, 0:512], lower) + dot(back[:, 512:1024], upper)
        total = query[:, lanes] * (long_part + skip[...] * signal[0:ROWS, lanes].astype(F32))
        result[pl.ds(q, ROWS, stride=TILES), :] = total
    out_ref[...] = result[...].reshape(DEVICES // 2, 2 * TILES, LANES).astype(BF16)


def convolve(packed, bands, skip, gain, ahead, back, fine, coarse, turn_rows, forward, inverse):
    return pl.pallas_call(
        conv_kernel,
        out_shape=jax.ShapeDtypeStruct((DEVICES // 2, 2 * TILES, LANES), BF16),
        in_specs=[VMEM] * 3 + [pl.BlockSpec(memory_space=pl.ANY)] + [VMEM] * 7,
        out_specs=VMEM,
        scratch_shapes=[
            pltpu.VMEM((MESSAGE_PAD + DEVICES * MESSAGE, LANES), F32),
            pltpu.VMEM((2 * ROWS, TILES * LANES), BF16),
            pltpu.VMEM((ROWS, TILES * LANES), F32),
            pltpu.VMEM((2 * ROWS, TILES * LANES), F32),
            pltpu.VMEM((TILES * ROWS, 4 * LANES), BF16),
            pltpu.VMEM((TILES * ROWS, 2 * LANES), F32),
            pltpu.VMEM((DEVICES * TILES, LANES), F32),
            pltpu.VMEM((TILES * ROWS, 2 * LANES), F32),
            pltpu.SemaphoreType.DMA,
        ],
        cost_estimate=pl.CostEstimate(flops=4_000_000_000, bytes_accessed=6_000_000, transcendentals=0),
        compiler_params=pltpu.CompilerParams(vmem_limit_bytes=24 * 2**20),
        name="convolve",
    )(packed, bands, skip, gain, ahead, back, fine, coarse, turn_rows, forward, inverse)


def unpack_kernel(mixed_ref, out_ref, after):
    for half in range(2):
        came = [[mixed_ref[half, d, pair].astype(F32) for d in range(GROUPS)] for pair in range(CH // 2)]
        done = [exchange(tiles) for tiles in came]
        for pair, tiles in enumerate(done):
            for t in range(GROUPS):
                after[half, pair, pl.ds(t, 8, stride=GROUPS), :] = tiles[t]
    for j in range(CH):
        for half in range(2):
            lanes = slice((2 * j + half) * LANES, (2 * j + half + 1) * LANES)
            out_ref[:, lanes] = after[half, j // 2, j % 2 * BLOCK : (j % 2 + 1) * BLOCK].astype(BF16)


def unpack(mixed):
    return pl.pallas_call(
        unpack_kernel,
        out_shape=jax.ShapeDtypeStruct((BLOCK, WIDTH), BF16),
        in_specs=[VMEM],
        out_specs=VMEM,
        scratch_shapes=[pltpu.VMEM((2, CH // 2, 2 * BLOCK, LANES), F32)],
        cost_estimate=pl.CostEstimate(flops=4_000_000, bytes_accessed=500_000, transcendentals=0),
        compiler_params=pltpu.CompilerParams(vmem_limit_bytes=8 * 2**20),
        name="unpack",
    )(mixed)


def band_kernel(taps, out_ref):
    for at in range(0, 2 * LANES, 64):
        row = lax.broadcasted_iota(jnp.int32, (64, LANES), 0) + at
        lane = lax.broadcasted_iota(jnp.int32, (64, LANES), 1)
        lag = (lane >> 4) - ((row & LANES - 1) >> 4) + jnp.where(row < LANES, GROUPS, 0)
        lag = jnp.where(((row ^ lane) & OWN - 1) == 0, lag, -1)
        for stream in range(STREAMS):
            band = jnp.zeros((64, LANES), F32)
            for r in range(SHORT):
                band = jnp.where(lag == r, taps[STREAMS * r + stream : STREAMS * r + stream + 1], band)
            out_ref[stream, at : at + 64, 0:LANES], out_ref[stream, at : at + 64, LANES:] = split(band)


def short_bands(taps):
    return pl.pallas_call(
        band_kernel,
        out_shape=jax.ShapeDtypeStruct((STREAMS, 2 * LANES, 2 * LANES), BF16),
        in_specs=[VMEM],
        out_specs=VMEM,
        cost_estimate=pl.CostEstimate(flops=2_000_000, bytes_accessed=500_000, transcendentals=0),
        compiler_params=pltpu.CompilerParams(vmem_limit_bytes=8 * 2**20),
        name="short_bands",
    )(taps)


def own_rows(short_weight, row):
    count = STREAMS * SHORT
    taps = lax.dynamic_slice(short_weight, (0, 0, row * OWN), (SHORT, STREAMS, OWN)).reshape(count, OWN)
    return jnp.tile(jnp.pad(taps, ((0, -count % 8), (0, 0))), (1, GROUPS))


def local(inputs, short_weight, long_filter, skip_gain):
    row = lax.axis_index("ctx")
    ahead, back, fine, coarse, turn_rows, forward, inverse = (jnp.asarray(t) for t in tables())
    packed = pack(jnp.transpose(inputs, (1, 0, 2))).reshape(DEVICES, STREAMS, TILES, LANES)
    packed = lax.all_to_all(packed, ("ctx", "ch"), 0, 0, tiled=True)
    packed = packed.reshape(DEVICES * MESSAGE // 8, 8, LANES)
    place = jnp.stack([row // GROUPS, row % GROUPS]).astype(jnp.int32)
    gain = filter_transform(place, long_filter, ahead, fine, coarse, turn_rows, forward)
    bands = short_bands(own_rows(short_weight, row))
    skip = jnp.tile(lax.dynamic_slice(skip_gain, (row * OWN,), (OWN,)), GROUPS).reshape(1, LANES)
    mixed = convolve(packed, bands, skip, gain, ahead, back, fine, coarse, turn_rows, forward, inverse)
    mixed = lax.all_to_all(mixed.reshape(DEVICES, TILES, LANES), ("ctx", "ch"), 0, 0, tiled=True)
    return unpack(mixed.reshape(2, GROUPS, CH // 2, 2 * TILES, LANES))


def solution(mesh):
    in_specs = (P(("ctx", "ch"), None, None), P(None, None, "ch"), P(None, "ch"), P("ch"))
    out_specs = P(("ctx", "ch"), None)
    return jax.shard_map(local, mesh=mesh, in_specs=in_specs, out_specs=out_specs, check_vma=False)
```

```python
import functools
import math

import jax
import jax.numpy as jnp
import ml_dtypes
import numpy as np
from jax import lax
from jax.experimental import pallas as pl
from jax.experimental.pallas import tpu as pltpu
from jax.sharding import PartitionSpec as P

SHORT = 7
STREAMS = 3
CTX = 16
CH = 16
DEVICES = CTX * CH
BLOCK = 32
LANES = 128
OWN = 16
GROUPS = LANES // OWN
TILES = BLOCK // GROUPS
LENGTH = DEVICES * BLOCK
WIDTH = DEVICES * OWN
HELD = 40
PAIRS = 2
MESSAGE = STREAMS * TILES
MESSAGE_PAD = 16
CHUNK = 16
ROWS = DEVICES
F32 = jnp.float32
VMEM = pl.BlockSpec(memory_space=pltpu.VMEM)
BF16 = jnp.bfloat16


def halves(table):
    upper = table.astype(ml_dtypes.bfloat16)
    lower = (table - upper.astype(np.float64)).astype(ml_dtypes.bfloat16)
    return upper, lower


@functools.lru_cache(maxsize=None)
def tables():
    turn = 2.0 * math.pi
    freq = (np.arange(ROWS) + 0.5) / (2 * ROWS)
    block = np.arange(ROWS)
    angle = turn * freq[:, None] * block[None, :]
    first = np.concatenate([np.cos(angle), -np.sin(angle)], axis=0)
    upper, lower = halves(first)
    ahead = np.concatenate([upper, lower], axis=1)

    last = np.concatenate([np.cos(angle), -np.sin(angle)], axis=0).T * (2.0 / (2 * LENGTH))
    upper, lower = halves(last)
    back = np.concatenate([upper, lower], axis=1)

    lane = np.arange(LANES)
    place = (np.arange(TILES)[:, None] * GROUPS + lane[None, :] // OWN).reshape(-1)
    fine = turn * freq[:CHUNK, None] * place[None, :] / BLOCK
    coarse = turn * (np.arange(ROWS // CHUNK) * CHUNK / (2 * ROWS))[:, None] * place[None, :] / BLOCK
    fine = np.concatenate([np.cos(fine), -np.sin(fine)], axis=1).astype(np.float32)
    coarse = np.concatenate([np.cos(coarse), -np.sin(coarse)], axis=1).astype(np.float32).reshape(-1, 2 * TILES, LANES)

    angle = turn * np.arange(TILES)[:, None] * (lane[None, :] // OWN) / BLOCK
    turn_rows = np.concatenate([np.cos(angle), -np.sin(angle)], axis=0).astype(np.float32)

    same = (lane[:, None] % OWN) == (lane[None, :] % OWN)
    angle = turn * (lane[:, None] // OWN) * (lane[None, :] // OWN) / GROUPS
    cosine = np.where(same, np.cos(angle), 0.0)
    sine = np.where(same, np.sin(angle), 0.0)
    forward = np.block([[cosine, -sine], [sine, cosine]])
    inverse = np.block([[cosine, sine], [-sine, cosine]])
    upper, lower = halves(forward)
    forward = np.concatenate([upper, lower], axis=0)
    upper, lower = halves(inverse)
    inverse = np.concatenate([upper, lower], axis=0)
    return ahead, back, fine, coarse, turn_rows, forward, inverse


def dot(left, right):
    return jnp.dot(left, right, preferred_element_type=F32)


def split(value):
    upper = value.astype(BF16)
    return upper, (value - upper.astype(F32)).astype(BF16)


def exchange(tiles):
    lane = lax.broadcasted_iota(jnp.int32, (GROUPS, LANES), 1)
    for step in (4, 2, 1):
        shift = step * OWN
        low = (lane & shift) == 0
        moved = list(tiles)
        for t in range(GROUPS):
            if t & step == 0:
                a, b = tiles[t], tiles[t + step]
                if step == 4:
                    across = pltpu.roll(jnp.where(low, b, a), shift, 1)
                    moved[t], moved[t + step] = jnp.where(low, a, across), jnp.where(low, across, b)
                else:
                    moved[t] = jnp.where(low, a, pltpu.roll(b, shift, 1))
                    moved[t + step] = jnp.where(low, pltpu.roll(a, LANES - shift, 1), b)
        tiles = moved
    return tiles


def half_lanes(j, half):
    return pl.ds(pl.multiple_of(j * 2 * LANES, LANES) + half * LANES, LANES)


def exchange_all(slots):
    before = [[slot[pl.ds(t, 8, stride=GROUPS), :] for t in range(GROUPS)] for slot in slots]
    return [exchange(tiles) for tiles in before]


def pack_kernel(streams, out_ref, held, slots, packed, arrived, sent):
    fetches = []
    for pair in range(CH // 2):
        lanes = slice(pair * 4 * LANES, (pair + 1) * 4 * LANES)
        fetches.append(pltpu.make_async_copy(streams.at[:, :, lanes], held.at[pair], arrived.at[pair]))
        fetches[-1].start()
    sends = []
    for first in range(0, CH // 2, PAIRS):
        here = [slots.at[first // PAIRS % 2, at] for at in range(6 * PAIRS)]
        for pair in range(first, first + PAIRS):
            fetches[pair].wait()
        for pair in range(first, first + PAIRS):
            for half in range(2):
                for at in range(6):
                    later, stream = divmod(at, 3)
                    tile = 2 * later + half
                    rows = held[pair, (stream + 1) % STREAMS, :, tile * LANES : (tile + 1) * LANES].astype(F32)
                    slot = here[((pair - first) * 2 + half) * 3 + at // 2]
                    slot[at % 2 * BLOCK : (at % 2 + 1) * BLOCK] = rows
        for at, tiles in enumerate(exchange_all(here)):
            which, third = divmod(at, 3)
            for d in range(GROUPS):
                packed[first + which // 2, which % 2, d, third] = tiles[d].astype(BF16)
        for pair in range(first, first + PAIRS):
            sends.append(pltpu.make_async_copy(packed.at[pair], out_ref.at[:, :, pair], sent.at[pair]))
            sends[-1].start()
    for send in sends:
        send.wait()


def pack(streams):
    pairs = CH // 2
    return pl.pallas_call(
        pack_kernel,
        out_shape=jax.ShapeDtypeStruct((2, GROUPS, pairs, 3, 8, LANES), BF16),
        in_specs=[pl.BlockSpec(memory_space=pl.ANY)],
        out_specs=pl.BlockSpec(memory_space=pl.ANY),
        scratch_shapes=[
            pltpu.VMEM((pairs, STREAMS, BLOCK, 4 * LANES), BF16),
            pltpu.VMEM((2, 6 * PAIRS, 2 * BLOCK, LANES), F32),
            pltpu.VMEM((pairs, 2, GROUPS, 3, 8, LANES), BF16),
            pltpu.SemaphoreType.DMA((pairs,)),
            pltpu.SemaphoreType.DMA((pairs,)),
        ],
        cost_estimate=pl.CostEstimate(flops=4_000_000, bytes_accessed=1_600_000, transcendentals=0),
        compiler_params=pltpu.CompilerParams(vmem_limit_bytes=58 * 2**20),
        name="pack",
    )(streams)


def spin_rows(fine, coarse, step):
    rows = coarse[step]
    spins = []
    for q in range(TILES):
        re = slice(q * LANES, (q + 1) * LANES)
        im = slice((TILES + q) * LANES, (TILES + q + 1) * LANES)
        a, b = fine[:, re], fine[:, im]
        c, d = rows[q : q + 1], rows[TILES + q : TILES + q + 1]
        spins.append((a * c - b * d, a * d + b * c))
    return spins


def table_dot(upper, lower, table):
    return dot(upper, table[0:256]) + dot(lower, table[0:256]) + dot(upper, table[256:512])


def forward_transform(signal, ahead, fine, coarse, turn_rows, stage, parts):
    stage[...] = dot(ahead[...], signal[...])

    def rows(step, carry):
        at = pl.multiple_of(step * 16, 16)
        here, below = pl.ds(at, 16), pl.ds(at + ROWS, 16)
        spins = spin_rows(fine, coarse, step)
        real, imag = [], []
        for q in range(TILES):
            lanes = slice(q * LANES, (q + 1) * LANES)
            a, b = stage[here, lanes], stage[below, lanes]
            c, d = spins[q]
            real.append(a * c - b * d)
            imag.append(a * d + b * c)
        er, ei = real[0] + real[2], imag[0] + imag[2]
        fr, fi = real[0] - real[2], imag[0] - imag[2]
        gr, gi = real[1] + real[3], imag[1] + imag[3]
        hr, hi = real[1] - real[3], imag[1] - imag[3]
        outs = ((er + gr, ei + gi), (fr + hi, fi - hr), (er - gr, ei - gi), (fr - hi, fi + hr))
        for k, (a, b) in enumerate(outs):
            if k > 0:
                c, d = turn_rows[k : k + 1], turn_rows[TILES + k : TILES + k + 1]
                a, b = a * c - b * d, a * d + b * c
            to = pl.ds(at + k * ROWS, 16)
            parts[to, 0:128], parts[to, 256:384] = split(a)
            parts[to, 128:256], parts[to, 384:512] = split(b)
        return carry

    lax.fori_loop(0, ROWS // 16, rows, 0, unroll=2)


def filter_kernel(place, filter_ref, ahead, fine, coarse, turn_rows, forward, out_ref, wide, signal, stage, parts, result, sent):
    step = pl.program_id(0)
    shift = place[1]
    wide[...] = filter_ref[...].astype(F32)
    group = lax.broadcasted_iota(jnp.int32, (BLOCK, LANES), 1) // OWN
    at = pl.multiple_of(step * BLOCK, BLOCK)
    for q in range(TILES):
        tile = jnp.zeros((BLOCK, LANES), F32)
        for t in range(GROUPS):
            rows = wide[pl.ds(q * GROUPS + t, BLOCK, stride=BLOCK), :]
            if t > 0:
                rows = pltpu.roll(rows, t * OWN, 1)
            tile = jnp.where(group == (shift + t) % GROUPS, rows, tile)
        tile = pltpu.roll(tile, (GROUPS - shift) % GROUPS * OWN, 1).astype(BF16)
        signal[pl.ds(at, BLOCK), q * LANES : (q + 1) * LANES] = tile
        signal[pl.ds(at + ROWS, BLOCK), q * LANES : (q + 1) * LANES] = tile

    @pl.when(step == pl.num_programs(0) - 1)
    def _():
        forward_transform(signal, ahead, fine, coarse, turn_rows, stage, parts)
        result[...] = table_dot(parts[:, 0:256], parts[:, 256:512], forward)
        send = pltpu.make_async_copy(result, out_ref.at[0 : TILES * ROWS], sent)
        send.start()
        send.wait()


def whole_spec(shape):
    return pl.BlockSpec(shape, lambda *_: (0,) * len(shape))


def filter_transform(place, long_filter, ahead, fine, coarse, turn_rows, forward):
    chunk = BLOCK * BLOCK
    consts = (ahead, fine, coarse, turn_rows, forward)
    return pl.pallas_call(
        filter_kernel,
        out_shape=jax.ShapeDtypeStruct((HELD * TILES * ROWS, 2 * LANES), F32),
        grid_spec=pltpu.PrefetchScalarGridSpec(
            num_scalar_prefetch=1,
            grid=(LENGTH // chunk,),
            in_specs=[pl.BlockSpec((chunk, LANES), lambda g, s: (g, s[0]))] + [whole_spec(c.shape) for c in consts],
            out_specs=pl.BlockSpec(memory_space=pl.ANY),
            scratch_shapes=[
                pltpu.VMEM((chunk, LANES), F32),
                pltpu.VMEM((2 * ROWS, TILES * LANES), BF16),
                pltpu.VMEM((2 * ROWS, TILES * LANES), F32),
                pltpu.VMEM((TILES * ROWS, 4 * LANES), BF16),
                pltpu.VMEM((TILES * ROWS, 2 * LANES), F32),
                pltpu.SemaphoreType.DMA,
            ],
        ),
        cost_estimate=pl.CostEstimate(flops=2_000_000_000, bytes_accessed=6_000_000, transcendentals=0),
        compiler_params=pltpu.CompilerParams(vmem_limit_bytes=58 * 2**20),
        name="filter_transform",
    )(place, long_filter, *consts)


def conv_kernel(
    packed, bands, skip, gain_ref, ahead, back, fine, coarse, turn_rows, forward, inverse, out_ref,
    wide, signal, query, stage, parts, product, result, gain, arrived,
):
    fetch = pltpu.make_async_copy(gain_ref.at[0 : TILES * ROWS], gain, arrived)
    fetch.start()
    wide[0:MESSAGE_PAD] = jnp.zeros((MESSAGE_PAD, LANES), F32)
    wide[MESSAGE_PAD:] = packed[...].astype(F32).reshape(DEVICES * MESSAGE, LANES)

    def rows_of(stream, q):
        at = MESSAGE_PAD + stream * TILES + q
        if q < 0:
            at += TILES - MESSAGE
        return wide[pl.ds(at, DEVICES, stride=MESSAGE), :].astype(BF16)

    for q in range(TILES):
        lanes = slice(q * LANES, (q + 1) * LANES)
        sums = []
        for stream in range(STREAMS):
            both = jnp.concatenate([rows_of(stream, q - 1), rows_of(stream, q)], axis=1)
            halves_of = dot(both, bands[(stream + 1) % STREAMS])
            sums.append(halves_of[:, 0:LANES] + halves_of[:, LANES:])
        query[:, lanes] = sums[2]
        gated = (sums[0] * sums[1]).astype(BF16)
        signal[0:ROWS, lanes] = gated
        signal[ROWS:, lanes] = gated
    forward_transform(signal, ahead, fine, coarse, turn_rows, stage, parts)
    fetch.wait()
    for k in range(TILES):
        rows = slice(k * ROWS, (k + 1) * ROWS)
        mid = table_dot(parts[rows, 0:256], parts[rows, 256:512], forward)
        a, b = mid[:, 0:LANES], mid[:, LANES:]
        c, d = gain[rows, 0:LANES], gain[rows, LANES:]
        re_upper, re_lower = split(a * c - b * d)
        im_upper, im_lower = split(a * d + b * c)
        upper = jnp.concatenate([re_upper, im_upper], axis=1)
        lower = jnp.concatenate([re_lower, im_lower], axis=1)
        product[rows] = table_dot(upper, lower, inverse)

    def unspin(step, carry):
        at = pl.multiple_of(step * 16, 16)
        spins = spin_rows(fine, coarse, step)
        real, imag = [], []
        for k in range(TILES):
            rows = pl.ds(at + k * ROWS, 16)
            a, b = product[rows, 0:128], product[rows, 128:256]
            if k > 0:
                c, d = turn_rows[k : k + 1], turn_rows[TILES + k : TILES + k + 1]
                a, b = a * c + b * d, b * c - a * d
            real.append(a)
            imag.append(b)
        er, ei = real[0] + real[2], imag[0] + imag[2]
        fr, fi = real[0] - real[2], imag[0] - imag[2]
        gr, gi = real[1] + real[3], imag[1] + imag[3]
        hr, hi = real[1] - real[3], imag[1] - imag[3]
        outs = ((er + gr, ei + gi), (fr - hi, fi + hr), (er - gr, ei - gi), (fr + hi, fi - hr))
        for q, (a, b) in enumerate(outs):
            lanes = slice(q * LANES, (q + 1) * LANES)
            c, d = spins[q]
            parts[pl.ds(at, 16), lanes], parts[pl.ds(at + 2 * ROWS, 16), lanes] = split(a * c + b * d)
            parts[pl.ds(at + ROWS, 16), lanes], parts[pl.ds(at + 3 * ROWS, 16), lanes] = split(b * c - a * d)
        return carry

    lax.fori_loop(0, ROWS // 16, unspin, 0, unroll=2)
    for q in range(TILES):
        lanes = slice(q * LANES, (q + 1) * LANES)
        upper, lower = parts[0:512, lanes], parts[512:1024, lanes]
        long_part = dot(back[:, 0:512], upper) + dot(back[:, 0:512], lower) + dot(back[:, 512:1024], upper)
        total = query[:, lanes] * (long_part + skip[...] * signal[0:ROWS, lanes].astype(F32))
        result[pl.ds(q, ROWS, stride=TILES), :] = total
    out_ref[...] = result[...].reshape(DEVICES // 2, 2 * TILES, LANES).astype(BF16)


def convolve(packed, bands, skip, gain, ahead, back, fine, coarse, turn_rows, forward, inverse):
    return pl.pallas_call(
        conv_kernel,
        out_shape=jax.ShapeDtypeStruct((DEVICES // 2, 2 * TILES, LANES), BF16),
        in_specs=[VMEM] * 3 + [pl.BlockSpec(memory_space=pl.ANY)] + [VMEM] * 7,
        out_specs=VMEM,
        scratch_shapes=[
            pltpu.VMEM((MESSAGE_PAD + DEVICES * MESSAGE, LANES), F32),
            pltpu.VMEM((2 * ROWS, TILES * LANES), BF16),
            pltpu.VMEM((ROWS, TILES * LANES), F32),
            pltpu.VMEM((2 * ROWS, TILES * LANES), F32),
            pltpu.VMEM((TILES * ROWS, 4 * LANES), BF16),
            pltpu.VMEM((TILES * ROWS, 2 * LANES), F32),
            pltpu.VMEM((DEVICES * TILES, LANES), F32),
            pltpu.VMEM((TILES * ROWS, 2 * LANES), F32),
            pltpu.SemaphoreType.DMA,
        ],
        cost_estimate=pl.CostEstimate(flops=4_000_000_000, bytes_accessed=6_000_000, transcendentals=0),
        compiler_params=pltpu.CompilerParams(vmem_limit_bytes=24 * 2**20),
        name="convolve",
    )(packed, bands, skip, gain, ahead, back, fine, coarse, turn_rows, forward, inverse)


def unpack_kernel(mixed_ref, out_ref, after):
    for half in range(2):
        came = [[mixed_ref[half, d, pair].astype(F32) for d in range(GROUPS)] for pair in range(CH // 2)]
        done = [exchange(tiles) for tiles in came]
        for pair, tiles in enumerate(done):
            for t in range(GROUPS):
                after[half, pair, pl.ds(t, 8, stride=GROUPS), :] = tiles[t]
    for j in range(CH):
        for half in range(2):
            lanes = slice((2 * j + half) * LANES, (2 * j + half + 1) * LANES)
            out_ref[:, lanes] = after[half, j // 2, j % 2 * BLOCK : (j % 2 + 1) * BLOCK].astype(BF16)


def unpack(mixed):
    return pl.pallas_call(
        unpack_kernel,
        out_shape=jax.ShapeDtypeStruct((BLOCK, WIDTH), BF16),
        in_specs=[VMEM],
        out_specs=VMEM,
        scratch_shapes=[pltpu.VMEM((2, CH // 2, 2 * BLOCK, LANES), F32)],
        cost_estimate=pl.CostEstimate(flops=4_000_000, bytes_accessed=500_000, transcendentals=0),
        compiler_params=pltpu.CompilerParams(vmem_limit_bytes=8 * 2**20),
        name="unpack",
    )(mixed)


def band_kernel(taps, out_ref):
    for at in range(0, 2 * LANES, 64):
        row = lax.broadcasted_iota(jnp.int32, (64, LANES), 0) + at
        lane = lax.broadcasted_iota(jnp.int32, (64, LANES), 1)
        lag = (lane >> 4) - ((row & LANES - 1) >> 4) + jnp.where(row < LANES, GROUPS, 0)
        lag = jnp.where(((row ^ lane) & OWN - 1) == 0, lag, -1)
        for stream in range(STREAMS):
            band = jnp.zeros((64, LANES), F32)
            for r in range(SHORT):
                band = jnp.where(lag == r, taps[STREAMS * r + stream : STREAMS * r + stream + 1], band)
            out_ref[stream, at : at + 64, 0:LANES], out_ref[stream, at : at + 64, LANES:] = split(band)


def short_bands(taps):
    return pl.pallas_call(
        band_kernel,
        out_shape=jax.ShapeDtypeStruct((STREAMS, 2 * LANES, 2 * LANES), BF16),
        in_specs=[VMEM],
        out_specs=VMEM,
        cost_estimate=pl.CostEstimate(flops=2_000_000, bytes_accessed=500_000, transcendentals=0),
        compiler_params=pltpu.CompilerParams(vmem_limit_bytes=8 * 2**20),
        name="short_bands",
    )(taps)


def own_rows(short_weight, row):
    count = STREAMS * SHORT
    taps = lax.dynamic_slice(short_weight, (0, 0, row * OWN), (SHORT, STREAMS, OWN)).reshape(count, OWN)
    return jnp.tile(jnp.pad(taps, ((0, -count % 8), (0, 0))), (1, GROUPS))


def local(inputs, short_weight, long_filter, skip_gain):
    row = lax.axis_index("ctx")
    ahead, back, fine, coarse, turn_rows, forward, inverse = (jnp.asarray(t) for t in tables())
    packed = pack(jnp.transpose(inputs, (1, 0, 2))).reshape(DEVICES, STREAMS, TILES, LANES)
    packed = lax.all_to_all(packed, ("ctx", "ch"), 0, 0, tiled=True)
    packed = packed.reshape(DEVICES * MESSAGE // 8, 8, LANES)
    place = jnp.stack([row // GROUPS, row % GROUPS]).astype(jnp.int32)
    gain = filter_transform(place, long_filter, ahead, fine, coarse, turn_rows, forward)
    bands = short_bands(own_rows(short_weight, row))
    skip = jnp.tile(lax.dynamic_slice(skip_gain, (row * OWN,), (OWN,)), GROUPS).reshape(1, LANES)
    mixed = convolve(packed, bands, skip, gain, ahead, back, fine, coarse, turn_rows, forward, inverse)
    mixed = lax.all_to_all(mixed.reshape(DEVICES, TILES, LANES), ("ctx", "ch"), 0, 0, tiled=True)
    return unpack(mixed.reshape(2, GROUPS, CH // 2, 2 * TILES, LANES))


def solution(mesh):
    in_specs = (P(("ctx", "ch"), None, None), P(None, None, "ch"), P(None, "ch"), P("ch"))
    out_specs = P(("ctx", "ch"), None)
    return jax.shard_map(local, mesh=mesh, in_specs=in_specs, out_specs=out_specs, check_vma=False)
```

```python
import functools
import math

import jax
import jax.numpy as jnp
import ml_dtypes
import numpy as np
from jax import lax
from jax.experimental import pallas as pl
from jax.experimental.pallas import tpu as pltpu
from jax.sharding import PartitionSpec as P

SHORT = 7
STREAMS = 3
CTX = 16
CH = 16
DEVICES = CTX * CH
BLOCK = 32
LANES = 128
OWN = 16
GROUPS = LANES // OWN
TILES = BLOCK // GROUPS
LENGTH = DEVICES * BLOCK
WIDTH = DEVICES * OWN
HELD = 40
PAIRS = 2
MESSAGE = STREAMS * TILES
MESSAGE_PAD = 16
CHUNK = 16
ROWS = DEVICES
F32 = jnp.float32
VMEM = pl.BlockSpec(memory_space=pltpu.VMEM)
BF16 = jnp.bfloat16


def halves(table):
    upper = table.astype(ml_dtypes.bfloat16)
    lower = (table - upper.astype(np.float64)).astype(ml_dtypes.bfloat16)
    return upper, lower


@functools.lru_cache(maxsize=None)
def tables():
    turn = 2.0 * math.pi
    freq = (np.arange(ROWS) + 0.5) / (2 * ROWS)
    block = np.arange(ROWS)
    angle = turn * freq[:, None] * block[None, :]
    first = np.concatenate([np.cos(angle), -np.sin(angle)], axis=0)
    upper, lower = halves(first)
    ahead = np.concatenate([upper, lower], axis=1)

    last = np.concatenate([np.cos(angle), -np.sin(angle)], axis=0).T * (2.0 / (2 * LENGTH))
    upper, lower = halves(last)
    back = np.concatenate([upper, lower], axis=1)

    lane = np.arange(LANES)
    place = (np.arange(TILES)[:, None] * GROUPS + lane[None, :] // OWN).reshape(-1)
    fine = turn * freq[:CHUNK, None] * place[None, :] / BLOCK
    coarse = turn * (np.arange(ROWS // CHUNK) * CHUNK / (2 * ROWS))[:, None] * place[None, :] / BLOCK
    fine = np.concatenate([np.cos(fine), -np.sin(fine)], axis=1).astype(np.float32)
    coarse = np.concatenate([np.cos(coarse), -np.sin(coarse)], axis=1).astype(np.float32).reshape(-1, 2 * TILES, LANES)

    angle = turn * np.arange(TILES)[:, None] * (lane[None, :] // OWN) / BLOCK
    turn_rows = np.concatenate([np.cos(angle), -np.sin(angle)], axis=0).astype(np.float32)

    same = (lane[:, None] % OWN) == (lane[None, :] % OWN)
    angle = turn * (lane[:, None] // OWN) * (lane[None, :] // OWN) / GROUPS
    cosine = np.where(same, np.cos(angle), 0.0)
    sine = np.where(same, np.sin(angle), 0.0)
    forward = np.block([[cosine, -sine], [sine, cosine]])
    inverse = np.block([[cosine, sine], [-sine, cosine]])
    upper, lower = halves(forward)
    forward = np.concatenate([upper, lower], axis=0)
    upper, lower = halves(inverse)
    inverse = np.concatenate([upper, lower], axis=0)
    return ahead, back, fine, coarse, turn_rows, forward, inverse


def dot(left, right):
    return jnp.dot(left, right, preferred_element_type=F32)


def split(value):
    upper = value.astype(BF16)
    return upper, (value - upper.astype(F32)).astype(BF16)


def exchange(tiles):
    lane = lax.broadcasted_iota(jnp.int32, (GROUPS, LANES), 1)
    for step in (4, 2, 1):
        shift = step * OWN
        low = (lane & shift) == 0
        moved = list(tiles)
        for t in range(GROUPS):
            if t & step == 0:
                a, b = tiles[t], tiles[t + step]
                if step == 4:
                    across = pltpu.roll(jnp.where(low, b, a), shift, 1)
                    moved[t], moved[t + step] = jnp.where(low, a, across), jnp.where(low, across, b)
                else:
                    moved[t] = jnp.where(low, a, pltpu.roll(b, shift, 1))
                    moved[t + step] = jnp.where(low, pltpu.roll(a, LANES - shift, 1), b)
        tiles = moved
    return tiles


def half_lanes(j, half):
    return pl.ds(pl.multiple_of(j * 2 * LANES, LANES) + half * LANES, LANES)


def exchange_all(slots):
    before = [[slot[pl.ds(t, 8, stride=GROUPS), :] for t in range(GROUPS)] for slot in slots]
    return [exchange(tiles) for tiles in before]


def pack_kernel(streams, out_ref, held, slots, packed, arrived, sent):
    fetches = []
    for pair in range(CH // 2):
        lanes = slice(pair * 4 * LANES, (pair + 1) * 4 * LANES)
        fetches.append(pltpu.make_async_copy(streams.at[:, :, lanes], held.at[pair], arrived.at[pair]))
        fetches[-1].start()
    sends = []
    for first in range(0, CH // 2, PAIRS):
        here = [slots.at[first // PAIRS % 2, at] for at in range(6 * PAIRS)]
        for pair in range(first, first + PAIRS):
            fetches[pair].wait()
        for pair in range(first, first + PAIRS):
            for half in range(2):
                for at in range(6):
                    later, stream = divmod(at, 3)
                    tile = 2 * later + half
                    rows = held[pair, (stream + 1) % STREAMS, :, tile * LANES : (tile + 1) * LANES].astype(F32)
                    slot = here[((pair - first) * 2 + half) * 3 + at // 2]
                    slot[at % 2 * BLOCK : (at % 2 + 1) * BLOCK] = rows
        for at, tiles in enumerate(exchange_all(here)):
            which, third = divmod(at, 3)
            for d in range(GROUPS):
                packed[first + which // 2, which % 2, d, third] = tiles[d].astype(BF16)
        for pair in range(first, first + PAIRS):
            sends.append(pltpu.make_async_copy(packed.at[pair], out_ref.at[:, :, pair], sent.at[pair]))
            sends[-1].start()
    for send in sends:
        send.wait()


def pack(streams):
    pairs = CH // 2
    return pl.pallas_call(
        pack_kernel,
        out_shape=jax.ShapeDtypeStruct((2, GROUPS, pairs, 3, 8, LANES), BF16),
        in_specs=[pl.BlockSpec(memory_space=pl.ANY)],
        out_specs=pl.BlockSpec(memory_space=pl.ANY),
        scratch_shapes=[
            pltpu.VMEM((pairs, STREAMS, BLOCK, 4 * LANES), BF16),
            pltpu.VMEM((2, 6 * PAIRS, 2 * BLOCK, LANES), F32),
            pltpu.VMEM((pairs, 2, GROUPS, 3, 8, LANES), BF16),
            pltpu.SemaphoreType.DMA((pairs,)),
            pltpu.SemaphoreType.DMA((pairs,)),
        ],
        cost_estimate=pl.CostEstimate(flops=4_000_000, bytes_accessed=1_600_000, transcendentals=0),
        compiler_params=pltpu.CompilerParams(vmem_limit_bytes=58 * 2**20),
        name="pack",
    )(streams)


def spin_rows(fine, coarse, step):
    rows = coarse[step]
    spins = []
    for q in range(TILES):
        re = slice(q * LANES, (q + 1) * LANES)
        im = slice((TILES + q) * LANES, (TILES + q + 1) * LANES)
        a, b = fine[:, re], fine[:, im]
        c, d = rows[q : q + 1], rows[TILES + q : TILES + q + 1]
        spins.append((a * c - b * d, a * d + b * c))
    return spins


def table_dot(upper, lower, table):
    return dot(upper, table[0:256]) + dot(lower, table[0:256]) + dot(upper, table[256:512])


def forward_transform(signal, ahead, fine, coarse, turn_rows, stage, parts):
    stage[...] = dot(ahead[...], signal[...])

    def rows(step, carry):
        at = pl.multiple_of(step * 16, 16)
        here, below = pl.ds(at, 16), pl.ds(at + ROWS, 16)
        spins = spin_rows(fine, coarse, step)
        real, imag = [], []
        for q in range(TILES):
            lanes = slice(q * LANES, (q + 1) * LANES)
            a, b = stage[here, lanes], stage[below, lanes]
            c, d = spins[q]
            real.append(a * c - b * d)
            imag.append(a * d + b * c)
        er, ei = real[0] + real[2], imag[0] + imag[2]
        fr, fi = real[0] - real[2], imag[0] - imag[2]
        gr, gi = real[1] + real[3], imag[1] + imag[3]
        hr, hi = real[1] - real[3], imag[1] - imag[3]
        outs = ((er + gr, ei + gi), (fr + hi, fi - hr), (er - gr, ei - gi), (fr - hi, fi + hr))
        for k, (a, b) in enumerate(outs):
            if k > 0:
                c, d = turn_rows[k : k + 1], turn_rows[TILES + k : TILES + k + 1]
                a, b = a * c - b * d, a * d + b * c
            to = pl.ds(at + k * ROWS, 16)
            parts[to, 0:128], parts[to, 256:384] = split(a)
            parts[to, 128:256], parts[to, 384:512] = split(b)
        return carry

    lax.fori_loop(0, ROWS // 16, rows, 0, unroll=True)


def filter_kernel(place, filter_ref, ahead, fine, coarse, turn_rows, forward, out_ref, wide, signal, stage, parts, result, sent):
    step = pl.program_id(0)
    shift = place[1]
    wide[...] = filter_ref[...].astype(F32)
    group = lax.broadcasted_iota(jnp.int32, (BLOCK, LANES), 1) // OWN
    at = pl.multiple_of(step * BLOCK, BLOCK)
    for q in range(TILES):
        tile = jnp.zeros((BLOCK, LANES), F32)
        for t in range(GROUPS):
            rows = wide[pl.ds(q * GROUPS + t, BLOCK, stride=BLOCK), :]
            if t > 0:
                rows = pltpu.roll(rows, t * OWN, 1)
            tile = jnp.where(group == (shift + t) % GROUPS, rows, tile)
        tile = pltpu.roll(tile, (GROUPS - shift) % GROUPS * OWN, 1).astype(BF16)
        signal[pl.ds(at, BLOCK), q * LANES : (q + 1) * LANES] = tile
        signal[pl.ds(at + ROWS, BLOCK), q * LANES : (q + 1) * LANES] = tile

    @pl.when(step == pl.num_programs(0) - 1)
    def _():
        forward_transform(signal, ahead, fine, coarse, turn_rows, stage, parts)
        result[...] = table_dot(parts[:, 0:256], parts[:, 256:512], forward)
        send = pltpu.make_async_copy(result, out_ref.at[0 : TILES * ROWS], sent)
        send.start()
        send.wait()


def whole_spec(shape):
    return pl.BlockSpec(shape, lambda *_: (0,) * len(shape))


def filter_transform(place, long_filter, ahead, fine, coarse, turn_rows, forward):
    chunk = BLOCK * BLOCK
    consts = (ahead, fine, coarse, turn_rows, forward)
    return pl.pallas_call(
        filter_kernel,
        out_shape=jax.ShapeDtypeStruct((HELD * TILES * ROWS, 2 * LANES), F32),
        grid_spec=pltpu.PrefetchScalarGridSpec(
            num_scalar_prefetch=1,
            grid=(LENGTH // chunk,),
            in_specs=[pl.BlockSpec((chunk, LANES), lambda g, s: (g, s[0]))] + [whole_spec(c.shape) for c in consts],
            out_specs=pl.BlockSpec(memory_space=pl.ANY),
            scratch_shapes=[
                pltpu.VMEM((chunk, LANES), F32),
                pltpu.VMEM((2 * ROWS, TILES * LANES), BF16),
                pltpu.VMEM((2 * ROWS, TILES * LANES), F32),
                pltpu.VMEM((TILES * ROWS, 4 * LANES), BF16),
                pltpu.VMEM((TILES * ROWS, 2 * LANES), F32),
                pltpu.SemaphoreType.DMA,
            ],
        ),
        cost_estimate=pl.CostEstimate(flops=2_000_000_000, bytes_accessed=6_000_000, transcendentals=0),
        compiler_params=pltpu.CompilerParams(vmem_limit_bytes=58 * 2**20),
        name="filter_transform",
    )(place, long_filter, *consts)


def conv_kernel(
    packed, bands, skip, gain_ref, ahead, back, fine, coarse, turn_rows, forward, inverse, out_ref,
    wide, signal, query, stage, parts, product, result, gain, arrived,
):
    fetch = pltpu.make_async_copy(gain_ref.at[0 : TILES * ROWS], gain, arrived)
    fetch.start()
    wide[0:MESSAGE_PAD] = jnp.zeros((MESSAGE_PAD, LANES), F32)
    wide[MESSAGE_PAD:] = packed[...].astype(F32).reshape(DEVICES * MESSAGE, LANES)

    def rows_of(stream, q):
        at = MESSAGE_PAD + stream * TILES + q
        if q < 0:
            at += TILES - MESSAGE
        return wide[pl.ds(at, DEVICES, stride=MESSAGE), :].astype(BF16)

    for q in range(TILES):
        lanes = slice(q * LANES, (q + 1) * LANES)
        sums = []
        for stream in range(STREAMS):
            both = jnp.concatenate([rows_of(stream, q - 1), rows_of(stream, q)], axis=1)
            halves_of = dot(both, bands[(stream + 1) % STREAMS])
            sums.append(halves_of[:, 0:LANES] + halves_of[:, LANES:])
        query[:, lanes] = sums[2]
        gated = (sums[0] * sums[1]).astype(BF16)
        signal[0:ROWS, lanes] = gated
        signal[ROWS:, lanes] = gated
    forward_transform(signal, ahead, fine, coarse, turn_rows, stage, parts)
    fetch.wait()
    for k in range(TILES):
        rows = slice(k * ROWS, (k + 1) * ROWS)
        mid = table_dot(parts[rows, 0:256], parts[rows, 256:512], forward)
        a, b = mid[:, 0:LANES], mid[:, LANES:]
        c, d = gain[rows, 0:LANES], gain[rows, LANES:]
        re_upper, re_lower = split(a * c - b * d)
        im_upper, im_lower = split(a * d + b * c)
        upper = jnp.concatenate([re_upper, im_upper], axis=1)
        lower = jnp.concatenate([re_lower, im_lower], axis=1)
        product[rows] = table_dot(upper, lower, inverse)

    def unspin(step, carry):
        at = pl.multiple_of(step * 16, 16)
        spins = spin_rows(fine, coarse, step)
        real, imag = [], []
        for k in range(TILES):
            rows = pl.ds(at + k * ROWS, 16)
            a, b = product[rows, 0:128], product[rows, 128:256]
            if k > 0:
                c, d = turn_rows[k : k + 1], turn_rows[TILES + k : TILES + k + 1]
                a, b = a * c + b * d, b * c - a * d
            real.append(a)
            imag.append(b)
        er, ei = real[0] + real[2], imag[0] + imag[2]
        fr, fi = real[0] - real[2], imag[0] - imag[2]
        gr, gi = real[1] + real[3], imag[1] + imag[3]
        hr, hi = real[1] - real[3], imag[1] - imag[3]
        outs = ((er + gr, ei + gi), (fr - hi, fi + hr), (er - gr, ei - gi), (fr + hi, fi - hr))
        for q, (a, b) in enumerate(outs):
            lanes = slice(q * LANES, (q + 1) * LANES)
            c, d = spins[q]
            parts[pl.ds(at, 16), lanes], parts[pl.ds(at + 2 * ROWS, 16), lanes] = split(a * c + b * d)
            parts[pl.ds(at + ROWS, 16), lanes], parts[pl.ds(at + 3 * ROWS, 16), lanes] = split(b * c - a * d)
        return carry

    lax.fori_loop(0, ROWS // 16, unspin, 0, unroll=True)
    for q in range(TILES):
        lanes = slice(q * LANES, (q + 1) * LANES)
        upper, lower = parts[0:512, lanes], parts[512:1024, lanes]
        long_part = dot(back[:, 0:512], upper) + dot(back[:, 0:512], lower) + dot(back[:, 512:1024], upper)
        total = query[:, lanes] * (long_part + skip[...] * signal[0:ROWS, lanes].astype(F32))
        result[pl.ds(q, ROWS, stride=TILES), :] = total
    out_ref[...] = result[...].reshape(DEVICES // 2, 2 * TILES, LANES).astype(BF16)


def convolve(packed, bands, skip, gain, ahead, back, fine, coarse, turn_rows, forward, inverse):
    return pl.pallas_call(
        conv_kernel,
        out_shape=jax.ShapeDtypeStruct((DEVICES // 2, 2 * TILES, LANES), BF16),
        in_specs=[VMEM] * 3 + [pl.BlockSpec(memory_space=pl.ANY)] + [VMEM] * 7,
        out_specs=VMEM,
        scratch_shapes=[
            pltpu.VMEM((MESSAGE_PAD + DEVICES * MESSAGE, LANES), F32),
            pltpu.VMEM((2 * ROWS, TILES * LANES), BF16),
            pltpu.VMEM((ROWS, TILES * LANES), F32),
            pltpu.VMEM((2 * ROWS, TILES * LANES), F32),
            pltpu.VMEM((TILES * ROWS, 4 * LANES), BF16),
            pltpu.VMEM((TILES * ROWS, 2 * LANES), F32),
            pltpu.VMEM((DEVICES * TILES, LANES), F32),
            pltpu.VMEM((TILES * ROWS, 2 * LANES), F32),
            pltpu.SemaphoreType.DMA,
        ],
        cost_estimate=pl.CostEstimate(flops=4_000_000_000, bytes_accessed=6_000_000, transcendentals=0),
        compiler_params=pltpu.CompilerParams(vmem_limit_bytes=24 * 2**20),
        name="convolve",
    )(packed, bands, skip, gain, ahead, back, fine, coarse, turn_rows, forward, inverse)


def unpack_kernel(mixed_ref, out_ref, after):
    for half in range(2):
        came = [[mixed_ref[half, d, pair].astype(F32) for d in range(GROUPS)] for pair in range(CH // 2)]
        done = [exchange(tiles) for tiles in came]
        for pair, tiles in enumerate(done):
            for t in range(GROUPS):
                after[half, pair, pl.ds(t, 8, stride=GROUPS), :] = tiles[t]
    for j in range(CH):
        for half in range(2):
            lanes = slice((2 * j + half) * LANES, (2 * j + half + 1) * LANES)
            out_ref[:, lanes] = after[half, j // 2, j % 2 * BLOCK : (j % 2 + 1) * BLOCK].astype(BF16)


def unpack(mixed):
    return pl.pallas_call(
        unpack_kernel,
        out_shape=jax.ShapeDtypeStruct((BLOCK, WIDTH), BF16),
        in_specs=[VMEM],
        out_specs=VMEM,
        scratch_shapes=[pltpu.VMEM((2, CH // 2, 2 * BLOCK, LANES), F32)],
        cost_estimate=pl.CostEstimate(flops=4_000_000, bytes_accessed=500_000, transcendentals=0),
        compiler_params=pltpu.CompilerParams(vmem_limit_bytes=8 * 2**20),
        name="unpack",
    )(mixed)


def band_kernel(taps, out_ref):
    for at in range(0, 2 * LANES, 64):
        row = lax.broadcasted_iota(jnp.int32, (64, LANES), 0) + at
        lane = lax.broadcasted_iota(jnp.int32, (64, LANES), 1)
        lag = (lane >> 4) - ((row & LANES - 1) >> 4) + jnp.where(row < LANES, GROUPS, 0)
        lag = jnp.where(((row ^ lane) & OWN - 1) == 0, lag, -1)
        for stream in range(STREAMS):
            band = jnp.zeros((64, LANES), F32)
            for r in range(SHORT):
                band = jnp.where(lag == r, taps[STREAMS * r + stream : STREAMS * r + stream + 1], band)
            out_ref[stream, at : at + 64, 0:LANES], out_ref[stream, at : at + 64, LANES:] = split(band)


def short_bands(taps):
    return pl.pallas_call(
        band_kernel,
        out_shape=jax.ShapeDtypeStruct((STREAMS, 2 * LANES, 2 * LANES), BF16),
        in_specs=[VMEM],
        out_specs=VMEM,
        cost_estimate=pl.CostEstimate(flops=2_000_000, bytes_accessed=500_000, transcendentals=0),
        compiler_params=pltpu.CompilerParams(vmem_limit_bytes=8 * 2**20),
        name="short_bands",
    )(taps)


def own_rows(short_weight, row):
    count = STREAMS * SHORT
    taps = lax.dynamic_slice(short_weight, (0, 0, row * OWN), (SHORT, STREAMS, OWN)).reshape(count, OWN)
    return jnp.tile(jnp.pad(taps, ((0, -count % 8), (0, 0))), (1, GROUPS))


def local(inputs, short_weight, long_filter, skip_gain):
    row = lax.axis_index("ctx")
    ahead, back, fine, coarse, turn_rows, forward, inverse = (jnp.asarray(t) for t in tables())
    packed = pack(jnp.transpose(inputs, (1, 0, 2))).reshape(DEVICES, STREAMS, TILES, LANES)
    packed = lax.all_to_all(packed, ("ctx", "ch"), 0, 0, tiled=True)
    packed = packed.reshape(DEVICES * MESSAGE // 8, 8, LANES)
    place = jnp.stack([row // GROUPS, row % GROUPS]).astype(jnp.int32)
    gain = filter_transform(place, long_filter, ahead, fine, coarse, turn_rows, forward)
    bands = short_bands(own_rows(short_weight, row))
    skip = jnp.tile(lax.dynamic_slice(skip_gain, (row * OWN,), (OWN,)), GROUPS).reshape(1, LANES)
    mixed = convolve(packed, bands, skip, gain, ahead, back, fine, coarse, turn_rows, forward, inverse)
    mixed = lax.all_to_all(mixed.reshape(DEVICES, TILES, LANES), ("ctx", "ch"), 0, 0, tiled=True)
    return unpack(mixed.reshape(2, GROUPS, CH // 2, 2 * TILES, LANES))


def solution(mesh):
    in_specs = (P(("ctx", "ch"), None, None), P(None, None, "ch"), P(None, "ch"), P("ch"))
    out_specs = P(("ctx", "ch"), None)
    return jax.shard_map(local, mesh=mesh, in_specs=in_specs, out_specs=out_specs, check_vma=False)
```

```python
import functools
import math

import jax
import jax.numpy as jnp
import ml_dtypes
import numpy as np
from jax import lax
from jax.experimental import pallas as pl
from jax.experimental.pallas import tpu as pltpu
from jax.sharding import PartitionSpec as P

SHORT = 7
STREAMS = 3
CTX = 16
CH = 16
DEVICES = CTX * CH
BLOCK = 32
LANES = 128
OWN = 16
GROUPS = LANES // OWN
TILES = BLOCK // GROUPS
LENGTH = DEVICES * BLOCK
WIDTH = DEVICES * OWN
HELD = 40
PAIRS = 2
MESSAGE = STREAMS * TILES
MESSAGE_PAD = 16
CHUNK = 16
ROWS = DEVICES
F32 = jnp.float32
VMEM = pl.BlockSpec(memory_space=pltpu.VMEM)
BF16 = jnp.bfloat16


def halves(table):
    upper = table.astype(ml_dtypes.bfloat16)
    lower = (table - upper.astype(np.float64)).astype(ml_dtypes.bfloat16)
    return upper, lower


@functools.lru_cache(maxsize=None)
def tables():
    turn = 2.0 * math.pi
    freq = (np.arange(ROWS) + 0.5) / (2 * ROWS)
    block = np.arange(ROWS)
    angle = turn * freq[:, None] * block[None, :]
    first = np.concatenate([np.cos(angle), -np.sin(angle)], axis=0)
    upper, lower = halves(first)
    ahead = np.concatenate([upper, lower], axis=1)

    last = np.concatenate([np.cos(angle), -np.sin(angle)], axis=0).T * (2.0 / (2 * LENGTH))
    upper, lower = halves(last)
    back = np.concatenate([upper, lower], axis=1)

    lane = np.arange(LANES)
    place = (np.arange(TILES)[:, None] * GROUPS + lane[None, :] // OWN).reshape(-1)
    fine = turn * freq[:CHUNK, None] * place[None, :] / BLOCK
    coarse = turn * (np.arange(ROWS // CHUNK) * CHUNK / (2 * ROWS))[:, None] * place[None, :] / BLOCK
    fine = np.concatenate([np.cos(fine), -np.sin(fine)], axis=1).astype(np.float32)
    coarse = np.concatenate([np.cos(coarse), -np.sin(coarse)], axis=1).astype(np.float32).reshape(-1, 2 * TILES, LANES)

    angle = turn * np.arange(TILES)[:, None] * (lane[None, :] // OWN) / BLOCK
    turn_rows = np.concatenate([np.cos(angle), -np.sin(angle)], axis=0).astype(np.float32)

    same = (lane[:, None] % OWN) == (lane[None, :] % OWN)
    angle = turn * (lane[:, None] // OWN) * (lane[None, :] // OWN) / GROUPS
    cosine = np.where(same, np.cos(angle), 0.0)
    sine = np.where(same, np.sin(angle), 0.0)
    forward = np.block([[cosine, -sine], [sine, cosine]])
    inverse = np.block([[cosine, sine], [-sine, cosine]])
    upper, lower = halves(forward)
    forward = np.concatenate([upper, lower], axis=0)
    upper, lower = halves(inverse)
    inverse = np.concatenate([upper, lower], axis=0)
    return ahead, back, fine, coarse, turn_rows, forward, inverse


def dot(left, right):
    return jnp.dot(left, right, preferred_element_type=F32)


def split(value):
    upper = value.astype(BF16)
    return upper, (value - upper.astype(F32)).astype(BF16)


def exchange(tiles):
    lane = lax.broadcasted_iota(jnp.int32, (GROUPS, LANES), 1)
    for step in (4, 2, 1):
        shift = step * OWN
        low = (lane & shift) == 0
        moved = list(tiles)
        for t in range(GROUPS):
            if t & step == 0:
                a, b = tiles[t], tiles[t + step]
                if step == 4:
                    across = pltpu.roll(jnp.where(low, b, a), shift, 1)
                    moved[t], moved[t + step] = jnp.where(low, a, across), jnp.where(low, across, b)
                else:
                    moved[t] = jnp.where(low, a, pltpu.roll(b, shift, 1))
                    moved[t + step] = jnp.where(low, pltpu.roll(a, LANES - shift, 1), b)
        tiles = moved
    return tiles


def half_lanes(j, half):
    return pl.ds(pl.multiple_of(j * 2 * LANES, LANES) + half * LANES, LANES)


def exchange_all(slots):
    before = [[slot[pl.ds(t, 8, stride=GROUPS), :] for t in range(GROUPS)] for slot in slots]
    return [exchange(tiles) for tiles in before]


def pack_kernel(streams, out_ref, held, slots, packed, arrived, sent):
    fetches = []
    for pair in range(CH // 2):
        lanes = slice(pair * 4 * LANES, (pair + 1) * 4 * LANES)
        fetches.append(pltpu.make_async_copy(streams.at[:, :, lanes], held.at[pair], arrived.at[pair]))
        fetches[-1].start()
    sends = []
    for first in range(0, CH // 2, PAIRS):
        here = [slots.at[first // PAIRS % 2, at] for at in range(6 * PAIRS)]
        for pair in range(first, first + PAIRS):
            fetches[pair].wait()
        for pair in range(first, first + PAIRS):
            for half in range(2):
                for at in range(6):
                    later, stream = divmod(at, 3)
                    tile = 2 * later + half
                    rows = held[pair, (stream + 1) % STREAMS, :, tile * LANES : (tile + 1) * LANES].astype(F32)
                    slot = here[((pair - first) * 2 + half) * 3 + at // 2]
                    slot[at % 2 * BLOCK : (at % 2 + 1) * BLOCK] = rows
        for at, tiles in enumerate(exchange_all(here)):
            which, third = divmod(at, 3)
            for d in range(GROUPS):
                packed[first + which // 2, which % 2, d, third] = tiles[d].astype(BF16)
        for pair in range(first, first + PAIRS):
            sends.append(pltpu.make_async_copy(packed.at[pair], out_ref.at[:, :, pair], sent.at[pair]))
            sends[-1].start()
    for send in sends:
        send.wait()


def pack(streams):
    pairs = CH // 2
    return pl.pallas_call(
        pack_kernel,
        out_shape=jax.ShapeDtypeStruct((2, GROUPS, pairs, 3, 8, LANES), BF16),
        in_specs=[pl.BlockSpec(memory_space=pl.ANY)],
        out_specs=pl.BlockSpec(memory_space=pl.ANY),
        scratch_shapes=[
            pltpu.VMEM((pairs, STREAMS, BLOCK, 4 * LANES), BF16),
            pltpu.VMEM((2, 6 * PAIRS, 2 * BLOCK, LANES), F32),
            pltpu.VMEM((pairs, 2, GROUPS, 3, 8, LANES), BF16),
            pltpu.SemaphoreType.DMA((pairs,)),
            pltpu.SemaphoreType.DMA((pairs,)),
        ],
        cost_estimate=pl.CostEstimate(flops=4_000_000, bytes_accessed=1_600_000, transcendentals=0),
        compiler_params=pltpu.CompilerParams(vmem_limit_bytes=58 * 2**20),
        name="pack",
    )(streams)


def spin_rows(fine, coarse, step):
    rows = coarse[step]
    spins = []
    for q in range(TILES):
        re = slice(q * LANES, (q + 1) * LANES)
        im = slice((TILES + q) * LANES, (TILES + q + 1) * LANES)
        a, b = fine[:, re], fine[:, im]
        c, d = rows[q : q + 1], rows[TILES + q : TILES + q + 1]
        spins.append((a * c - b * d, a * d + b * c))
    return spins


def table_dot(upper, lower, table):
    return dot(upper, table[0:256]) + dot(lower, table[0:256]) + dot(upper, table[256:512])


def forward_transform(signal, ahead, fine, coarse, turn_rows, stage, parts):
    stage[...] = dot(ahead[...], signal[...])

    def rows(step, carry):
        at = pl.multiple_of(step * 16, 16)
        here, below = pl.ds(at, 16), pl.ds(at + ROWS, 16)
        spins = spin_rows(fine, coarse, step)
        real, imag = [], []
        for q in range(TILES):
            lanes = slice(q * LANES, (q + 1) * LANES)
            a, b = stage[here, lanes], stage[below, lanes]
            c, d = spins[q]
            real.append(a * c - b * d)
            imag.append(a * d + b * c)
        er, ei = real[0] + real[2], imag[0] + imag[2]
        fr, fi = real[0] - real[2], imag[0] - imag[2]
        gr, gi = real[1] + real[3], imag[1] + imag[3]
        hr, hi = real[1] - real[3], imag[1] - imag[3]
        outs = ((er + gr, ei + gi), (fr + hi, fi - hr), (er - gr, ei - gi), (fr - hi, fi + hr))
        for k, (a, b) in enumerate(outs):
            if k > 0:
                c, d = turn_rows[k : k + 1], turn_rows[TILES + k : TILES + k + 1]
                a, b = a * c - b * d, a * d + b * c
            to = pl.ds(at + k * ROWS, 16)
            parts[to, 0:128], parts[to, 256:384] = split(a)
            parts[to, 128:256], parts[to, 384:512] = split(b)
        return carry

    lax.fori_loop(0, ROWS // 16, rows, 0, unroll=True)


def filter_kernel(place, filter_ref, ahead, fine, coarse, turn_rows, forward, out_ref, wide, signal, stage, parts, result, sent):
    step = pl.program_id(0)
    shift = place[1]
    wide[...] = filter_ref[...].astype(F32)
    group = lax.broadcasted_iota(jnp.int32, (BLOCK, LANES), 1) // OWN
    at = pl.multiple_of(step * BLOCK, BLOCK)
    for q in range(TILES):
        tile = jnp.zeros((BLOCK, LANES), F32)
        for t in range(GROUPS):
            rows = wide[pl.ds(q * GROUPS + t, BLOCK, stride=BLOCK), :]
            if t > 0:
                rows = pltpu.roll(rows, t * OWN, 1)
            tile = jnp.where(group == (shift + t) % GROUPS, rows, tile)
        tile = pltpu.roll(tile, (GROUPS - shift) % GROUPS * OWN, 1).astype(BF16)
        signal[pl.ds(at, BLOCK), q * LANES : (q + 1) * LANES] = tile
        signal[pl.ds(at + ROWS, BLOCK), q * LANES : (q + 1) * LANES] = tile

    @pl.when(step == pl.num_programs(0) - 1)
    def _():
        forward_transform(signal, ahead, fine, coarse, turn_rows, stage, parts)
        result[...] = table_dot(parts[:, 0:256], parts[:, 256:512], forward)
        send = pltpu.make_async_copy(result, out_ref.at[0 : TILES * ROWS], sent)
        send.start()
        send.wait()


def whole_spec(shape):
    return pl.BlockSpec(shape, lambda *_: (0,) * len(shape))


def filter_transform(place, long_filter, ahead, fine, coarse, turn_rows, forward):
    chunk = BLOCK * BLOCK
    consts = (ahead, fine, coarse, turn_rows, forward)
    return pl.pallas_call(
        filter_kernel,
        out_shape=jax.ShapeDtypeStruct((HELD * TILES * ROWS, 2 * LANES), F32),
        grid_spec=pltpu.PrefetchScalarGridSpec(
            num_scalar_prefetch=1,
            grid=(LENGTH // chunk,),
            in_specs=[pl.BlockSpec((chunk, LANES), lambda g, s: (g, s[0]))] + [whole_spec(c.shape) for c in consts],
            out_specs=pl.BlockSpec(memory_space=pl.ANY),
            scratch_shapes=[
                pltpu.VMEM((chunk, LANES), F32),
                pltpu.VMEM((2 * ROWS, TILES * LANES), BF16),
                pltpu.VMEM((2 * ROWS, TILES * LANES), F32),
                pltpu.VMEM((TILES * ROWS, 4 * LANES), BF16),
                pltpu.VMEM((TILES * ROWS, 2 * LANES), F32),
                pltpu.SemaphoreType.DMA,
            ],
        ),
        cost_estimate=pl.CostEstimate(flops=2_000_000_000, bytes_accessed=6_000_000, transcendentals=0),
        compiler_params=pltpu.CompilerParams(vmem_limit_bytes=58 * 2**20),
        name="filter_transform",
    )(place, long_filter, *consts)


def conv_kernel(
    packed, bands, skip, gain_ref, ahead, back, fine, coarse, turn_rows, forward, inverse, out_ref,
    wide, signal, query, stage, parts, product, result, gain, arrived,
):
    fetch = pltpu.make_async_copy(gain_ref.at[0 : TILES * ROWS], gain, arrived)
    fetch.start()
    wide[0:MESSAGE_PAD] = jnp.zeros((MESSAGE_PAD, LANES), F32)
    wide[MESSAGE_PAD:] = packed[...].astype(F32).reshape(DEVICES * MESSAGE, LANES)

    def rows_of(stream, q):
        at = MESSAGE_PAD + stream * TILES + q
        if q < 0:
            at += TILES - MESSAGE
        return wide[pl.ds(at, DEVICES, stride=MESSAGE), :].astype(BF16)

    for q in range(TILES):
        lanes = slice(q * LANES, (q + 1) * LANES)
        sums = []
        for stream in range(STREAMS):
            both = jnp.concatenate([rows_of(stream, q - 1), rows_of(stream, q)], axis=1)
            halves_of = dot(both, bands[(stream + 1) % STREAMS])
            sums.append(halves_of[:, 0:LANES] + halves_of[:, LANES:])
        query[:, lanes] = sums[2]
        gated = (sums[0] * sums[1]).astype(BF16)
        signal[0:ROWS, lanes] = gated
        signal[ROWS:, lanes] = gated
    forward_transform(signal, ahead, fine, coarse, turn_rows, stage, parts)
    fetch.wait()
    for k in range(TILES):
        rows = slice(k * ROWS, (k + 1) * ROWS)
        mid = table_dot(parts[rows, 0:256], parts[rows, 256:512], forward)
        a, b = mid[:, 0:LANES], mid[:, LANES:]
        c, d = gain[rows, 0:LANES], gain[rows, LANES:]
        re_upper, re_lower = split(a * c - b * d)
        im_upper, im_lower = split(a * d + b * c)
        upper = jnp.concatenate([re_upper, im_upper], axis=1)
        lower = jnp.concatenate([re_lower, im_lower], axis=1)
        product[rows] = table_dot(upper, lower, inverse)

    def unspin(step, carry):
        at = pl.multiple_of(step * 16, 16)
        spins = spin_rows(fine, coarse, step)
        real, imag = [], []
        for k in range(TILES):
            rows = pl.ds(at + k * ROWS, 16)
            a, b = product[rows, 0:128], product[rows, 128:256]
            if k > 0:
                c, d = turn_rows[k : k + 1], turn_rows[TILES + k : TILES + k + 1]
                a, b = a * c + b * d, b * c - a * d
            real.append(a)
            imag.append(b)
        er, ei = real[0] + real[2], imag[0] + imag[2]
        fr, fi = real[0] - real[2], imag[0] - imag[2]
        gr, gi = real[1] + real[3], imag[1] + imag[3]
        hr, hi = real[1] - real[3], imag[1] - imag[3]
        outs = ((er + gr, ei + gi), (fr - hi, fi + hr), (er - gr, ei - gi), (fr + hi, fi - hr))
        for q, (a, b) in enumerate(outs):
            lanes = slice(q * LANES, (q + 1) * LANES)
            c, d = spins[q]
            parts[pl.ds(at, 16), lanes], parts[pl.ds(at + 2 * ROWS, 16), lanes] = split(a * c + b * d)
            parts[pl.ds(at + ROWS, 16), lanes], parts[pl.ds(at + 3 * ROWS, 16), lanes] = split(b * c - a * d)
        return carry

    lax.fori_loop(0, ROWS // 16, unspin, 0, unroll=True)
    for q in range(0, TILES, 2):
        lanes = slice(q * LANES, (q + 2) * LANES)
        upper, lower = parts[0:512, lanes], parts[512:1024, lanes]
        long_part = dot(back[:, 0:512], upper) + dot(back[:, 0:512], lower) + dot(back[:, 512:1024], upper)
        for at in range(2):
            lanes = slice((q + at) * LANES, (q + at + 1) * LANES)
            direct = skip[...] * signal[0:ROWS, lanes].astype(F32)
            total = query[:, lanes] * (long_part[:, at * LANES : (at + 1) * LANES] + direct)
            result[pl.ds(q + at, ROWS, stride=TILES), :] = total
    out_ref[...] = result[...].reshape(DEVICES // 2, 2 * TILES, LANES).astype(BF16)


def convolve(packed, bands, skip, gain, ahead, back, fine, coarse, turn_rows, forward, inverse):
    return pl.pallas_call(
        conv_kernel,
        out_shape=jax.ShapeDtypeStruct((DEVICES // 2, 2 * TILES, LANES), BF16),
        in_specs=[VMEM] * 3 + [pl.BlockSpec(memory_space=pl.ANY)] + [VMEM] * 7,
        out_specs=VMEM,
        scratch_shapes=[
            pltpu.VMEM((MESSAGE_PAD + DEVICES * MESSAGE, LANES), F32),
            pltpu.VMEM((2 * ROWS, TILES * LANES), BF16),
            pltpu.VMEM((ROWS, TILES * LANES), F32),
            pltpu.VMEM((2 * ROWS, TILES * LANES), F32),
            pltpu.VMEM((TILES * ROWS, 4 * LANES), BF16),
            pltpu.VMEM((TILES * ROWS, 2 * LANES), F32),
            pltpu.VMEM((DEVICES * TILES, LANES), F32),
            pltpu.VMEM((TILES * ROWS, 2 * LANES), F32),
            pltpu.SemaphoreType.DMA,
        ],
        cost_estimate=pl.CostEstimate(flops=4_000_000_000, bytes_accessed=6_000_000, transcendentals=0),
        compiler_params=pltpu.CompilerParams(vmem_limit_bytes=24 * 2**20),
        name="convolve",
    )(packed, bands, skip, gain, ahead, back, fine, coarse, turn_rows, forward, inverse)


def unpack_kernel(mixed_ref, out_ref, after):
    for half in range(2):
        came = [[mixed_ref[half, d, pair].astype(F32) for d in range(GROUPS)] for pair in range(CH // 2)]
        done = [exchange(tiles) for tiles in came]
        for pair, tiles in enumerate(done):
            for t in range(GROUPS):
                after[half, pair, pl.ds(t, 8, stride=GROUPS), :] = tiles[t]
    for j in range(CH):
        for half in range(2):
            lanes = slice((2 * j + half) * LANES, (2 * j + half + 1) * LANES)
            out_ref[:, lanes] = after[half, j // 2, j % 2 * BLOCK : (j % 2 + 1) * BLOCK].astype(BF16)


def unpack(mixed):
    return pl.pallas_call(
        unpack_kernel,
        out_shape=jax.ShapeDtypeStruct((BLOCK, WIDTH), BF16),
        in_specs=[VMEM],
        out_specs=VMEM,
        scratch_shapes=[pltpu.VMEM((2, CH // 2, 2 * BLOCK, LANES), F32)],
        cost_estimate=pl.CostEstimate(flops=4_000_000, bytes_accessed=500_000, transcendentals=0),
        compiler_params=pltpu.CompilerParams(vmem_limit_bytes=8 * 2**20),
        name="unpack",
    )(mixed)


def band_kernel(taps, out_ref):
    for at in range(0, 2 * LANES, 64):
        row = lax.broadcasted_iota(jnp.int32, (64, LANES), 0) + at
        lane = lax.broadcasted_iota(jnp.int32, (64, LANES), 1)
        lag = (lane >> 4) - ((row & LANES - 1) >> 4) + jnp.where(row < LANES, GROUPS, 0)
        lag = jnp.where(((row ^ lane) & OWN - 1) == 0, lag, -1)
        for stream in range(STREAMS):
            band = jnp.zeros((64, LANES), F32)
            for r in range(SHORT):
                band = jnp.where(lag == r, taps[STREAMS * r + stream : STREAMS * r + stream + 1], band)
            out_ref[stream, at : at + 64, 0:LANES], out_ref[stream, at : at + 64, LANES:] = split(band)


def short_bands(taps):
    return pl.pallas_call(
        band_kernel,
        out_shape=jax.ShapeDtypeStruct((STREAMS, 2 * LANES, 2 * LANES), BF16),
        in_specs=[VMEM],
        out_specs=VMEM,
        cost_estimate=pl.CostEstimate(flops=2_000_000, bytes_accessed=500_000, transcendentals=0),
        compiler_params=pltpu.CompilerParams(vmem_limit_bytes=8 * 2**20),
        name="short_bands",
    )(taps)


def own_rows(short_weight, row):
    count = STREAMS * SHORT
    taps = lax.dynamic_slice(short_weight, (0, 0, row * OWN), (SHORT, STREAMS, OWN)).reshape(count, OWN)
    return jnp.tile(jnp.pad(taps, ((0, -count % 8), (0, 0))), (1, GROUPS))


def local(inputs, short_weight, long_filter, skip_gain):
    row = lax.axis_index("ctx")
    ahead, back, fine, coarse, turn_rows, forward, inverse = (jnp.asarray(t) for t in tables())
    packed = pack(jnp.transpose(inputs, (1, 0, 2))).reshape(DEVICES, STREAMS, TILES, LANES)
    packed = lax.all_to_all(packed, ("ctx", "ch"), 0, 0, tiled=True)
    packed = packed.reshape(DEVICES * MESSAGE // 8, 8, LANES)
    place = jnp.stack([row // GROUPS, row % GROUPS]).astype(jnp.int32)
    gain = filter_transform(place, long_filter, ahead, fine, coarse, turn_rows, forward)
    bands = short_bands(own_rows(short_weight, row))
    skip = jnp.tile(lax.dynamic_slice(skip_gain, (row * OWN,), (OWN,)), GROUPS).reshape(1, LANES)
    mixed = convolve(packed, bands, skip, gain, ahead, back, fine, coarse, turn_rows, forward, inverse)
    mixed = lax.all_to_all(mixed.reshape(DEVICES, TILES, LANES), ("ctx", "ch"), 0, 0, tiled=True)
    return unpack(mixed.reshape(2, GROUPS, CH // 2, 2 * TILES, LANES))


def solution(mesh):
    in_specs = (P(("ctx", "ch"), None, None), P(None, None, "ch"), P(None, "ch"), P("ch"))
    out_specs = P(("ctx", "ch"), None)
    return jax.shard_map(local, mesh=mesh, in_specs=in_specs, out_specs=out_specs, check_vma=False)
```
